32 devices in a mesh: row: 2 (over core), col: 4 (over y, x), ch: 4 (over z).
Axes of the slice: x: 2, y: 2, z: 4, core: 2. Of those that a mesh axis runs over, the one named last changes fastest.
Arguments:
- grad_out: float32 [4096, 1024], P(('row', 'col'), 'ch'), may hold values from -6 to 6
- relu_mask: int32 [4096, 1024], P(('row', 'col'), 'ch'), may hold values 0 or 1
- saved_agg: float32 [4096, 1024], P(('row', 'col'), 'ch'), may hold values from -0.1875 to 0.1875
- weight: float32 [1024, 1024], P('ch'), may hold values from -0.1875 to 0.1875
- tile_vals: float32 [2, 4, 128, 128, 128], P('row', 'col'), may hold values from -0.125 to 0.125
- tile_pos: int32 [2, 4, 128], P('row', 'col'), may hold values from 0 to 127, as said below
- tile_count: int32 [2, 4], P('row', 'col'), may hold values from 32 to 128, as said below
Outputs:
- weight_grad: float32 [1024, 1024], P(('row', 'col'), 'ch')
- input_grad: float32 [4096, 1024], P('col', 'ch')
The draws below stay inside these ranges and needn't reach their ends.
Inputs may be any that keep to these rules, and one draw needn't show every extreme that they name: `tile_pos`: each block's entries are a permutation of 0 to 127; the first tile_count of them are the block's nonzero tiles, the others list its zero tiles and their slots' values are ignored. `tile_count`: some block is full in every draw.
All inputs are finite; a program needn't handle non-finite values. No bound on the sum of `relu_mask` on one device may be relied on, other than what follows from the above.
Results may differ from the reference program's by a relative error of at most 0.0003.
Values sent between devices are 32-bit elements; how exact they have to be, the bound alone decides.
A program may use at most 128 MiB of HBM per device.

```python
import jax
import jax.numpy as jnp
from jax import lax

F = 1024
TILE = 128
OUT_TILES = 16
IN_TILES = 8
BLOCK_TILES = 128
ROWS_OUT = 4096
ROWS_IN = 4096
N_ROW = 2
N_COL = 4


def draw_tile_pos(key, part):
    row_groups = ROWS_OUT // (TILE * OUT_TILES)
    col_groups = ROWS_IN // (TILE * IN_TILES)
    block_keys = jax.random.split(jax.random.fold_in(key, 11), row_groups * col_groups)
    orders = jax.vmap(lambda single: jax.random.permutation(single, BLOCK_TILES))(block_keys)
    return orders.reshape(row_groups, col_groups, BLOCK_TILES).astype(jnp.int32)


def draw_tile_count(key, part):
    row_groups = ROWS_OUT // (TILE * OUT_TILES)
    col_groups = ROWS_IN // (TILE * IN_TILES)
    lowest = max(BLOCK_TILES // 4, 1)
    counts = jax.random.randint(jax.random.fold_in(key, 23), (row_groups * col_groups,), lowest, BLOCK_TILES + 1)
    chosen = jax.random.randint(jax.random.fold_in(key, 29), (), 0, row_groups * col_groups)
    counts = jnp.where(jnp.arange(row_groups * col_groups, dtype=jnp.int32) == chosen, BLOCK_TILES, counts)
    return counts.reshape(row_groups, col_groups).astype(jnp.int32)


def touch_ends(array, stream_key, least, top_value):
    spot = [jax.random.randint(jax.random.fold_in(stream_key, axis), (), 0, length) for axis, length in enumerate(array.shape)]
    main_axis = array.shape.index(max(array.shape))
    next_to = spot[:main_axis] + [(spot[main_axis] + 1) % array.shape[main_axis]] + spot[main_axis + 1:]
    return array.at[tuple(spot)].set(least).at[tuple(next_to)].set(top_value)


def strengthened(drawn, key, source, target, blocks, factor):
    def block_of(dim):
        return (jnp.arange(drawn.shape[dim]) // (drawn.shape[dim] // blocks)).reshape((-1,) + (1,) * (drawn.ndim - 1 - dim))

    one_side = jax.random.permutation(key, blocks)[block_of(target)]
    other_side = (block_of(target) + blocks // 2) % blocks
    return jnp.where((block_of(source) == one_side) | (block_of(source) == other_side), factor * drawn, drawn)


def block_scale(rng, extent, cuts, least, largest):
    def one(axis_at, parts):
        draws = jax.random.uniform(jax.random.fold_in(jax.random.fold_in(rng, 6), axis_at), (parts,), jnp.float32, least / len(cuts), largest / len(cuts))
        return jnp.repeat(jnp.exp(draws), extent[axis_at] // parts).reshape((-1,) + (1,) * (len(extent) - axis_at - 1))

    factor_of = one(*cuts[0])
    for cut in cuts[1:]:
        factor_of = factor_of * one(*cut)
    return factor_of


def noise(own_key, shape, spread, limit, shards=(), held_as=jnp.bfloat16):
    factor_of = block_scale(own_key, shape, shards, -0.22, 0.18) if shards else 1.0
    drawn = jax.random.normal(own_key, shape, jnp.float32) * spread * factor_of
    return jnp.minimum(jnp.maximum(drawn, -limit), limit).astype(held_as)


def noise_with(rng, shape, width, bound, cuts, heavy, kind=jnp.bfloat16):
    result = width * jax.random.normal(rng, shape, jnp.float32)
    if cuts:
        result = result * block_scale(rng, shape, cuts, -0.22, 0.18)
    return jnp.clip(strengthened(result, jax.random.fold_in(rng, 3), *heavy), -bound, bound).astype(kind)


def setup_inputs(seed: int = 0) -> dict:
    splits = jax.random.split(jax.random.key(seed), 8)
    grad_out = noise(splits[0], (ROWS_OUT, F), 1.0, 6.0, ((0, 8), (1, 4)), jnp.float32)
    relu_mask = touch_ends((jax.random.randint(splits[1], (ROWS_OUT, F), 0, 2) < 1).astype(jnp.int32), jax.random.fold_in(splits[1], 1), 0, 1)
    saved_agg = noise_with(splits[2], (ROWS_OUT, F), (2.0 / ROWS_OUT ** 0.5), 0.1875, ((0, 8), (1, 4)), (0, 1, 8, 2.0), jnp.float32)
    weight = noise(splits[3], (F, F), F ** -0.5, 0.1875, ((0, 4),), jnp.float32)
    tile_vals = noise(splits[4], (N_ROW, N_COL, BLOCK_TILES, TILE, TILE), (TILE * OUT_TILES * N_ROW // 2) ** -0.5, 0.125, ((0, 2), (1, 4)), jnp.float32)
    tile_pos = draw_tile_pos(jax.random.fold_in(splits[7], 71), 0)
    tile_count = draw_tile_count(jax.random.fold_in(splits[7], 71), 0)
    return dict(grad_out=grad_out, relu_mask=relu_mask, saved_agg=saved_agg, weight=weight, tile_vals=tile_vals, tile_pos=tile_pos, tile_count=tile_count)


HIGHEST = lax.Precision.HIGHEST

def block_grad(tile_set, positions, live_count, grad_rows):
    slot_total = tile_set.shape[0]
    channels = grad_rows.shape[1]
    active = (jnp.arange(slot_total, dtype=jnp.int32) < live_count).astype(jnp.float32)
    out_tile = (positions // IN_TILES).astype(jnp.int32)
    in_tile = (positions % IN_TILES).astype(jnp.int32)
    blocks = grad_rows.reshape(OUT_TILES, TILE, channels)
    picked = jnp.take(blocks, out_tile, axis=0)
    product = jnp.einsum('tij,tif->tjf', tile_set, picked, precision=HIGHEST)
    onehot = (in_tile[:, None] == jnp.arange(IN_TILES, dtype=jnp.int32)[None, :]).astype(jnp.float32) * active[:, None]
    summed = jnp.einsum('tc,tjf->cjf', onehot, product, precision=HIGHEST)
    return summed.reshape(IN_TILES * TILE, channels)

def reference(grad_out, relu_mask, saved_agg, weight, tile_vals, tile_pos, tile_count):
    masked = grad_out * relu_mask.astype(jnp.float32)
    weight_grad = jnp.dot(saved_agg.T, masked, precision=HIGHEST, preferred_element_type=jnp.float32)
    agg_grad = jnp.dot(masked, weight.T, precision=HIGHEST, preferred_element_type=jnp.float32)
    row_groups = tile_vals.shape[0]
    col_groups = tile_vals.shape[1]
    channels = agg_grad.shape[1]
    grad_blocks = agg_grad.reshape(row_groups, OUT_TILES * TILE, channels)

    def per_column(col_index):

        def add_block(running, row_index):
            return (running + block_grad(tile_vals[row_index, col_index], tile_pos[row_index, col_index], tile_count[row_index, col_index], grad_blocks[row_index]), None)
        running, _ = lax.scan(add_block, jnp.zeros((IN_TILES * TILE, channels), jnp.float32), jnp.arange(row_groups, dtype=jnp.int32))
        return running
    input_grad = lax.map(per_column, jnp.arange(col_groups, dtype=jnp.int32))
    return (weight_grad, input_grad.reshape(col_groups * IN_TILES * TILE, channels))
```

```python
import functools

import jax
import jax.numpy as jnp
from jax import lax
from jax.experimental import pallas as pl
from jax.experimental.pallas import tpu as pltpu
from jax.sharding import PartitionSpec as P

TILE = 128
MESH = pl.DeviceIdType.MESH
F32 = jnp.float32
BF16 = jnp.bfloat16


def split(x):
    hi = x.astype(BF16)
    return hi, (x - hi.astype(F32)).astype(BF16)


def nn(a, b):
    return lax.dot_general(a, b, (((1,), (0,)), ((), ())), preferred_element_type=F32)


def nt(a, b):
    return lax.dot_general(a, b, (((1,), (1,)), ((), ())), preferred_element_type=F32)


def kernel(
    R, C, N, K,
    slot_ref, g_ref, mask_ref, sa_hbm, w_hbm, tiles_hbm,
    wg_ref, ig_ref, igr,
    M, G, tiles, at_hi, at_lo, w_f, w_hi, w_lo, sa, g_hi, g_lo,
    wgp, wgr, wgs, wgc, wgo,
    local_sem, zsend, zrecv, csend, crecv, wrsend, wrrecv, wcsend, wcrecv, wfsend, wfrecv,
    irsend, irrecv, iasend, iarecv,
):
    r, c, z = lax.axis_index("row"), lax.axis_index("col"), lax.axis_index("ch")
    HB, D = M.shape[2], M.shape[3]
    RC = R * C
    per = RC // N
    blk = wgp.shape[1]
    slots = tiles.shape[0]
    acc = ig_ref
    IN = acc.shape[0]
    in_tiles = IN // TILE
    tpb = HB // TILE
    piece = IN // R

    cp_w = pltpu.make_async_copy(w_hbm, w_f, local_sem.at[0])
    cp_sa = pltpu.make_async_copy(sa_hbm, sa, local_sem.at[1])
    cp_t = pltpu.make_async_copy(tiles_hbm, tiles, local_sem.at[2])
    cp_w.start()
    cp_sa.start()
    cp_t.start()

    def dev(r_, c_, z_):
        return {"row": r_, "col": c_, "ch": z_}

    q = r * C + c
    d_idx = z * per + q // N
    d_r, d_c, d_z = d_idx // C, d_idx % C, q % N
    s_q = (q % per) * N + z
    s_r, s_c, s_z = s_q // C, s_q % C, q // per
    away = jnp.logical_not((d_r == r) & (d_c == c) & (d_z == z))

    barrier = pltpu.get_barrier_semaphore()

    def hello(r_, c_, z_):
        pl.semaphore_signal(barrier, inc=1, device_id=dev(r_, c_, z_), device_id_type=MESH)

    for j in range(1, R):
        hello((r + j) % R, c, z)
    for j in range(1, C):
        hello(r, (c + j) % C, z)

    @pl.when(z > 0)
    def _():
        hello(r, c, z - 1)

    @pl.when(z < N - 1)
    def _():
        hello(r, c, z + 1)

    @pl.when(away)
    def _():
        hello(d_r, d_c, d_z)
        hello(s_r, s_c, s_z)

    def own(k):
        rows = pl.ds(pl.multiple_of(k * HB, HB), HB)
        M[z, k] = g_ref[rows, :] * mask_ref[rows, :].astype(F32)

    own(0)
    own(1)
    one_if = lambda cond: jnp.where(cond, 1, 0)
    greeted = R - 1 + C - 1 + one_if(z > 0) + one_if(z < N - 1) + 2 * one_if(away)
    pl.semaphore_wait(barrier, greeted)

    def zcopy(origin, k, step):
        way = 0 if step < 0 else 1
        return pltpu.make_async_remote_copy(
            src_ref=M.at[origin, k], dst_ref=M.at[origin, k],
            send_sem=zsend.at[way, origin, k], recv_sem=zrecv.at[origin, k],
            device_id=dev(r, c, z + step), device_id_type=MESH,
        )

    def own_send(k):
        @pl.when(z > 0)
        def _():
            zcopy(z, k, -1).start()

        @pl.when(z < N - 1)
        def _():
            zcopy(z, k, 1).start()

    own_send(0)
    own_send(1)
    acc[...] = jnp.zeros_like(acc)
    wgp[...] = jnp.zeros_like(wgp)
    cp_w.wait()
    for n in range(N):
        cols = slice(n * D, (n + 1) * D)
        w_hi[:, cols], w_lo[:, cols] = split(w_f[:, cols])
    cp_sa.wait()
    cp_t.wait()

    def prep(k, cc):
        for t in range(tpb):
            def one(i, _):
                p = ((cc * K + k) * tpb + t) * in_tiles + i
                v = slot_ref[p]
                tile = tiles[lax.rem(v, slots)]
                tile = jnp.where(v < slots, tile, jnp.zeros_like(tile))
                hi, lo = split(tile.T)
                rows = pl.ds(pl.multiple_of(i * TILE, TILE), TILE)
                cols = slice(cc * HB + t * TILE, cc * HB + (t + 1) * TILE)
                at_hi[k, rows, cols] = hi
                at_lo[k, rows, cols] = lo
                return 0

            lax.fori_loop(0, in_tiles, one, 0, unroll=2)

    def ccopy(k, j):
        return pltpu.make_async_remote_copy(
            src_ref=G.at[k, c], dst_ref=G.at[k, c],
            send_sem=csend.at[k, j], recv_sem=crecv.at[k, j],
            device_id=dev(r, (c + j) % C, z), device_id_type=MESH,
        )

    def cwait(k, j):
        o = (c + C - j) % C
        return pltpu.make_async_remote_copy(
            src_ref=G.at[k, o], dst_ref=G.at[k, o],
            send_sem=csend.at[k, j], recv_sem=crecv.at[k, j],
            device_id=dev(r, (c + j) % C, z), device_id_type=MESH,
        )

    def consume(k):
        for j in range(1, C):
            cwait(k, j).wait_recv()
        for n in range(C):
            rows = slice(n * HB, (n + 1) * HB)
            g_hi[rows, :], g_lo[rows, :] = split(G[k, n])

        def part(i, _):
            rows = pl.ds(pl.multiple_of(i * 256, 256), 256)
            a = at_hi[k, rows, :]
            acc[rows, :] += nn(a, g_hi[...]) + nn(a, g_lo[...]) + nn(at_lo[k, rows, :], g_hi[...])
            return 0

        lax.fori_loop(0, IN // 256, part, 0)

    def wrcopy(j):
        t = (r + j) % R
        return pltpu.make_async_remote_copy(
            src_ref=wgp.at[pl.ds(t * C, C)], dst_ref=wgr.at[j],
            send_sem=wrsend.at[j], recv_sem=wrrecv.at[j],
            device_id=dev(t, c, z), device_id_type=MESH,
        )

    groups = [[] for _ in range(N - 1)]
    for cc in range(C):
        groups[cc * max(N - 2, 1) // C].append(cc)

    def body(k, _):
        for d in range(1, N):
            @pl.when(z >= d)
            def _():
                zcopy(z - d, k, 1).wait_recv()

                @pl.when(z < N - 1)
                def _():
                    zcopy(z - d, k, 1).start()

            @pl.when(z + d < N)
            def _():
                zcopy(z + d, k, -1).wait_recv()

                @pl.when(z > 0)
                def _():
                    zcopy(z + d, k, -1).start()

            if d == 1:
                @pl.when(k + 2 < K)
                def _():
                    own(k + 2)
                    own_send(k + 2)

            for cc in groups[d - 1]:
                prep(k, cc)

        agg = jnp.zeros((HB, D), F32)
        for n in range(N):
            cols = slice(n * D, (n + 1) * D)
            hi, lo = split(M[n, k])
            agg += nt(hi, w_hi[:, cols]) + nt(lo, w_hi[:, cols]) + nt(hi, w_lo[:, cols])
        G[k, c] = agg
        for j in range(1, C):
            ccopy(k, j).start()

        rows = pl.ds(pl.multiple_of(k * HB, HB), HB)
        s_hi, s_lo = split(sa[rows, :].T)
        for n in range(N):
            hi, lo = split(M[n, k])
            res = nn(s_hi, hi) + nn(s_hi, lo) + nn(s_lo, hi)
            for h in range(per):
                wgp[h * N + n] += res[h * blk:(h + 1) * blk, :]

        @pl.when(k == K - 1)
        def _():
            for j in range(1, R):
                wrcopy(j).start()

        @pl.when(k > 0)
        def _():
            consume(k - 1)

        return 0

    lax.fori_loop(0, K, body, 0)

    def wccopy(j):
        t = (c + j) % C
        return pltpu.make_async_remote_copy(
            src_ref=wgs.at[t], dst_ref=wgc.at[j],
            send_sem=wcsend.at[j], recv_sem=wcrecv.at[j],
            device_id=dev(r, t, z), device_id_type=MESH,
        )

    wfcopy = pltpu.make_async_remote_copy(
        src_ref=wgo, dst_ref=wg_ref, send_sem=wfsend, recv_sem=wfrecv,
        device_id=dev(d_r, d_c, d_z), device_id_type=MESH,
    )

    def ircopy(j):
        t = (r + j) % R
        whole = R == 2
        rows = pl.ds(0, IN) if whole else pl.ds(pl.multiple_of(t * piece, piece), piece)
        return pltpu.make_async_remote_copy(
            src_ref=acc.at[rows], dst_ref=igr if whole else igr.at[j],
            send_sem=irsend.at[j], recv_sem=irrecv.at[j],
            device_id=dev(t, c, z), device_id_type=MESH,
        )

    mine = pl.ds(pl.multiple_of(r * piece, piece), piece)

    def iacopy(j):
        return pltpu.make_async_remote_copy(
            src_ref=ig_ref.at[mine], dst_ref=ig_ref.at[mine],
            send_sem=iasend.at[j], recv_sem=iarecv.at[j],
            device_id=dev((r + j) % R, c, z), device_id_type=MESH,
        )

    def iawait(j):
        theirs = pl.ds(pl.multiple_of(((r + R - j) % R) * piece, piece), piece)
        return pltpu.make_async_remote_copy(
            src_ref=ig_ref.at[theirs], dst_ref=ig_ref.at[theirs],
            send_sem=iasend.at[j], recv_sem=iarecv.at[j],
            device_id=dev((r + j) % R, c, z), device_id_type=MESH,
        )

    for j in range(1, R):
        wrcopy(j).wait_recv()
    total = wgp[pl.ds(r * C, C)]
    for j in range(1, R):
        total += wgr[j]
    wgs[...] = total
    for j in range(1, C):
        wccopy(j).start()

    consume(K - 1)
    for j in range(1, R):
        ircopy(j).start()
    for j in range(1, C):
        wccopy(j).wait_recv()
    wpart = wgs[c]
    for j in range(1, C):
        wpart += wgc[j]

    @pl.when(away)
    def _():
        wgo[...] = wpart
        wfcopy.start()
        wfcopy.wait()

    @pl.when(jnp.logical_not(away))
    def _():
        wg_ref[...] = wpart

    for j in range(1, R):
        ircopy(j).wait_recv()
    if R > 2:
        summed = acc[mine, :]
        for j in range(1, R):
            summed += igr[j]
        ig_ref[mine, :] = summed
        for j in range(1, R):
            iacopy(j).start()
        for j in range(1, R):
            iawait(j).wait_recv()

    for j in range(1, R):
        wrcopy(j).wait_send()
        ircopy(j).wait_send()
        if R > 2:
            iacopy(j).wait_send()
    for j in range(1, C):
        wccopy(j).wait_send()

    def drain(k, _):
        for j in range(1, C):
            ccopy(k, j).wait_send()
        for n in range(N):
            @pl.when((z > 0) & (z <= n))
            def _():
                zcopy(n, k, -1).wait_send()

            @pl.when((z < N - 1) & (z >= n))
            def _():
                zcopy(n, k, 1).wait_send()

        return 0

    lax.fori_loop(0, K, drain, 0)


def general(R, C, N, grad_out, relu_mask, saved_agg, weight, tile_vals, tile_pos, tile_count):
    H, D = grad_out.shape
    F = weight.shape[1]
    tiles = tile_vals[0, 0]
    slots = tiles.shape[0]
    out_rows = C * H
    IN = slots * TILE * TILE // out_rows
    HB = TILE
    K = H // HB
    blk = F // (R * C)
    s = jnp.arange(slots, dtype=jnp.int32)
    code = jnp.where(s < tile_count[0, 0], s, s + slots)
    where = jnp.sum(jnp.where(tile_pos[0, 0][None, :] == s[:, None], code[None, :], 0), axis=1).astype(jnp.int32)
    vmem = pl.BlockSpec(memory_space=pltpu.VMEM)
    hbm = pl.BlockSpec(memory_space=pl.ANY)
    dma = pltpu.SemaphoreType.DMA
    igr_shape = (IN, D) if R == 2 else (R, IN // R, D)
    wg, ig, igr = pl.pallas_call(
        functools.partial(kernel, R, C, N, K),
        out_shape=(
            jax.ShapeDtypeStruct((blk, D), F32),
            jax.ShapeDtypeStruct((IN, D), F32),
            jax.ShapeDtypeStruct(igr_shape, F32),
        ),
        in_specs=[pl.BlockSpec(memory_space=pltpu.SMEM), vmem, vmem, hbm, hbm, hbm],
        out_specs=(vmem, vmem, vmem),
        scratch_shapes=[
            pltpu.VMEM((N, K, HB, D), F32),
            pltpu.VMEM((K, C, HB, D), F32),
            pltpu.VMEM((slots, TILE, TILE), F32),
            pltpu.VMEM((K, IN, C * HB), BF16),
            pltpu.VMEM((K, IN, C * HB), BF16),
            pltpu.VMEM((D, F), F32),
            pltpu.VMEM((D, F), BF16),
            pltpu.VMEM((D, F), BF16),
            pltpu.VMEM((H, D), F32),
            pltpu.VMEM((C * HB, D), BF16),
            pltpu.VMEM((C * HB, D), BF16),
            pltpu.VMEM((R * C, blk, D), F32),
            pltpu.VMEM((R, C, blk, D), F32),
            pltpu.VMEM((C, blk, D), F32),
            pltpu.VMEM((C, blk, D), F32),
            pltpu.VMEM((blk, D), F32),
            dma((3,)),
            dma((2, N, K)), dma((N, K)),
            dma((K, C)), dma((K, C)),
            dma((R,)), dma((R,)),
            dma((C,)), dma((C,)),
            dma, dma,
            dma((R,)), dma((R,)),
            dma((R,)), dma((R,)),
        ],
        compiler_params=pltpu.CompilerParams(
            collective_id=0, has_side_effects=True, vmem_limit_bytes=60 * 1024 * 1024
        ),
    )(where, grad_out, relu_mask, saved_agg, weight, tiles)

    def finish(wg_in, a, b, wg_out, ig_out):
        wg_out[...] = wg_in[...]
        ig_out[...] = a[...] + b[...] if R == 2 else a[...]

    return pl.pallas_call(
        finish,
        out_shape=(jax.ShapeDtypeStruct((blk, D), F32), jax.ShapeDtypeStruct((IN, D), F32)),
        in_specs=[vmem, vmem, vmem if R == 2 else hbm],
        out_specs=(vmem, vmem),
    )(wg, ig, igr)


def line_kernel(
    R, C, N, K, modes,
    slot_ref, g_ref, mask_ref, sa_hbm, w_hbm, tiles_hbm,
    wg_ref, ig_ref, igr,
    M, G, tiles, at_hi, at_lo, w_f, w_hi, w_lo, sa, g_hi, g_lo,
    we_f, we_hi, we_lo, sae, part, wgp, wgr, wgs, wgc, wgo, wgd,
    local_sem, zsend, zrecv, wesend, werecv, sasend, sarecv, psend, precv,
    csend, crecv, rsend, rrecv, tsend, trecv, dsend, drecv, irsend, irrecv,
):
    r, c, z = lax.axis_index("row"), lax.axis_index("col"), lax.axis_index("ch")
    HB, D = M.shape[2], M.shape[3]
    two = TILE // HB
    per = R * C // N
    sub = wgo.shape[1]
    slots = tiles.shape[0]
    IN = ig_ref.shape[0]
    in_tiles = IN // TILE
    wide = (N - 1) * D
    wrows = D // (R * C)
    mids = [k for k in range(K) if modes[k // two]]
    midt = [t for t in range(K // two) if modes[t]]

    low = z < N // 2
    end = (z == 0) | (z == N - 1)
    inner = jnp.logical_not(end)
    z_in = jnp.where(low, z + 1, z - 1)
    z_out = jnp.where(low, z - 1, z + 1)
    e0 = jnp.where(low, 0, N - 1)
    e1 = jnp.where(low, 1, N - 2)
    o1 = jnp.where(low, 2, N - 3)
    o0 = jnp.where(low, N - 1, 0)
    p = r * C + c

    cp_w = pltpu.make_async_copy(w_hbm, w_f, local_sem.at[0])
    cp_sa = pltpu.make_async_copy(sa_hbm, sa, local_sem.at[1])
    cp_t = pltpu.make_async_copy(tiles_hbm, tiles, local_sem.at[2])
    cp_w.start()
    cp_sa.start()
    cp_t.start()

    def dev(r_, c_, z_):
        return {"row": r_, "col": c_, "ch": z_}

    one_if = lambda cond: jnp.where(cond, 1, 0)
    same = lambda r_, c_, z_: (r_ == r) & (c_ == c) & (z_ == z)
    far = jnp.logical_not

    pending = []

    def send(src, dst, ss, rs, to, cond=None):
        def make():
            return pltpu.make_async_remote_copy(
                src_ref=src, dst_ref=dst, send_sem=ss, recv_sem=rs, device_id=to, device_id_type=MESH
            )

        pending.append((cond, make))
        if cond is None:
            make().start()
        else:
            pl.when(cond)(lambda: make().start())

    def recv(dst, ss, rs):
        pltpu.make_async_remote_copy(
            src_ref=dst, dst_ref=dst, send_sem=ss, recv_sem=rs, device_id=dev(1 - r, c, z), device_id_type=MESH
        ).wait_recv()

    own_q = per * z + r
    end_q = per * e0 + r
    block_n = [lax.rem(z + d, N) for d in range(N)] + [e1, o1, o0]
    block_q = [own_q] * N + [end_q] * (N - 1)

    def goal(b):
        return block_q[b] // C, block_q[b] % C, block_n[b]

    my_a, my_r = p // per, p % per
    my_end = ((my_a == 0) | (my_a == N - 1)) & (my_a != z)
    my_i = jnp.where(my_a == 0, 1, N - 2)
    helped = len(midt) > 0

    barrier = pltpu.get_barrier_semaphore()

    def hello(r_, c_, z_):
        pl.semaphore_signal(barrier, inc=1, device_id=dev(r_, c_, z_), device_id_type=MESH)

    hello(1 - r, c, z)
    for j in range(1, C):
        hello(r, (c + j) % C, z)
    hello(r, c, z_in)
    pl.when(inner)(lambda: hello(r, c, z_out))
    for j in range(C):
        pl.when(far(same(my_r, j, my_a)))(lambda: hello(my_r, j, my_a))
        if helped:
            pl.when(my_end & far(same(my_r, j, my_i)))(lambda: hello(my_r, j, my_i))
    greeted = R - 1 + C - 1 + 1 + one_if(inner)
    for b in range(N):
        greeted += one_if(far(same(*goal(b))))
    if helped:
        for b in range(N, 2 * N - 1):
            greeted += one_if(inner & far(same(*goal(b))))

    def mask(k):
        rows = pl.ds(k * HB, HB)
        M[z, k] = g_ref[rows, :] * mask_ref[rows, :].astype(F32)

    def zpass(o, k, inward, cond=None):
        way = 0 if inward else 1
        send(M.at[o, k], M.at[o, k], zsend.at[way, o, k], zrecv.at[o, k], dev(r, c, z_in if inward else z_out), cond)

    def zwait(o, k):
        recv(M.at[o, k], zsend.at[0, o, k], zrecv.at[o, k])

    def own_send(k):
        zpass(z, k, True)
        if not modes[k // two]:
            zpass(z, k, False, inner)

    ahead = 3
    for k in range(ahead):
        mask(k)
    pl.semaphore_wait(barrier, greeted)
    own_send(0)
    cp_w.wait()
    if helped:
        cols = pl.ds(pl.multiple_of(jnp.where(low, D, 0), D), wide)
        rows = pl.ds(pl.multiple_of(p * wrows, wrows), wrows)
        send(w_f.at[rows, cols], we_f.at[p], wesend.at[0], werecv.at[0], dev(r, c, z_in), end)
    for k in range(1, ahead):
        own_send(k)
    for k in range(ahead, K):
        mask(k)
    for n in range(N):
        cols = slice(n * D, (n + 1) * D)
        w_hi[:, cols], w_lo[:, cols] = split(w_f[:, cols])
    cp_sa.wait()

    def rows_of(o, t):
        return M[o, t * two:(t + 1) * two].reshape(TILE, D)

    def outer(s, m):
        hi, lo = split(m)
        return nn(s[0], hi) + nn(s[0], lo) + nn(s[1], hi)

    def wadd(b, value, first):
        value = value.reshape(R, D // R, D)
        if first:
            wgp[b] = value
        else:
            wgp[b] += value

    def sa_own(t):
        return split(sa[t * TILE:(t + 1) * TILE, :].T)

    def wgrad_own():
        for t in range(K // two):
            wadd(0, outer(sa_own(t), rows_of(z, t)), t == 0)

    raw_t = [t for t in range(K // two) if not modes[t]]

    def wgrad(t):
        def own_blocks(zero):
            s = sa_own(t)
            for d in range(1, N):
                wadd(d, outer(s, rows_of(block_n[d], t)), zero)

        if not modes[t]:
            own_blocks(t == 0)
            return

        @pl.when(inner)
        def _():
            own_blocks(t == 0)
            i = midt.index(t)
            recv(sae.at[i], sasend.at[i], sarecv.at[i])
            s = split(sae[i].T)
            for b in range(N, 2 * N - 1):
                wadd(b, outer(s, rows_of(block_n[b], t)), i == 0)

    assert 0 in raw_t

    def red_row(n, lo, hi, cond=None):
        bs = pl.ds(lo, hi - lo)
        send(wgp.at[bs, 1 - r], wgr.at[bs], rsend.at[n], rrecv.at[n], dev(1 - r, c, z), cond)

    def red_col(n, lo, hi, cond=None):
        bs = pl.ds(lo, hi - lo)

        def go():
            recv(wgr.at[bs], rsend.at[n], rrecv.at[n])
            for b in range(lo, hi):
                total = wgp[b, r] + wgr[b]
                for t in range(C):
                    wgs[t, b] = total[t * sub:(t + 1) * sub]

        go() if cond is None else pl.when(cond)(go)
        for j in range(1, C):
            t = (c + j) % C
            send(wgs.at[t, bs], wgc.at[j, bs], tsend.at[n, j], trecv.at[n, j], dev(r, t, z), cond)

    def red_out(n, lo, hi, cond=None):
        bs = pl.ds(lo, hi - lo)

        def go():
            for j in range(1, C):
                recv(wgc.at[j, bs], tsend.at[n, j], trecv.at[n, j])
            for b in range(lo, hi):
                total = wgs[c, b]
                for j in range(1, C):
                    total += wgc[j, b]
                wgo[b] = total

        go() if cond is None else pl.when(cond)(go)
        for b in range(lo, hi):
            x = 0 if b < N else 1
            away = far(same(*goal(b)))
            here = same(*goal(b))
            if cond is not None:
                away, here = away & cond, here & cond
            send(wgo.at[b], wgd.at[x, c], dsend.at[b], drecv.at[x, c], dev(*goal(b)), away)

            @pl.when(here)
            def _():
                wgd[x, c] = wgo[b]

    def prep(t, half):
        pairs = range(C // two) if half is None else [half]

        def one(i, _):
            for m in pairs:
                got = []
                for j in range(two):
                    v = slot_ref[((two * m + j) * (K // two) + t) * in_tiles + i]
                    tile = tiles[lax.rem(v, slots)]
                    got.append(jnp.where(v < slots, tile, jnp.zeros_like(tile)))
                for h in range(two):
                    mix = jnp.concatenate([x[h * HB:(h + 1) * HB] for x in got], axis=0)
                    hi, lo = split(mix.T)
                    rows = pl.ds(pl.multiple_of(i * TILE, TILE), TILE)
                    cols = slice(m * TILE, (m + 1) * TILE)
                    at_hi[t * two + h, rows, cols] = hi
                    at_lo[t * two + h, rows, cols] = lo
            return 0

        lax.fori_loop(0, in_tiles, one, 0)

    def gather_g(k):
        G_src = G.at[k, c]
        for j in range(1, C):
            send(G_src, G_src, csend.at[k, j], crecv.at[k, j], dev(r, (c + j) % C, z))

    def consume(k):
        for j in range(1, C):
            o = (c + C - j) % C
            recv(G.at[k, o], csend.at[k, j], crecv.at[k, j])
        for n in range(C):
            rows = slice(n * HB, (n + 1) * HB)
            g_hi[rows, :], g_lo[rows, :] = split(G[k, n])
        step = IN // 4

        def block(i, rows):
            a = at_hi[k, rows, :]
            add = nn(a, g_hi[...]) + nn(a, g_lo[...]) + nn(at_lo[k, rows, :], g_hi[...])
            if k == 0:
                ig_ref[rows, :] = add
            else:
                ig_ref[rows, :] += add

        if k < K - 1:
            def body(i, _):
                block(i, pl.ds(pl.multiple_of(i * step, step), step))
                return 0

            lax.fori_loop(0, 4, body, 0)
        else:
            for i in range(4):
                rows = pl.ds(i * step, step)
                block(i, rows)
                send(ig_ref.at[rows], igr.at[rows], irsend.at[i], irrecv.at[i], dev(1 - r, c, z))

    def times_w(os, k, hi_w, lo_w, col_of):
        total = None
        for o in os:
            hi, lo = split(M[o, k])
            cols = col_of(o)
            add = nt(hi, hi_w[:, cols]) + nt(lo, hi_w[:, cols]) + nt(hi, lo_w[:, cols])
            total = add if total is None else total + add
        return total

    def own_cols(o):
        return slice(o * D, (o + 1) * D) if isinstance(o, int) else pl.ds(pl.multiple_of(o * D, D), D)

    def end_cols(o):
        return pl.ds(pl.multiple_of((o - one_if(low)) * D, D), D)

    def agg(k):
        if not modes[k // two]:
            G[k, c] = times_w(range(N), k, w_hi, w_lo, own_cols)
            return
        i = mids.index(k)
        pc = part.at[i]

        @pl.when(inner)
        def _():
            part[i] = times_w([e1, o1, o0], k, we_hi, we_lo, end_cols)

        send(pc, pc, psend.at[i], precv.at[i], dev(r, c, z_out), inner)

        @pl.when(inner)
        def _():
            G[k, c] = times_w(range(N), k, w_hi, w_lo, own_cols)

        @pl.when(end)
        def _():
            mine = times_w([z], k, w_hi, w_lo, own_cols)
            recv(pc, psend.at[i], precv.at[i])
            G[k, c] = mine + part[i]

    def end_weights(stage):
        if not helped:
            return
        if stage == 0:
            pl.when(inner)(lambda: recv(we_f.at[p], wesend.at[0], werecv.at[0]))
            for j in range(1, C):
                send(we_f.at[p], we_f.at[p], wesend.at[j], werecv.at[j], dev(r, (c + j) % C, z), inner)
        if stage == 1:
            @pl.when(inner)
            def _():
                for j in range(1, C):
                    recv(we_f.at[r * C + (c + C - j) % C], wesend.at[j], werecv.at[j])

            mine = pl.ds(r * C, C)
            send(we_f.at[mine], we_f.at[mine], wesend.at[C], werecv.at[C], dev(1 - r, c, z), inner)
        if stage == 2:
            @pl.when(inner)
            def _():
                recv(we_f.at[pl.ds((1 - r) * C, C)], wesend.at[C], werecv.at[C])
                for i in range(R * C):
                    rows = slice(i * wrows, (i + 1) * wrows)
                    we_hi[rows, :], we_lo[rows, :] = split(we_f[i])

    cp_t.wait()
    wgrad_own()
    red_row(0, 0, 1)
    prep(0, 0)

    for k in range(K):
        mid = modes[k // two]

        @pl.when(inner)
        def _():
            zwait(e0, k)

        zpass(e0, k, True, inner)

        @pl.when(inner)
        def _():
            zwait(o1, k)

        if not mid:
            zpass(o1, k, False, inner)
            pl.when(end)(lambda: zwait(e1, k))
        if k + ahead < K:
            own_send(k + ahead)
        if mid and k % two == 0:
            i, rows = midt.index(k // two), pl.ds(k * HB, TILE)
            send(sa.at[rows], sae.at[i], sasend.at[i], sarecv.at[i], dev(r, c, z_in), end)
        if k < 3:
            end_weights(k)
        if k % two == 0:
            prep(k // two, 1)
        elif k < K - 1:
            prep(k // two + 1, 0)

        pl.when(inner)(lambda: zwait(o0, k))
        if not mid:
            zpass(o0, k, False, inner)

            @pl.when(end)
            def _():
                zwait(o1, k)
                zwait(o0, k)

        agg(k)
        gather_g(k)
        if k == 1:
            red_col(0, 0, 1)
        if k == 3:
            red_out(0, 0, 1)
        if k % two == two - 1:
            wgrad(k // two)
        if k == K - 1:
            red_row(1, 1, N)
            if helped:
                red_row(2, N, 2 * N - 1, inner)
        if k > 0:
            consume(k - 1)

    red_col(1, 1, N)
    if helped:
        red_col(2, N, 2 * N - 1, inner)
    consume(K - 1)
    red_out(1, 1, N)
    if helped:
        red_out(2, N, 2 * N - 1, inner)

    for j in range(C):
        pl.when(far(same(my_r, j, my_a)))(lambda: recv(wgd.at[0, j], dsend.at[0], drecv.at[0, j]))
        rows = slice(j * sub, (j + 1) * sub)
        wg_ref[rows, :] = wgd[0, j]
        if helped:
            pl.when(my_end & far(same(my_r, j, my_i)))(lambda: recv(wgd.at[1, j], dsend.at[0], drecv.at[1, j]))

            @pl.when(my_end)
            def _():
                wg_ref[rows, :] += wgd[1, j]

    for i in range(4):
        rows = pl.ds(i * (IN // 4), IN // 4)
        recv(igr.at[rows], irsend.at[i], irrecv.at[i])
    for cond, make in pending:
        if cond is None:
            make().wait_send()
        else:
            pl.when(cond)(lambda: make().wait_send())


def on_line(R, C, N, grad_out, relu_mask, saved_agg, weight, tile_vals, tile_pos, tile_count):
    H, D = grad_out.shape
    F = weight.shape[1]
    tiles = tile_vals[0, 0]
    slots = tiles.shape[0]
    IN = slots * TILE * TILE // (C * H)
    HB = TILE // 2
    K = H // HB
    modes = tuple(MODES[t % len(MODES)] for t in range(H // TILE))
    blk = F // (R * C)
    sub = D // (R * C)
    nb = 2 * N - 1
    s = jnp.arange(slots, dtype=jnp.int32)
    code = jnp.where(s < tile_count[0, 0], s, s + slots)
    where = jnp.sum(jnp.where(tile_pos[0, 0][None, :] == s[:, None], code[None, :], 0), axis=1).astype(jnp.int32)
    vmem = pl.BlockSpec(memory_space=pltpu.VMEM)
    hbm = pl.BlockSpec(memory_space=pl.ANY)
    dma = pltpu.SemaphoreType.DMA
    half = sum(modes)
    wg, ig, igr = pl.pallas_call(
        functools.partial(line_kernel, R, C, N, K, modes),
        out_shape=(
            jax.ShapeDtypeStruct((blk, D), F32),
            jax.ShapeDtypeStruct((IN, D), F32),
            jax.ShapeDtypeStruct((IN, D), F32),
        ),
        in_specs=[pl.BlockSpec(memory_space=pltpu.SMEM), vmem, vmem, hbm, hbm, hbm],
        out_specs=(vmem, vmem, vmem),
        scratch_shapes=[
            pltpu.VMEM((N, K, HB, D), F32),
            pltpu.VMEM((K, C, HB, D), F32),
            pltpu.VMEM((slots, TILE, TILE), F32),
            pltpu.VMEM((K, IN, C * HB), BF16),
            pltpu.VMEM((K, IN, C * HB), BF16),
            pltpu.VMEM((D, F), F32),
            pltpu.VMEM((D, F), BF16),
            pltpu.VMEM((D, F), BF16),
            pltpu.VMEM((H, D), F32),
            pltpu.VMEM((C * HB, D), BF16),
            pltpu.VMEM((C * HB, D), BF16),
            pltpu.VMEM((R * C, sub, (N - 1) * D), F32),
            pltpu.VMEM((D, (N - 1) * D), BF16),
            pltpu.VMEM((D, (N - 1) * D), BF16),
            pltpu.VMEM((max(half, 1), TILE, D), F32),
            pltpu.VMEM((max(2 * half, 1), HB, D), F32),
            pltpu.VMEM((nb, R, D // R, D), F32),
            pltpu.VMEM((nb, D // R, D), F32),
            pltpu.VMEM((C, nb, sub, D), F32),
            pltpu.VMEM((C, nb, sub, D), F32),
            pltpu.VMEM((nb, sub, D), F32),
            pltpu.VMEM((2, C, sub, D), F32),
            dma((3,)),
            dma((2, N, K)), dma((N, K)),
            dma((C + 1,)), dma((C + 1,)),
            dma((max(half, 1),)), dma((max(half, 1),)),
            dma((max(2 * half, 1),)), dma((max(2 * half, 1),)),
            dma((K, C)), dma((K, C)),
            dma((3,)), dma((3,)),
            dma((3, C)), dma((3, C)),
            dma((nb,)), dma((2, C)),
            dma((4,)), dma((4,)),
        ],
        compiler_params=pltpu.CompilerParams(
            collective_id=0, has_side_effects=True, vmem_limit_bytes=60 * 1024 * 1024
        ),
    )(where, grad_out, relu_mask, saved_agg, weight, tiles)

    def finish(wg_in, a, b, wg_out, ig_out):
        wg_out[...] = wg_in[...]
        ig_out[...] = a[...] + b[...]

    return pl.pallas_call(
        finish,
        out_shape=(jax.ShapeDtypeStruct((blk, D), F32), jax.ShapeDtypeStruct((IN, D), F32)),
        in_specs=[vmem, vmem, vmem],
        out_specs=(vmem, vmem),
    )(wg, ig, igr)


MODES = (0, 1, 0, 1)


def per_device(R, C, N, grad_out, *rest):
    H, D = grad_out.shape
    line = R == 2 and N == 4 and R * C // N == R and C % 2 == 0 and D % (8 * R * C) == 0 and H % TILE == 0
    return (on_line if line else general)(R, C, N, grad_out, *rest)


def solution(mesh):
    in_specs = (
        P(("row", "col"), "ch"),
        P(("row", "col"), "ch"),
        P(("row", "col"), "ch"),
        P("ch", None),
        P("row", "col", None, None, None),
        P("row", "col", None),
        P("row", "col"),
    )
    out_specs = (P(("row", "col"), "ch"), P("col", "ch"))
    R, C, N = mesh.shape["row"], mesh.shape["col"], mesh.shape["ch"]
    return jax.shard_map(
        functools.partial(per_device, R, C, N), mesh=mesh, in_specs=in_specs, out_specs=out_specs, check_vma=False
    )
```

```python
import functools

import jax
import jax.numpy as jnp
from jax import lax
from jax.experimental import pallas as pl
from jax.experimental.pallas import tpu as pltpu
from jax.sharding import PartitionSpec as P

TILE = 128
MESH = pl.DeviceIdType.MESH
F32 = jnp.float32
BF16 = jnp.bfloat16


def split(x):
    hi = x.astype(BF16)
    return hi, (x - hi.astype(F32)).astype(BF16)


def nn(a, b):
    return lax.dot_general(a, b, (((1,), (0,)), ((), ())), preferred_element_type=F32)


def nt(a, b):
    return lax.dot_general(a, b, (((1,), (1,)), ((), ())), preferred_element_type=F32)


def kernel(
    R, C, N, K,
    slot_ref, g_ref, mask_ref, sa_hbm, w_hbm, tiles_hbm,
    wg_ref, ig_ref, igr,
    M, G, tiles, at_hi, at_lo, w_f, w_hi, w_lo, sa, g_hi, g_lo,
    wgp, wgr, wgs, wgc, wgo,
    local_sem, zsend, zrecv, csend, crecv, wrsend, wrrecv, wcsend, wcrecv, wfsend, wfrecv,
    irsend, irrecv, iasend, iarecv,
):
    r, c, z = lax.axis_index("row"), lax.axis_index("col"), lax.axis_index("ch")
    HB, D = M.shape[2], M.shape[3]
    RC = R * C
    per = RC // N
    blk = wgp.shape[1]
    slots = tiles.shape[0]
    acc = ig_ref
    IN = acc.shape[0]
    in_tiles = IN // TILE
    tpb = HB // TILE
    piece = IN // R

    cp_w = pltpu.make_async_copy(w_hbm, w_f, local_sem.at[0])
    cp_sa = pltpu.make_async_copy(sa_hbm, sa, local_sem.at[1])
    cp_t = pltpu.make_async_copy(tiles_hbm, tiles, local_sem.at[2])
    cp_w.start()
    cp_sa.start()
    cp_t.start()

    def dev(r_, c_, z_):
        return {"row": r_, "col": c_, "ch": z_}

    q = r * C + c
    d_idx = z * per + q // N
    d_r, d_c, d_z = d_idx // C, d_idx % C, q % N
    s_q = (q % per) * N + z
    s_r, s_c, s_z = s_q // C, s_q % C, q // per
    away = jnp.logical_not((d_r == r) & (d_c == c) & (d_z == z))

    barrier = pltpu.get_barrier_semaphore()

    def hello(r_, c_, z_):
        pl.semaphore_signal(barrier, inc=1, device_id=dev(r_, c_, z_), device_id_type=MESH)

    for j in range(1, R):
        hello((r + j) % R, c, z)
    for j in range(1, C):
        hello(r, (c + j) % C, z)

    @pl.when(z > 0)
    def _():
        hello(r, c, z - 1)

    @pl.when(z < N - 1)
    def _():
        hello(r, c, z + 1)

    @pl.when(away)
    def _():
        hello(d_r, d_c, d_z)
        hello(s_r, s_c, s_z)

    def own(k):
        rows = pl.ds(pl.multiple_of(k * HB, HB), HB)
        M[z, k] = g_ref[rows, :] * mask_ref[rows, :].astype(F32)

    own(0)
    own(1)
    one_if = lambda cond: jnp.where(cond, 1, 0)
    greeted = R - 1 + C - 1 + one_if(z > 0) + one_if(z < N - 1) + 2 * one_if(away)
    pl.semaphore_wait(barrier, greeted)

    def zcopy(origin, k, step):
        way = 0 if step < 0 else 1
        return pltpu.make_async_remote_copy(
            src_ref=M.at[origin, k], dst_ref=M.at[origin, k],
            send_sem=zsend.at[way, origin, k], recv_sem=zrecv.at[origin, k],
            device_id=dev(r, c, z + step), device_id_type=MESH,
        )

    def own_send(k):
        @pl.when(z > 0)
        def _():
            zcopy(z, k, -1).start()

        @pl.when(z < N - 1)
        def _():
            zcopy(z, k, 1).start()

    own_send(0)
    own_send(1)
    acc[...] = jnp.zeros_like(acc)
    wgp[...] = jnp.zeros_like(wgp)
    cp_w.wait()
    for n in range(N):
        cols = slice(n * D, (n + 1) * D)
        w_hi[:, cols], w_lo[:, cols] = split(w_f[:, cols])
    cp_sa.wait()
    cp_t.wait()

    def prep(k, cc):
        for t in range(tpb):
            def one(i, _):
                p = ((cc * K + k) * tpb + t) * in_tiles + i
                v = slot_ref[p]
                tile = tiles[lax.rem(v, slots)]
                tile = jnp.where(v < slots, tile, jnp.zeros_like(tile))
                hi, lo = split(tile.T)
                rows = pl.ds(pl.multiple_of(i * TILE, TILE), TILE)
                cols = slice(cc * HB + t * TILE, cc * HB + (t + 1) * TILE)
                at_hi[k, rows, cols] = hi
                at_lo[k, rows, cols] = lo
                return 0

            lax.fori_loop(0, in_tiles, one, 0, unroll=2)

    def ccopy(k, j):
        return pltpu.make_async_remote_copy(
            src_ref=G.at[k, c], dst_ref=G.at[k, c],
            send_sem=csend.at[k, j], recv_sem=crecv.at[k, j],
            device_id=dev(r, (c + j) % C, z), device_id_type=MESH,
        )

    def cwait(k, j):
        o = (c + C - j) % C
        return pltpu.make_async_remote_copy(
            src_ref=G.at[k, o], dst_ref=G.at[k, o],
            send_sem=csend.at[k, j], recv_sem=crecv.at[k, j],
            device_id=dev(r, (c + j) % C, z), device_id_type=MESH,
        )

    def consume(k):
        for j in range(1, C):
            cwait(k, j).wait_recv()
        for n in range(C):
            rows = slice(n * HB, (n + 1) * HB)
            g_hi[rows, :], g_lo[rows, :] = split(G[k, n])

        def part(i, _):
            rows = pl.ds(pl.multiple_of(i * 256, 256), 256)
            a = at_hi[k, rows, :]
            acc[rows, :] += nn(a, g_hi[...]) + nn(a, g_lo[...]) + nn(at_lo[k, rows, :], g_hi[...])
            return 0

        lax.fori_loop(0, IN // 256, part, 0)

    def wrcopy(j):
        t = (r + j) % R
        return pltpu.make_async_remote_copy(
            src_ref=wgp.at[pl.ds(t * C, C)], dst_ref=wgr.at[j],
            send_sem=wrsend.at[j], recv_sem=wrrecv.at[j],
            device_id=dev(t, c, z), device_id_type=MESH,
        )

    groups = [[] for _ in range(N - 1)]
    for cc in range(C):
        groups[cc * max(N - 2, 1) // C].append(cc)

    def body(k, _):
        for d in range(1, N):
            @pl.when(z >= d)
            def _():
                zcopy(z - d, k, 1).wait_recv()

                @pl.when(z < N - 1)
                def _():
                    zcopy(z - d, k, 1).start()

            @pl.when(z + d < N)
            def _():
                zcopy(z + d, k, -1).wait_recv()

                @pl.when(z > 0)
                def _():
                    zcopy(z + d, k, -1).start()

            if d == 1:
                @pl.when(k + 2 < K)
                def _():
                    own(k + 2)
                    own_send(k + 2)

            for cc in groups[d - 1]:
                prep(k, cc)

        agg = jnp.zeros((HB, D), F32)
        for n in range(N):
            cols = slice(n * D, (n + 1) * D)
            hi, lo = split(M[n, k])
            agg += nt(hi, w_hi[:, cols]) + nt(lo, w_hi[:, cols]) + nt(hi, w_lo[:, cols])
        G[k, c] = agg
        for j in range(1, C):
            ccopy(k, j).start()

        rows = pl.ds(pl.multiple_of(k * HB, HB), HB)
        s_hi, s_lo = split(sa[rows, :].T)
        for n in range(N):
            hi, lo = split(M[n, k])
            res = nn(s_hi, hi) + nn(s_hi, lo) + nn(s_lo, hi)
            for h in range(per):
                wgp[h * N + n] += res[h * blk:(h + 1) * blk, :]

        @pl.when(k == K - 1)
        def _():
            for j in range(1, R):
                wrcopy(j).start()

        @pl.when(k > 0)
        def _():
            consume(k - 1)

        return 0

    lax.fori_loop(0, K, body, 0)

    def wccopy(j):
        t = (c + j) % C
        return pltpu.make_async_remote_copy(
            src_ref=wgs.at[t], dst_ref=wgc.at[j],
            send_sem=wcsend.at[j], recv_sem=wcrecv.at[j],
            device_id=dev(r, t, z), device_id_type=MESH,
        )

    wfcopy = pltpu.make_async_remote_copy(
        src_ref=wgo, dst_ref=wg_ref, send_sem=wfsend, recv_sem=wfrecv,
        device_id=dev(d_r, d_c, d_z), device_id_type=MESH,
    )

    def ircopy(j):
        t = (r + j) % R
        whole = R == 2
        rows = pl.ds(0, IN) if whole else pl.ds(pl.multiple_of(t * piece, piece), piece)
        return pltpu.make_async_remote_copy(
            src_ref=acc.at[rows], dst_ref=igr if whole else igr.at[j],
            send_sem=irsend.at[j], recv_sem=irrecv.at[j],
            device_id=dev(t, c, z), device_id_type=MESH,
        )

    mine = pl.ds(pl.multiple_of(r * piece, piece), piece)

    def iacopy(j):
        return pltpu.make_async_remote_copy(
            src_ref=ig_ref.at[mine], dst_ref=ig_ref.at[mine],
            send_sem=iasend.at[j], recv_sem=iarecv.at[j],
            device_id=dev((r + j) % R, c, z), device_id_type=MESH,
        )

    def iawait(j):
        theirs = pl.ds(pl.multiple_of(((r + R - j) % R) * piece, piece), piece)
        return pltpu.make_async_remote_copy(
            src_ref=ig_ref.at[theirs], dst_ref=ig_ref.at[theirs],
            send_sem=iasend.at[j], recv_sem=iarecv.at[j],
            device_id=dev((r + j) % R, c, z), device_id_type=MESH,
        )

    for j in range(1, R):
        wrcopy(j).wait_recv()
    total = wgp[pl.ds(r * C, C)]
    for j in range(1, R):
        total += wgr[j]
    wgs[...] = total
    for j in range(1, C):
        wccopy(j).start()

    consume(K - 1)
    for j in range(1, R):
        ircopy(j).start()
    for j in range(1, C):
        wccopy(j).wait_recv()
    wpart = wgs[c]
    for j in range(1, C):
        wpart += wgc[j]

    @pl.when(away)
    def _():
        wgo[...] = wpart
        wfcopy.start()
        wfcopy.wait()

    @pl.when(jnp.logical_not(away))
    def _():
        wg_ref[...] = wpart

    for j in range(1, R):
        ircopy(j).wait_recv()
    if R > 2:
        summed = acc[mine, :]
        for j in range(1, R):
            summed += igr[j]
        ig_ref[mine, :] = summed
        for j in range(1, R):
            iacopy(j).start()
        for j in range(1, R):
            iawait(j).wait_recv()

    for j in range(1, R):
        wrcopy(j).wait_send()
        ircopy(j).wait_send()
        if R > 2:
            iacopy(j).wait_send()
    for j in range(1, C):
        wccopy(j).wait_send()

    def drain(k, _):
        for j in range(1, C):
            ccopy(k, j).wait_send()
        for n in range(N):
            @pl.when((z > 0) & (z <= n))
            def _():
                zcopy(n, k, -1).wait_send()

            @pl.when((z < N - 1) & (z >= n))
            def _():
                zcopy(n, k, 1).wait_send()

        return 0

    lax.fori_loop(0, K, drain, 0)


def general(R, C, N, grad_out, relu_mask, saved_agg, weight, tile_vals, tile_pos, tile_count):
    H, D = grad_out.shape
    F = weight.shape[1]
    tiles = tile_vals[0, 0]
    slots = tiles.shape[0]
    out_rows = C * H
    IN = slots * TILE * TILE // out_rows
    HB = TILE
    K = H // HB
    blk = F // (R * C)
    s = jnp.arange(slots, dtype=jnp.int32)
    code = jnp.where(s < tile_count[0, 0], s, s + slots)
    where = jnp.sum(jnp.where(tile_pos[0, 0][None, :] == s[:, None], code[None, :], 0), axis=1).astype(jnp.int32)
    vmem = pl.BlockSpec(memory_space=pltpu.VMEM)
    hbm = pl.BlockSpec(memory_space=pl.ANY)
    dma = pltpu.SemaphoreType.DMA
    igr_shape = (IN, D) if R == 2 else (R, IN // R, D)
    wg, ig, igr = pl.pallas_call(
        functools.partial(kernel, R, C, N, K),
        out_shape=(
            jax.ShapeDtypeStruct((blk, D), F32),
            jax.ShapeDtypeStruct((IN, D), F32),
            jax.ShapeDtypeStruct(igr_shape, F32),
        ),
        in_specs=[pl.BlockSpec(memory_space=pltpu.SMEM), vmem, vmem, hbm, hbm, hbm],
        out_specs=(vmem, vmem, vmem),
        scratch_shapes=[
            pltpu.VMEM((N, K, HB, D), F32),
            pltpu.VMEM((K, C, HB, D), F32),
            pltpu.VMEM((slots, TILE, TILE), F32),
            pltpu.VMEM((K, IN, C * HB), BF16),
            pltpu.VMEM((K, IN, C * HB), BF16),
            pltpu.VMEM((D, F), F32),
            pltpu.VMEM((D, F), BF16),
            pltpu.VMEM((D, F), BF16),
            pltpu.VMEM((H, D), F32),
            pltpu.VMEM((C * HB, D), BF16),
            pltpu.VMEM((C * HB, D), BF16),
            pltpu.VMEM((R * C, blk, D), F32),
            pltpu.VMEM((R, C, blk, D), F32),
            pltpu.VMEM((C, blk, D), F32),
            pltpu.VMEM((C, blk, D), F32),
            pltpu.VMEM((blk, D), F32),
            dma((3,)),
            dma((2, N, K)), dma((N, K)),
            dma((K, C)), dma((K, C)),
            dma((R,)), dma((R,)),
            dma((C,)), dma((C,)),
            dma, dma,
            dma((R,)), dma((R,)),
            dma((R,)), dma((R,)),
        ],
        compiler_params=pltpu.CompilerParams(
            collective_id=0, has_side_effects=True, vmem_limit_bytes=60 * 1024 * 1024
        ),
    )(where, grad_out, relu_mask, saved_agg, weight, tiles)

    def finish(wg_in, a, b, wg_out, ig_out):
        wg_out[...] = wg_in[...]
        ig_out[...] = a[...] + b[...] if R == 2 else a[...]

    return pl.pallas_call(
        finish,
        out_shape=(jax.ShapeDtypeStruct((blk, D), F32), jax.ShapeDtypeStruct((IN, D), F32)),
        in_specs=[vmem, vmem, vmem if R == 2 else hbm],
        out_specs=(vmem, vmem),
    )(wg, ig, igr)


def cat_nn(a, b):
    return nn(jnp.concatenate([a[0], a[0], a[1]], axis=1), jnp.concatenate([b[0], b[1], b[0]], axis=0))


def line_kernel(
    R, C, N, chunks,
    slot_ref, g_ref, mask_ref, sa_hbm, w_hbm, tiles_hbm,
    wg_ref, ig_ref, igr,
    M, G, tiles, at_hi, at_lo, w_f, w_hi, w_lo, sa,
    we_f, we_hi, we_lo, sae, part, wgp, wgr, wgs, wgc, wgo, wgd,
    local_sem, zsend, zrecv, wesend, werecv, sasend, sarecv, psend, precv,
    csend, crecv, rsend, rrecv, tsend, trecv, dsend, drecv, irsend, irrecv,
):
    r, c, z = lax.axis_index("row"), lax.axis_index("col"), lax.axis_index("ch")
    H, D = M.shape[1], M.shape[2]
    T, K = H // TILE, len(chunks)
    per = R * C // N
    sub = wgo.shape[1]
    slots = tiles.shape[0]
    IN = ig_ref.shape[0]
    in_tiles = IN // TILE
    wide = (N - 1) * D
    nb = 2 * N - 1

    low = z < N // 2
    end = (z == 0) | (z == N - 1)
    inner = jnp.logical_not(end)
    z_in = jnp.where(low, z + 1, z - 1)
    z_out = jnp.where(low, z - 1, z + 1)
    e0 = jnp.where(low, 0, N - 1)
    e1 = jnp.where(low, 1, N - 2)
    o1 = jnp.where(low, 2, N - 3)
    o0 = jnp.where(low, N - 1, 0)
    p = r * C + c

    cp_w = pltpu.make_async_copy(w_hbm, w_f, local_sem.at[0])
    cp_sa = pltpu.make_async_copy(sa_hbm, sa, local_sem.at[1])
    cp_t = pltpu.make_async_copy(tiles_hbm, tiles, local_sem.at[2])
    cp_w.start()
    cp_sa.start()
    cp_t.start()

    def dev(r_, c_, z_):
        return {"row": r_, "col": c_, "ch": z_}

    one_if = lambda cond: jnp.where(cond, 1, 0)
    same = lambda r_, c_, z_: (r_ == r) & (c_ == c) & (z_ == z)
    far = jnp.logical_not

    pending = []

    def send(src, dst, ss, rs, to, cond=None):
        def make():
            return pltpu.make_async_remote_copy(
                src_ref=src, dst_ref=dst, send_sem=ss, recv_sem=rs, device_id=to, device_id_type=MESH
            )

        pending.append((cond, make))
        if cond is None:
            make().start()
        else:
            pl.when(cond)(lambda: make().start())

    def recv(dst, ss, rs):
        pltpu.make_async_remote_copy(
            src_ref=dst, dst_ref=dst, send_sem=ss, recv_sem=rs, device_id=dev(1 - r, c, z), device_id_type=MESH
        ).wait_recv()

    own_q = per * z + r
    end_q = per * e0 + r
    block_n = [lax.rem(z + d, N) for d in range(N)] + [e1, o1, o0]
    block_q = [own_q] * N + [end_q] * (N - 1)

    def goal(b):
        return block_q[b] // C, block_q[b] % C, block_n[b]

    my_a, my_r = p // per, p % per
    my_z = jnp.where(my_a == z, z, jnp.where(my_a == 0, 1, jnp.where(my_a == N - 1, N - 2, my_a)))

    barrier = pltpu.get_barrier_semaphore()

    def hello(r_, c_, z_):
        pl.semaphore_signal(barrier, inc=1, device_id=dev(r_, c_, z_), device_id_type=MESH)

    hello(1 - r, c, z)
    for j in range(1, C):
        hello(r, (c + j) % C, z)
    hello(r, c, z_in)
    pl.when(inner)(lambda: hello(r, c, z_out))
    for j in range(C):
        pl.when(far(same(my_r, j, my_z)))(lambda: hello(my_r, j, my_z))
    greeted = R - 1 + C - 1 + 1 + one_if(inner) + one_if(far(same(*goal(0))))
    for b in range(1, nb):
        greeted += one_if(inner & far(same(*goal(b))))

    def rows_of(k):
        return pl.ds(*chunks[k])

    def mask(k):
        rows = rows_of(k)
        M[z, rows, :] = g_ref[rows, :] * mask_ref[rows, :].astype(F32)

    def zpass(o, k, cond=None):
        blk = M.at[o, rows_of(k)]
        send(blk, blk, zsend.at[o, k], zrecv.at[o, k], dev(r, c, z_in), cond)

    def zwait(o, k):
        recv(M.at[o, rows_of(k)], zsend.at[o, k], zrecv.at[o, k])

    def onward(k, more):
        pl.when(inner)(lambda: zwait(e0, k))
        zpass(e0, k, inner)
        for m in more:
            zpass(z, m, inner)

    def sa_pass(t):
        send(sa.at[pl.ds(t * TILE, TILE)], sae.at[t], sasend.at[t], sarecv.at[t], dev(r, c, z_in), end)

    def outer(s, m):
        return cat_nn(s, split(m))

    def wadd(b, value, first):
        value = value.reshape(R, D // R, D)
        if first:
            wgp[b] = value
        else:
            wgp[b] += value

    def sa_own(t):
        return split(sa[t * TILE:(t + 1) * TILE, :].T)

    def tile_rows(o, t):
        return M[o, t * TILE:(t + 1) * TILE, :]

    def wgrad_own():
        for t in range(T):
            wadd(0, outer(sa_own(t), tile_rows(z, t)), t == 0)

    def wgrad(t):
        @pl.when(inner)
        def _():
            s = sa_own(t)
            for b in range(1, N):
                wadd(b, outer(s, tile_rows(block_n[b], t)), t == 0)
            recv(sae.at[t], sasend.at[t], sarecv.at[t])
            s = split(sae[t].T)
            for b in range(N, nb):
                wadd(b, outer(s, tile_rows(block_n[b], t)), t == 0)

    def red_row(n, lo, hi, cond=None):
        bs = pl.ds(lo, hi - lo)
        send(wgp.at[bs, 1 - r], wgr.at[bs], rsend.at[n], rrecv.at[n], dev(1 - r, c, z), cond)

    def red_col(n, lo, hi, cond=None):
        bs = pl.ds(lo, hi - lo)

        def go():
            recv(wgr.at[bs], rsend.at[n], rrecv.at[n])
            for b in range(lo, hi):
                total = wgp[b, r] + wgr[b]
                for t in range(C):
                    wgs[t, b] = total[t * sub:(t + 1) * sub]

        go() if cond is None else pl.when(cond)(go)
        for j in range(1, C):
            t = (c + j) % C
            send(wgs.at[t, bs], wgc.at[j, bs], tsend.at[n, j], trecv.at[n, j], dev(r, t, z), cond)

    def red_out(n, lo, hi, cond=None):
        bs = pl.ds(lo, hi - lo)

        def go():
            for j in range(1, C):
                recv(wgc.at[j, bs], tsend.at[n, j], trecv.at[n, j])
            for b in range(lo, hi):
                total = wgs[c, b]
                for j in range(1, C):
                    total += wgc[j, b]
                wgo[b] = total

        go() if cond is None else pl.when(cond)(go)
        for b in range(lo, hi):
            away = far(same(*goal(b)))
            here = same(*goal(b))
            if cond is not None:
                away, here = away & cond, here & cond
            send(wgo.at[b], wgd.at[c], dsend.at[b], drecv.at[c], dev(*goal(b)), away)

            @pl.when(here)
            def _():
                wgd[c] = wgo[b]

    def prep(t):
        inside = [k for k, (at, n) in enumerate(chunks) if at // TILE == t]
        HB = chunks[inside[0]][1]
        two = TILE // HB

        def one(i, _):
            rows = pl.ds(pl.multiple_of(i * TILE, TILE), TILE)
            for m in range(C // two):
                got = []
                for j in range(two):
                    v = slot_ref[((two * m + j) * T + t) * in_tiles + i]
                    tile = tiles[lax.rem(v, slots)]
                    got.append(jnp.where(v < slots, tile, jnp.zeros_like(tile)))
                for h, k in enumerate(inside):
                    mix = jnp.concatenate([x[h * HB:(h + 1) * HB] for x in got], axis=0)
                    hi, lo = split(mix.T)
                    base = C * chunks[k][0] + m * TILE
                    at_hi[rows, base:base + TILE] = hi
                    at_lo[rows, base:base + TILE] = lo
            return 0

        lax.fori_loop(0, in_tiles, one, 0)

    def gather_g(k, cond=None):
        blk = G.at[c, rows_of(k)]
        for j in range(1, C):
            send(blk, blk, csend.at[k, j], crecv.at[k, j], dev(r, (c + j) % C, z), cond)

    def consume(k):
        at, n = chunks[k]
        for j in range(1, C):
            o = (c + C - j) % C
            recv(G.at[o, rows_of(k)], csend.at[k, j], crecv.at[k, j])
        cols = slice(C * at, C * (at + n))
        g = split(G[:, at:at + n, :].reshape(C * n, D))
        step = IN // 4

        def block(rows):
            add = cat_nn((at_hi[rows, cols], at_lo[rows, cols]), g)
            if k == 0:
                ig_ref[rows, :] = add
            else:
                ig_ref[rows, :] += add

        for i in range(4):
            rows = pl.ds(i * step, step)
            block(rows)
            if k == K - 1:
                send(ig_ref.at[rows], igr.at[rows], irsend.at[i], irrecv.at[i], dev(1 - r, c, z))

    def own_cols(o):
        return pl.ds(pl.multiple_of(o * D, D), D)

    def end_cols(o):
        return pl.ds(pl.multiple_of((o - one_if(low)) * D, D), D)

    def times_w(os, rows, hi_w, lo_w, col_of):
        left, right = [], []
        for o in os:
            hi, lo = split(M[o, rows, :])
            cols = col_of(o)
            wh = hi_w[:, cols]
            left += [hi, lo, hi]
            right += [wh, wh, lo_w[:, cols]]
        return nt(jnp.concatenate(left, axis=1), jnp.concatenate(right, axis=1))

    whole = pl.ds(0, H)

    def partial_own():
        @pl.when(inner)
        def _():
            part[...] = times_w([e1], whole, we_hi, we_lo, end_cols)

    def partial(k):
        rows = rows_of(k)
        pc = part.at[rows]

        @pl.when(inner)
        def _():
            part[rows, :] += times_w([o1, o0], rows, we_hi, we_lo, end_cols)

        send(pc, pc, psend.at[k], precv.at[k], dev(r, c, z_out), inner)

    def agg_inner(k):
        rows = rows_of(k)

        @pl.when(inner)
        def _():
            G[c, rows, :] += times_w([e0, o1, o0], rows, w_hi, w_lo, own_cols)

    def agg_end(k):
        rows = rows_of(k)

        @pl.when(end)
        def _():
            recv(part.at[rows], psend.at[k], precv.at[k])
            G[c, rows, :] += part[rows, :]

    def end_weights(stage):
        if stage == 0:
            pl.when(inner)(lambda: recv(we_f.at[p], wesend.at[0], werecv.at[0]))
            for j in range(1, C):
                send(we_f.at[p], we_f.at[p], wesend.at[j], werecv.at[j], dev(r, (c + j) % C, z), inner)
        if stage == 1:
            @pl.when(inner)
            def _():
                for j in range(1, C):
                    recv(we_f.at[r * C + (c + C - j) % C], wesend.at[j], werecv.at[j])

            mine = pl.ds(r * C, C)
            send(we_f.at[mine], we_f.at[mine], wesend.at[C], werecv.at[C], dev(1 - r, c, z), inner)
        if stage == 2:
            @pl.when(inner)
            def _():
                recv(we_f.at[pl.ds((1 - r) * C, C)], wesend.at[C], werecv.at[C])
                for i in range(R * C):
                    rows = slice(i * sub, (i + 1) * sub)
                    we_hi[rows, :], we_lo[rows, :] = split(we_f[i])

    def arrived(k):
        @pl.when(inner)
        def _():
            zwait(o1, k)
            zwait(o0, k)

    for k in range(K):
        mask(k)
    pl.semaphore_wait(barrier, greeted)
    zpass(z, 0)
    cp_w.wait()
    cols = pl.ds(pl.multiple_of(jnp.where(low, D, 0), D), wide)
    rows = pl.ds(pl.multiple_of(p * sub, sub), sub)
    send(w_f.at[rows, cols], we_f.at[p], wesend.at[0], werecv.at[0], dev(r, c, z_in), end)
    zpass(z, 1)
    cp_sa.wait()
    sa_pass(0)
    for k in range(2, K):
        zpass(z, k, end)
    for t in range(1, T):
        sa_pass(t)
    for n in range(N):
        cols = slice(n * D, (n + 1) * D)
        w_hi[:, cols], w_lo[:, cols] = split(w_f[:, cols])
    wgrad_own()
    red_row(0, 0, 1)
    onward(0, [2])
    G[c] = times_w([z], whole, w_hi, w_lo, own_cols)
    cp_t.wait()
    prep(0)
    end_weights(0)
    red_col(0, 0, 1)
    onward(1, range(3, K))
    prep(1)
    arrived(0)
    agg_inner(0)
    gather_g(0, inner)
    end_weights(1)
    prep(2)
    end_weights(2)
    partial_own()
    partial(0)
    onward(2, [])
    pl.when(end)(lambda: prep(3))
    agg_end(0)
    gather_g(0, end)
    red_out(0, 0, 1)

    for k in range(1, K):
        arrived(k)
        partial(k)
        agg_inner(k)
        agg_end(k)
        gather_g(k)
        if k == 1:
            onward(3, [])
        if k == 2:
            pl.when(inner)(lambda: prep(3))
        if k == K - 1:
            for t in range(k - 1, T):
                wgrad(t)
            red_row(1, 1, nb, inner)
        else:
            wgrad(k - 1)
        if k == 1:
            for m in range(4, K):
                onward(m, [])
        consume(k - 1)

    red_col(1, 1, nb, inner)
    consume(K - 1)
    red_out(1, 1, nb, inner)
    for j in range(C):
        pl.when(far(same(my_r, j, my_z)))(lambda: recv(wgd.at[j], dsend.at[0], drecv.at[j]))
        wg_ref[j * sub:(j + 1) * sub, :] = wgd[j]
    for i in range(4):
        rows = pl.ds(i * (IN // 4), IN // 4)
        recv(igr.at[rows], irsend.at[i], irrecv.at[i])
    for cond, make in pending:
        if cond is None:
            make().wait_send()
        else:
            pl.when(cond)(lambda: make().wait_send())


def on_line(R, C, N, grad_out, relu_mask, saved_agg, weight, tile_vals, tile_pos, tile_count):
    H, D = grad_out.shape
    F = weight.shape[1]
    tiles = tile_vals[0, 0]
    slots = tiles.shape[0]
    IN = slots * TILE * TILE // (C * H)
    T = H // TILE
    half = TILE // 2
    chunks = [(t * TILE, TILE) for t in range(T - 1)] + [(H - TILE, half), (H - half, half)]
    K = len(chunks)
    blk = F // (R * C)
    sub = D // (R * C)
    nb = 2 * N - 1
    s = jnp.arange(slots, dtype=jnp.int32)
    code = jnp.where(s < tile_count[0, 0], s, s + slots)
    where = jnp.sum(jnp.where(tile_pos[0, 0][None, :] == s[:, None], code[None, :], 0), axis=1).astype(jnp.int32)
    vmem = pl.BlockSpec(memory_space=pltpu.VMEM)
    hbm = pl.BlockSpec(memory_space=pl.ANY)
    dma = pltpu.SemaphoreType.DMA
    wg, ig, igr = pl.pallas_call(
        functools.partial(line_kernel, R, C, N, chunks),
        out_shape=(
            jax.ShapeDtypeStruct((blk, D), F32),
            jax.ShapeDtypeStruct((IN, D), F32),
            jax.ShapeDtypeStruct((IN, D), F32),
        ),
        in_specs=[pl.BlockSpec(memory_space=pltpu.SMEM), vmem, vmem, hbm, hbm, hbm],
        out_specs=(vmem, vmem, vmem),
        scratch_shapes=[
            pltpu.VMEM((N, H, D), F32),
            pltpu.VMEM((C, H, D), F32),
            pltpu.VMEM((slots, TILE, TILE), F32),
            pltpu.VMEM((IN, C * H), BF16),
            pltpu.VMEM((IN, C * H), BF16),
            pltpu.VMEM((D, F), F32),
            pltpu.VMEM((D, F), BF16),
            pltpu.VMEM((D, F), BF16),
            pltpu.VMEM((H, D), F32),
            pltpu.VMEM((R * C, sub, (N - 1) * D), F32),
            pltpu.VMEM((D, (N - 1) * D), BF16),
            pltpu.VMEM((D, (N - 1) * D), BF16),
            pltpu.VMEM((T, TILE, D), F32),
            pltpu.VMEM((H, D), F32),
            pltpu.VMEM((nb, R, D // R, D), F32),
            pltpu.VMEM((nb, D // R, D), F32),
            pltpu.VMEM((C, nb, sub, D), F32),
            pltpu.VMEM((C, nb, sub, D), F32),
            pltpu.VMEM((nb, sub, D), F32),
            pltpu.VMEM((C, sub, D), F32),
            dma((3,)),
            dma((N, K)), dma((N, K)),
            dma((C + 1,)), dma((C + 1,)),
            dma((T,)), dma((T,)),
            dma((K,)), dma((K,)),
            dma((K, C)), dma((K, C)),
            dma((2,)), dma((2,)),
            dma((2, C)), dma((2, C)),
            dma((nb,)), dma((C,)),
            dma((4,)), dma((4,)),
        ],
        compiler_params=pltpu.CompilerParams(
            collective_id=0, has_side_effects=True, vmem_limit_bytes=60 * 1024 * 1024
        ),
    )(where, grad_out, relu_mask, saved_agg, weight, tiles)

    def finish(wg_in, a, b, wg_out, ig_out):
        wg_out[...] = wg_in[...]
        ig_out[...] = a[...] + b[...]

    return pl.pallas_call(
        finish,
        out_shape=(jax.ShapeDtypeStruct((blk, D), F32), jax.ShapeDtypeStruct((IN, D), F32)),
        in_specs=[vmem, vmem, vmem],
        out_specs=(vmem, vmem),
    )(wg, ig, igr)


def per_device(R, C, N, grad_out, *rest):
    H, D = grad_out.shape
    line = R == 2 and N == 4 and R * C // N == R and C % 2 == 0 and D % (8 * R * C) == 0
    line = line and H % TILE == 0 and H // TILE == 4
    return (on_line if line else general)(R, C, N, grad_out, *rest)


def solution(mesh):
    in_specs = (
        P(("row", "col"), "ch"),
        P(("row", "col"), "ch"),
        P(("row", "col"), "ch"),
        P("ch", None),
        P("row", "col", None, None, None),
        P("row", "col", None),
        P("row", "col"),
    )
    out_specs = (P(("row", "col"), "ch"), P("col", "ch"))
    R, C, N = mesh.shape["row"], mesh.shape["col"], mesh.shape["ch"]
    return jax.shard_map(
        functools.partial(per_device, R, C, N), mesh=mesh, in_specs=in_specs, out_specs=out_specs, check_vma=False
    )
```

```python
import functools

import jax
import jax.numpy as jnp
from jax import lax
from jax.experimental import pallas as pl
from jax.experimental.pallas import tpu as pltpu
from jax.sharding import PartitionSpec as P

TILE = 128
MESH = pl.DeviceIdType.MESH
F32 = jnp.float32
BF16 = jnp.bfloat16


def split(x):
    hi = x.astype(BF16)
    return hi, (x - hi.astype(F32)).astype(BF16)


def nn(a, b):
    return lax.dot_general(a, b, (((1,), (0,)), ((), ())), preferred_element_type=F32)


def nt(a, b):
    return lax.dot_general(a, b, (((1,), (1,)), ((), ())), preferred_element_type=F32)


def kernel(
    R, C, N, K,
    slot_ref, g_ref, mask_ref, sa_hbm, w_hbm, tiles_hbm,
    wg_ref, ig_ref, igr,
    M, G, tiles, at_hi, at_lo, w_f, w_hi, w_lo, sa, g_hi, g_lo,
    wgp, wgr, wgs, wgc, wgo,
    local_sem, zsend, zrecv, csend, crecv, wrsend, wrrecv, wcsend, wcrecv, wfsend, wfrecv,
    irsend, irrecv, iasend, iarecv,
):
    r, c, z = lax.axis_index("row"), lax.axis_index("col"), lax.axis_index("ch")
    HB, D = M.shape[2], M.shape[3]
    RC = R * C
    per = RC // N
    blk = wgp.shape[1]
    slots = tiles.shape[0]
    acc = ig_ref
    IN = acc.shape[0]
    in_tiles = IN // TILE
    tpb = HB // TILE
    piece = IN // R

    cp_w = pltpu.make_async_copy(w_hbm, w_f, local_sem.at[0])
    cp_sa = pltpu.make_async_copy(sa_hbm, sa, local_sem.at[1])
    cp_t = pltpu.make_async_copy(tiles_hbm, tiles, local_sem.at[2])
    cp_w.start()
    cp_sa.start()
    cp_t.start()

    def dev(r_, c_, z_):
        return {"row": r_, "col": c_, "ch": z_}

    q = r * C + c
    d_idx = z * per + q // N
    d_r, d_c, d_z = d_idx // C, d_idx % C, q % N
    s_q = (q % per) * N + z
    s_r, s_c, s_z = s_q // C, s_q % C, q // per
    away = jnp.logical_not((d_r == r) & (d_c == c) & (d_z == z))

    barrier = pltpu.get_barrier_semaphore()

    def hello(r_, c_, z_):
        pl.semaphore_signal(barrier, inc=1, device_id=dev(r_, c_, z_), device_id_type=MESH)

    for j in range(1, R):
        hello((r + j) % R, c, z)
    for j in range(1, C):
        hello(r, (c + j) % C, z)

    @pl.when(z > 0)
    def _():
        hello(r, c, z - 1)

    @pl.when(z < N - 1)
    def _():
        hello(r, c, z + 1)

    @pl.when(away)
    def _():
        hello(d_r, d_c, d_z)
        hello(s_r, s_c, s_z)

    def own(k):
        rows = pl.ds(pl.multiple_of(k * HB, HB), HB)
        M[z, k] = g_ref[rows, :] * mask_ref[rows, :].astype(F32)

    own(0)
    own(1)
    one_if = lambda cond: jnp.where(cond, 1, 0)
    greeted = R - 1 + C - 1 + one_if(z > 0) + one_if(z < N - 1) + 2 * one_if(away)
    pl.semaphore_wait(barrier, greeted)

    def zcopy(origin, k, step):
        way = 0 if step < 0 else 1
        return pltpu.make_async_remote_copy(
            src_ref=M.at[origin, k], dst_ref=M.at[origin, k],
            send_sem=zsend.at[way, origin, k], recv_sem=zrecv.at[origin, k],
            device_id=dev(r, c, z + step), device_id_type=MESH,
        )

    def own_send(k):
        @pl.when(z > 0)
        def _():
            zcopy(z, k, -1).start()

        @pl.when(z < N - 1)
        def _():
            zcopy(z, k, 1).start()

    own_send(0)
    own_send(1)
    acc[...] = jnp.zeros_like(acc)
    wgp[...] = jnp.zeros_like(wgp)
    cp_w.wait()
    for n in range(N):
        cols = slice(n * D, (n + 1) * D)
        w_hi[:, cols], w_lo[:, cols] = split(w_f[:, cols])
    cp_sa.wait()
    cp_t.wait()

    def prep(k, cc):
        for t in range(tpb):
            def one(i, _):
                p = ((cc * K + k) * tpb + t) * in_tiles + i
                v = slot_ref[p]
                tile = tiles[lax.rem(v, slots)]
                tile = jnp.where(v < slots, tile, jnp.zeros_like(tile))
                hi, lo = split(tile.T)
                rows = pl.ds(pl.multiple_of(i * TILE, TILE), TILE)
                cols = slice(cc * HB + t * TILE, cc * HB + (t + 1) * TILE)
                at_hi[k, rows, cols] = hi
                at_lo[k, rows, cols] = lo
                return 0

            lax.fori_loop(0, in_tiles, one, 0, unroll=2)

    def ccopy(k, j):
        return pltpu.make_async_remote_copy(
            src_ref=G.at[k, c], dst_ref=G.at[k, c],
            send_sem=csend.at[k, j], recv_sem=crecv.at[k, j],
            device_id=dev(r, (c + j) % C, z), device_id_type=MESH,
        )

    def cwait(k, j):
        o = (c + C - j) % C
        return pltpu.make_async_remote_copy(
            src_ref=G.at[k, o], dst_ref=G.at[k, o],
            send_sem=csend.at[k, j], recv_sem=crecv.at[k, j],
            device_id=dev(r, (c + j) % C, z), device_id_type=MESH,
        )

    def consume(k):
        for j in range(1, C):
            cwait(k, j).wait_recv()
        for n in range(C):
            rows = slice(n * HB, (n + 1) * HB)
            g_hi[rows, :], g_lo[rows, :] = split(G[k, n])

        def part(i, _):
            rows = pl.ds(pl.multiple_of(i * 256, 256), 256)
            a = at_hi[k, rows, :]
            acc[rows, :] += nn(a, g_hi[...]) + nn(a, g_lo[...]) + nn(at_lo[k, rows, :], g_hi[...])
            return 0

        lax.fori_loop(0, IN // 256, part, 0)

    def wrcopy(j):
        t = (r + j) % R
        return pltpu.make_async_remote_copy(
            src_ref=wgp.at[pl.ds(t * C, C)], dst_ref=wgr.at[j],
            send_sem=wrsend.at[j], recv_sem=wrrecv.at[j],
            device_id=dev(t, c, z), device_id_type=MESH,
        )

    groups = [[] for _ in range(N - 1)]
    for cc in range(C):
        groups[cc * max(N - 2, 1) // C].append(cc)

    def body(k, _):
        for d in range(1, N):
            @pl.when(z >= d)
            def _():
                zcopy(z - d, k, 1).wait_recv()

                @pl.when(z < N - 1)
                def _():
                    zcopy(z - d, k, 1).start()

            @pl.when(z + d < N)
            def _():
                zcopy(z + d, k, -1).wait_recv()

                @pl.when(z > 0)
                def _():
                    zcopy(z + d, k, -1).start()

            if d == 1:
                @pl.when(k + 2 < K)
                def _():
                    own(k + 2)
                    own_send(k + 2)

            for cc in groups[d - 1]:
                prep(k, cc)

        agg = jnp.zeros((HB, D), F32)
        for n in range(N):
            cols = slice(n * D, (n + 1) * D)
            hi, lo = split(M[n, k])
            agg += nt(hi, w_hi[:, cols]) + nt(lo, w_hi[:, cols]) + nt(hi, w_lo[:, cols])
        G[k, c] = agg
        for j in range(1, C):
            ccopy(k, j).start()

        rows = pl.ds(pl.multiple_of(k * HB, HB), HB)
        s_hi, s_lo = split(sa[rows, :].T)
        for n in range(N):
            hi, lo = split(M[n, k])
            res = nn(s_hi, hi) + nn(s_hi, lo) + nn(s_lo, hi)
            for h in range(per):
                wgp[h * N + n] += res[h * blk:(h + 1) * blk, :]

        @pl.when(k == K - 1)
        def _():
            for j in range(1, R):
                wrcopy(j).start()

        @pl.when(k > 0)
        def _():
            consume(k - 1)

        return 0

    lax.fori_loop(0, K, body, 0)

    def wccopy(j):
        t = (c + j) % C
        return pltpu.make_async_remote_copy(
            src_ref=wgs.at[t], dst_ref=wgc.at[j],
            send_sem=wcsend.at[j], recv_sem=wcrecv.at[j],
            device_id=dev(r, t, z), device_id_type=MESH,
        )

    wfcopy = pltpu.make_async_remote_copy(
        src_ref=wgo, dst_ref=wg_ref, send_sem=wfsend, recv_sem=wfrecv,
        device_id=dev(d_r, d_c, d_z), device_id_type=MESH,
    )

    def ircopy(j):
        t = (r + j) % R
        whole = R == 2
        rows = pl.ds(0, IN) if whole else pl.ds(pl.multiple_of(t * piece, piece), piece)
        return pltpu.make_async_remote_copy(
            src_ref=acc.at[rows], dst_ref=igr if whole else igr.at[j],
            send_sem=irsend.at[j], recv_sem=irrecv.at[j],
            device_id=dev(t, c, z), device_id_type=MESH,
        )

    mine = pl.ds(pl.multiple_of(r * piece, piece), piece)

    def iacopy(j):
        return pltpu.make_async_remote_copy(
            src_ref=ig_ref.at[mine], dst_ref=ig_ref.at[mine],
            send_sem=iasend.at[j], recv_sem=iarecv.at[j],
            device_id=dev((r + j) % R, c, z), device_id_type=MESH,
        )

    def iawait(j):
        theirs = pl.ds(pl.multiple_of(((r + R - j) % R) * piece, piece), piece)
        return pltpu.make_async_remote_copy(
            src_ref=ig_ref.at[theirs], dst_ref=ig_ref.at[theirs],
            send_sem=iasend.at[j], recv_sem=iarecv.at[j],
            device_id=dev((r + j) % R, c, z), device_id_type=MESH,
        )

    for j in range(1, R):
        wrcopy(j).wait_recv()
    total = wgp[pl.ds(r * C, C)]
    for j in range(1, R):
        total += wgr[j]
    wgs[...] = total
    for j in range(1, C):
        wccopy(j).start()

    consume(K - 1)
    for j in range(1, R):
        ircopy(j).start()
    for j in range(1, C):
        wccopy(j).wait_recv()
    wpart = wgs[c]
    for j in range(1, C):
        wpart += wgc[j]

    @pl.when(away)
    def _():
        wgo[...] = wpart
        wfcopy.start()
        wfcopy.wait()

    @pl.when(jnp.logical_not(away))
    def _():
        wg_ref[...] = wpart

    for j in range(1, R):
        ircopy(j).wait_recv()
    if R > 2:
        summed = acc[mine, :]
        for j in range(1, R):
            summed += igr[j]
        ig_ref[mine, :] = summed
        for j in range(1, R):
            iacopy(j).start()
        for j in range(1, R):
            iawait(j).wait_recv()

    for j in range(1, R):
        wrcopy(j).wait_send()
        ircopy(j).wait_send()
        if R > 2:
            iacopy(j).wait_send()
    for j in range(1, C):
        wccopy(j).wait_send()

    def drain(k, _):
        for j in range(1, C):
            ccopy(k, j).wait_send()
        for n in range(N):
            @pl.when((z > 0) & (z <= n))
            def _():
                zcopy(n, k, -1).wait_send()

            @pl.when((z < N - 1) & (z >= n))
            def _():
                zcopy(n, k, 1).wait_send()

        return 0

    lax.fori_loop(0, K, drain, 0)


def general(R, C, N, grad_out, relu_mask, saved_agg, weight, tile_vals, tile_pos, tile_count):
    H, D = grad_out.shape
    F = weight.shape[1]
    tiles = tile_vals[0, 0]
    slots = tiles.shape[0]
    out_rows = C * H
    IN = slots * TILE * TILE // out_rows
    HB = TILE
    K = H // HB
    blk = F // (R * C)
    s = jnp.arange(slots, dtype=jnp.int32)
    code = jnp.where(s < tile_count[0, 0], s, s + slots)
    where = jnp.sum(jnp.where(tile_pos[0, 0][None, :] == s[:, None], code[None, :], 0), axis=1).astype(jnp.int32)
    vmem = pl.BlockSpec(memory_space=pltpu.VMEM)
    hbm = pl.BlockSpec(memory_space=pl.ANY)
    dma = pltpu.SemaphoreType.DMA
    igr_shape = (IN, D) if R == 2 else (R, IN // R, D)
    wg, ig, igr = pl.pallas_call(
        functools.partial(kernel, R, C, N, K),
        out_shape=(
            jax.ShapeDtypeStruct((blk, D), F32),
            jax.ShapeDtypeStruct((IN, D), F32),
            jax.ShapeDtypeStruct(igr_shape, F32),
        ),
        in_specs=[pl.BlockSpec(memory_space=pltpu.SMEM), vmem, vmem, hbm, hbm, hbm],
        out_specs=(vmem, vmem, vmem),
        scratch_shapes=[
            pltpu.VMEM((N, K, HB, D), F32),
            pltpu.VMEM((K, C, HB, D), F32),
            pltpu.VMEM((slots, TILE, TILE), F32),
            pltpu.VMEM((K, IN, C * HB), BF16),
            pltpu.VMEM((K, IN, C * HB), BF16),
            pltpu.VMEM((D, F), F32),
            pltpu.VMEM((D, F), BF16),
            pltpu.VMEM((D, F), BF16),
            pltpu.VMEM((H, D), F32),
            pltpu.VMEM((C * HB, D), BF16),
            pltpu.VMEM((C * HB, D), BF16),
            pltpu.VMEM((R * C, blk, D), F32),
            pltpu.VMEM((R, C, blk, D), F32),
            pltpu.VMEM((C, blk, D), F32),
            pltpu.VMEM((C, blk, D), F32),
            pltpu.VMEM((blk, D), F32),
            dma((3,)),
            dma((2, N, K)), dma((N, K)),
            dma((K, C)), dma((K, C)),
            dma((R,)), dma((R,)),
            dma((C,)), dma((C,)),
            dma, dma,
            dma((R,)), dma((R,)),
            dma((R,)), dma((R,)),
        ],
        compiler_params=pltpu.CompilerParams(
            collective_id=0, has_side_effects=True, vmem_limit_bytes=60 * 1024 * 1024
        ),
    )(where, grad_out, relu_mask, saved_agg, weight, tiles)

    def finish(wg_in, a, b, wg_out, ig_out):
        wg_out[...] = wg_in[...]
        ig_out[...] = a[...] + b[...] if R == 2 else a[...]

    return pl.pallas_call(
        finish,
        out_shape=(jax.ShapeDtypeStruct((blk, D), F32), jax.ShapeDtypeStruct((IN, D), F32)),
        in_specs=[vmem, vmem, vmem if R == 2 else hbm],
        out_specs=(vmem, vmem),
    )(wg, ig, igr)


def cat_nn(a, b):
    return nn(jnp.concatenate([a[0], a[0], a[1]], axis=1), jnp.concatenate([b[0], b[1], b[0]], axis=0))


def line_kernel(
    R, C, N, chunks, raws, relays,
    slot_ref, g_ref, mask_ref, sa_hbm, w_hbm, tiles_hbm,
    wg_ref, ig_ref, igr,
    M, G, tiles, at_hi, at_lo, w_f, w_hi, w_lo, sa,
    we_f, we_hi, we_lo, sae, part, wgp, wgr, wgs, wgc, wgo, wgd,
    local_sem, zsend, zrecv, wesend, werecv, sasend, sarecv, psend, precv,
    csend, crecv, rsend, rrecv, tsend, trecv, dsend, drecv, irsend, irrecv,
):
    r, c, z = lax.axis_index("row"), lax.axis_index("col"), lax.axis_index("ch")
    H, D = M.shape[1], M.shape[2]
    T, K = H // TILE, len(chunks)
    per = R * C // N
    sub = wgo.shape[1]
    slots = tiles.shape[0]
    IN = ig_ref.shape[0]
    in_tiles = IN // TILE
    wide = (N - 1) * D
    nb = 2 * N - 1

    low = z < N // 2
    end = (z == 0) | (z == N - 1)
    inner = jnp.logical_not(end)
    z_in = jnp.where(low, z + 1, z - 1)
    z_out = jnp.where(low, z - 1, z + 1)
    e0 = jnp.where(low, 0, N - 1)
    e1 = jnp.where(low, 1, N - 2)
    o1 = jnp.where(low, 2, N - 3)
    o0 = jnp.where(low, N - 1, 0)
    p = r * C + c

    cp_w = pltpu.make_async_copy(w_hbm, w_f, local_sem.at[0])
    cp_sa = pltpu.make_async_copy(sa_hbm, sa, local_sem.at[1])
    cp_t = pltpu.make_async_copy(tiles_hbm, tiles, local_sem.at[2])
    cp_w.start()
    cp_sa.start()
    cp_t.start()

    def dev(r_, c_, z_):
        return {"row": r_, "col": c_, "ch": z_}

    one_if = lambda cond: jnp.where(cond, 1, 0)
    same = lambda r_, c_, z_: (r_ == r) & (c_ == c) & (z_ == z)
    far = jnp.logical_not

    pending = []

    def send(src, dst, ss, rs, to, cond=None):
        def make():
            return pltpu.make_async_remote_copy(
                src_ref=src, dst_ref=dst, send_sem=ss, recv_sem=rs, device_id=to, device_id_type=MESH
            )

        pending.append((cond, make))
        if cond is None:
            make().start()
        else:
            pl.when(cond)(lambda: make().start())

    def recv(dst, ss, rs):
        pltpu.make_async_remote_copy(
            src_ref=dst, dst_ref=dst, send_sem=ss, recv_sem=rs, device_id=dev(1 - r, c, z), device_id_type=MESH
        ).wait_recv()

    own_q = per * z + r
    end_q = per * e0 + r
    block_n = [z, e0, o1, o0, e1, o1, o0]
    block_q = [own_q] * N + [end_q] * (N - 1)

    def goal(b):
        return block_q[b] // C, block_q[b] % C, block_n[b]

    my_a, my_r = p // per, p % per
    my_z = jnp.where(my_a == z, z, jnp.where(my_a == 0, 1, jnp.where(my_a == N - 1, N - 2, my_a)))

    barrier = pltpu.get_barrier_semaphore()

    def hello(r_, c_, z_):
        pl.semaphore_signal(barrier, inc=1, device_id=dev(r_, c_, z_), device_id_type=MESH)

    hello(1 - r, c, z)
    for j in range(1, C):
        hello(r, (c + j) % C, z)
    hello(r, c, z_in)
    pl.when(inner)(lambda: hello(r, c, z_out))
    for j in range(C):
        pl.when(far(same(my_r, j, my_z)))(lambda: hello(my_r, j, my_z))
    greeted = R - 1 + C - 1 + 1 + one_if(inner) + one_if(far(same(*goal(0))))
    for b in range(1, nb):
        greeted += one_if(inner & far(same(*goal(b))))

    def rows_of(k):
        return pl.ds(*chunks[k])

    def mask(k):
        rows = rows_of(k)
        M[z, rows, :] = g_ref[rows, :] * mask_ref[rows, :].astype(F32)

    def zpass(o, k, cond=None):
        blk = M.at[o, rows_of(k)]
        send(blk, blk, zsend.at[0, o, k], zrecv.at[o, k], dev(r, c, z_in), cond)

    def zout(o, k):
        if k in raws:
            blk = M.at[o, rows_of(k)]
            send(blk, blk, zsend.at[1, o, k], zrecv.at[o, k], dev(r, c, z_out), inner)

    def zwait(o, k):
        recv(M.at[o, rows_of(k)], zsend.at[0, o, k], zrecv.at[o, k])

    def onward(k, more):
        pl.when(inner)(lambda: zwait(e0, k))
        zpass(e0, k, inner)
        for m in more:
            zpass(z, m, inner)

    def sa_pass(t):
        send(sa.at[pl.ds(t * TILE, TILE)], sae.at[t], sasend.at[t], sarecv.at[t], dev(r, c, z_in), end)

    def outer(s, m):
        return cat_nn(s, split(m))

    def wadd(b, value, first):
        value = value.reshape(R, D // R, D)
        if first:
            wgp[b] = value
        else:
            wgp[b] += value

    def sa_own(t):
        return split(sa[t * TILE:(t + 1) * TILE, :].T)

    def tile_rows(o, t):
        return M[o, t * TILE:(t + 1) * TILE, :]

    def wgrad_own():
        for t in range(T):
            wadd(0, outer(sa_own(t), tile_rows(z, t)), t == 0)

    def wgrad_mine(t, bs):
        @pl.when(inner)
        def _():
            s = sa_own(t)
            for b in bs:
                wadd(b, outer(s, tile_rows(block_n[b], t)), t == 0)

    def wgrad_ends(t):
        @pl.when(inner)
        def _():
            recv(sae.at[t], sasend.at[t], sarecv.at[t])
            s = split(sae[t].T)
            for b in range(N, nb):
                wadd(b, outer(s, tile_rows(block_n[b], t)), t == 0)

    def red_row(n, lo, hi, cond=None):
        bs = pl.ds(lo, hi - lo)
        send(wgp.at[bs, 1 - r], wgr.at[bs], rsend.at[n], rrecv.at[n], dev(1 - r, c, z), cond)

    def red_col(n, lo, hi, cond=None):
        bs = pl.ds(lo, hi - lo)

        def go():
            recv(wgr.at[bs], rsend.at[n], rrecv.at[n])
            for b in range(lo, hi):
                total = wgp[b, r] + wgr[b]
                for t in range(C):
                    wgs[t, b] = total[t * sub:(t + 1) * sub]

        go() if cond is None else pl.when(cond)(go)
        for j in range(1, C):
            t = (c + j) % C
            send(wgs.at[t, bs], wgc.at[j, bs], tsend.at[n, j], trecv.at[n, j], dev(r, t, z), cond)

    def red_out(n, lo, hi, cond=None):
        bs = pl.ds(lo, hi - lo)

        def go():
            for j in range(1, C):
                recv(wgc.at[j, bs], tsend.at[n, j], trecv.at[n, j])
            for b in range(lo, hi):
                total = wgs[c, b]
                for j in range(1, C):
                    total += wgc[j, b]
                wgo[b] = total

        go() if cond is None else pl.when(cond)(go)
        for b in range(lo, hi):
            away = far(same(*goal(b)))
            here = same(*goal(b))
            if cond is not None:
                away, here = away & cond, here & cond
            send(wgo.at[b], wgd.at[c], dsend.at[b], drecv.at[c], dev(*goal(b)), away)

            @pl.when(here)
            def _():
                wgd[c] = wgo[b]

    def prep(t):
        inside = [k for k, (at, n) in enumerate(chunks) if at // TILE == t]
        HB = chunks[inside[0]][1]
        two = TILE // HB

        def one(i, _):
            rows = pl.ds(pl.multiple_of(i * TILE, TILE), TILE)
            for m in range(C // two):
                got = []
                for j in range(two):
                    v = slot_ref[((two * m + j) * T + t) * in_tiles + i]
                    tile = tiles[lax.rem(v, slots)]
                    got.append(jnp.where(v < slots, tile, jnp.zeros_like(tile)))
                for h, k in enumerate(inside):
                    mix = jnp.concatenate([x[h * HB:(h + 1) * HB] for x in got], axis=0)
                    hi, lo = split(mix.T)
                    base = C * chunks[k][0] + m * TILE
                    at_hi[rows, base:base + TILE] = hi
                    at_lo[rows, base:base + TILE] = lo
            return 0

        lax.fori_loop(0, in_tiles, one, 0)

    c_x = c + 1 - 2 * (c % 2)
    c_y = (c + 2) % C
    c_d = (c_x + 2) % C

    def gather_g(k, cond=None):
        blk = G.at[c, rows_of(k)]
        send(blk, blk, csend.at[k, 0], crecv.at[k, 0], dev(r, c_x, z), cond)
        send(blk, blk, csend.at[k, 1], crecv.at[k, 1], dev(r, c_y, z), cond)
        if k not in relays:
            send(blk, blk, csend.at[k, 2], crecv.at[k, 2], dev(r, c_d, z), cond)

    def relay(k, cond):
        at, n = chunks[k]
        first, second = pl.ds(at, n // 2), pl.ds(at + n // 2, n // 2)
        pl.when(cond)(lambda: recv(G.at[c_x, rows_of(k)], csend.at[k, 0], crecv.at[k, 0]))
        blk = G.at[c_x, first]
        send(blk, blk, csend.at[k, 2], crecv.at[k, 2], dev(r, c_y, z), cond)
        pl.when(cond)(lambda: recv(G.at[c_y, rows_of(k)], csend.at[k, 1], crecv.at[k, 1]))
        blk = G.at[c_y, second]
        send(blk, blk, csend.at[k, 3], crecv.at[k, 3], dev(r, c_x, z), cond)

    def consume(k):
        at, n = chunks[k]
        if k in relays:
            recv(G.at[c_d, pl.ds(at, n // 2)], csend.at[k, 2], crecv.at[k, 2])
            recv(G.at[c_d, pl.ds(at + n // 2, n // 2)], csend.at[k, 3], crecv.at[k, 3])
        else:
            for j, o in enumerate((c_x, c_y, c_d)):
                recv(G.at[o, rows_of(k)], csend.at[k, j], crecv.at[k, j])
        cols = slice(C * at, C * (at + n))
        g = split(G[:, at:at + n, :].reshape(C * n, D))
        step = IN // 4

        def block(rows):
            add = cat_nn((at_hi[rows, cols], at_lo[rows, cols]), g)
            if k == 0:
                ig_ref[rows, :] = add
            else:
                ig_ref[rows, :] += add

        for i in range(4):
            rows = pl.ds(i * step, step)
            block(rows)
            if k == K - 1:
                send(ig_ref.at[rows], igr.at[rows], irsend.at[i], irrecv.at[i], dev(1 - r, c, z))

    def own_cols(o):
        return pl.ds(pl.multiple_of(o * D, D), D)

    def end_cols(o):
        return pl.ds(pl.multiple_of((o - one_if(low)) * D, D), D)

    def times_w(os, rows, hi_w, lo_w, col_of):
        left, right = [], []
        for o in os:
            hi, lo = split(M[o, rows, :])
            cols = col_of(o)
            wh = hi_w[:, cols]
            left += [hi, lo, hi]
            right += [wh, wh, lo_w[:, cols]]
        return nt(jnp.concatenate(left, axis=1), jnp.concatenate(right, axis=1))

    whole = pl.ds(0, H)

    def partial_own():
        @pl.when(inner)
        def _():
            part[...] = times_w([e1], whole, we_hi, we_lo, end_cols)

    def partial(k):
        rows = rows_of(k)
        pc = part.at[rows]

        @pl.when(inner)
        def _():
            part[rows, :] += times_w([o1, o0], rows, we_hi, we_lo, end_cols)

        send(pc, pc, psend.at[k], precv.at[k], dev(r, c, z_out), inner)

    def agg_inner(k):
        rows = rows_of(k)

        @pl.when(inner)
        def _():
            G[c, rows, :] += times_w([e0, o1, o0], rows, w_hi, w_lo, own_cols)

        gather_g(k, inner)

    def agg_end(k):
        rows = rows_of(k)

        @pl.when(end)
        def _():
            if k in raws:
                for o in (e1, o1, o0):
                    zwait(o, k)
                G[c, rows, :] += times_w([e1, o1, o0], rows, w_hi, w_lo, own_cols)
            else:
                recv(part.at[rows], psend.at[k], precv.at[k])
                G[c, rows, :] += part[rows, :]

        gather_g(k, end)

    def end_weights(stage):
        if stage == 0:
            pl.when(inner)(lambda: recv(we_f.at[p], wesend.at[0], werecv.at[0]))
            for j in range(1, C):
                send(we_f.at[p], we_f.at[p], wesend.at[j], werecv.at[j], dev(r, (c + j) % C, z), inner)
        if stage == 1:
            @pl.when(inner)
            def _():
                for j in range(1, C):
                    recv(we_f.at[r * C + (c + C - j) % C], wesend.at[j], werecv.at[j])

            mine = pl.ds(r * C, C)
            send(we_f.at[mine], we_f.at[mine], wesend.at[C], werecv.at[C], dev(1 - r, c, z), inner)
        if stage == 2:
            @pl.when(inner)
            def _():
                recv(we_f.at[pl.ds((1 - r) * C, C)], wesend.at[C], werecv.at[C])
                for i in range(R * C):
                    rows = slice(i * sub, (i + 1) * sub)
                    we_hi[rows, :], we_lo[rows, :] = split(we_f[i])

    def arrived(k):
        for o in (o1, o0):
            pl.when(inner)(lambda: zwait(o, k))
            zout(o, k)


    for k in range(K):
        mask(k)
    pl.semaphore_wait(barrier, greeted)
    for k in raws:
        zpass(z, k)
        zout(z, k)
    cp_w.wait()
    cols = pl.ds(pl.multiple_of(jnp.where(low, D, 0), D), wide)
    rows = pl.ds(pl.multiple_of(p * sub, sub), sub)
    send(w_f.at[rows, cols], we_f.at[p], wesend.at[0], werecv.at[0], dev(r, c, z_in), end)
    zpass(z, 2, end)
    cp_sa.wait()
    sa_pass(0)
    for k in range(3, K):
        zpass(z, k, end)
    for t in range(1, T):
        sa_pass(t)
    for n in range(N):
        cols = slice(n * D, (n + 1) * D)
        w_hi[:, cols], w_lo[:, cols] = split(w_f[:, cols])
    wgrad_own()
    red_row(0, 0, 1)
    onward(0, [])
    G[c] = times_w([z], whole, w_hi, w_lo, own_cols)
    cp_t.wait()
    prep(0)
    onward(1, [2, 3])
    arrived(0)
    agg_inner(0)
    arrived(1)
    agg_inner(1)
    end_weights(0)
    red_col(0, 0, 1)
    prep(1)
    onward(2, range(4, K))
    agg_end(0)
    agg_end(1)
    prep(2)
    end_weights(1)
    red_out(0, 0, 1)
    prep(3)
    end_weights(2)
    partial_own()
    onward(3, [])
    arrived(2)
    partial(2)
    agg_inner(2)
    consume(0)
    agg_end(2)
    wgrad_mine(0, range(1, N))
    wgrad_ends(0)
    consume(1)
    onward(4, [])
    onward(5, [])
    arrived(3)
    partial(3)
    agg_inner(3)
    relay(2, inner)
    for t in range(1, T):
        wgrad_mine(t, [1])
    red_row(1, 1, 2, inner)
    arrived(4)
    partial(4)
    agg_inner(4)
    relay(2, end)
    agg_end(3)
    arrived(5)
    partial(5)
    agg_inner(5)
    relay(3, inner)
    red_col(1, 1, 2, inner)
    agg_end(4)
    for t in range(1, T):
        wgrad_mine(t, [2, 3])
    red_row(2, 2, N, inner)
    agg_end(5)
    consume(2)
    relay(3, end)
    wgrad_ends(1)
    red_col(2, 2, N, inner)
    consume(3)
    wgrad_ends(2)
    wgrad_ends(3)
    red_row(3, N, nb, inner)
    consume(4)
    red_col(3, N, nb, inner)
    consume(5)
    red_out(1, 1, 2, inner)
    red_out(2, 2, N, inner)
    red_out(3, N, nb, inner)
    for j in range(C):
        pl.when(far(same(my_r, j, my_z)))(lambda: recv(wgd.at[j], dsend.at[0], drecv.at[j]))
        wg_ref[j * sub:(j + 1) * sub, :] = wgd[j]
    for i in range(4):
        rows = pl.ds(i * (IN // 4), IN // 4)
        recv(igr.at[rows], irsend.at[i], irrecv.at[i])
    for cond, make in pending:
        if cond is None:
            make().wait_send()
        else:
            pl.when(cond)(lambda: make().wait_send())


def on_line(R, C, N, grad_out, relu_mask, saved_agg, weight, tile_vals, tile_pos, tile_count):
    H, D = grad_out.shape
    F = weight.shape[1]
    tiles = tile_vals[0, 0]
    slots = tiles.shape[0]
    IN = slots * TILE * TILE // (C * H)
    T = H // TILE
    half = TILE // 2
    fine = lambda at: [(at, half), (at + half, half)]
    chunks = fine(0) + [(t * TILE, TILE) for t in range(1, T - 1)] + fine(H - TILE)
    K = len(chunks)
    blk = F // (R * C)
    sub = D // (R * C)
    nb = 2 * N - 1
    s = jnp.arange(slots, dtype=jnp.int32)
    code = jnp.where(s < tile_count[0, 0], s, s + slots)
    where = jnp.sum(jnp.where(tile_pos[0, 0][None, :] == s[:, None], code[None, :], 0), axis=1).astype(jnp.int32)
    vmem = pl.BlockSpec(memory_space=pltpu.VMEM)
    hbm = pl.BlockSpec(memory_space=pl.ANY)
    dma = pltpu.SemaphoreType.DMA
    wg, ig, igr = pl.pallas_call(
        functools.partial(line_kernel, R, C, N, chunks, (0, 1), (2, 3)),
        out_shape=(
            jax.ShapeDtypeStruct((blk, D), F32),
            jax.ShapeDtypeStruct((IN, D), F32),
            jax.ShapeDtypeStruct((IN, D), F32),
        ),
        in_specs=[pl.BlockSpec(memory_space=pltpu.SMEM), vmem, vmem, hbm, hbm, hbm],
        out_specs=(vmem, vmem, vmem),
        scratch_shapes=[
            pltpu.VMEM((N, H, D), F32),
            pltpu.VMEM((C, H, D), F32),
            pltpu.VMEM((slots, TILE, TILE), F32),
            pltpu.VMEM((IN, C * H), BF16),
            pltpu.VMEM((IN, C * H), BF16),
            pltpu.VMEM((D, F), F32),
            pltpu.VMEM((D, F), BF16),
            pltpu.VMEM((D, F), BF16),
            pltpu.VMEM((H, D), F32),
            pltpu.VMEM((R * C, sub, (N - 1) * D), F32),
            pltpu.VMEM((D, (N - 1) * D), BF16),
            pltpu.VMEM((D, (N - 1) * D), BF16),
            pltpu.VMEM((T, TILE, D), F32),
            pltpu.VMEM((H, D), F32),
            pltpu.VMEM((nb, R, D // R, D), F32),
            pltpu.VMEM((nb, D // R, D), F32),
            pltpu.VMEM((C, nb, sub, D), F32),
            pltpu.VMEM((C, nb, sub, D), F32),
            pltpu.VMEM((nb, sub, D), F32),
            pltpu.VMEM((C, sub, D), F32),
            dma((3,)),
            dma((2, N, K)), dma((N, K)),
            dma((C + 1,)), dma((C + 1,)),
            dma((T,)), dma((T,)),
            dma((K,)), dma((K,)),
            dma((K, C)), dma((K, C)),
            dma((4,)), dma((4,)),
            dma((4, C)), dma((4, C)),
            dma((nb,)), dma((C,)),
            dma((4,)), dma((4,)),
        ],
        compiler_params=pltpu.CompilerParams(
            collective_id=0, has_side_effects=True, vmem_limit_bytes=60 * 1024 * 1024
        ),
    )(where, grad_out, relu_mask, saved_agg, weight, tiles)

    def finish(wg_in, a, b, wg_out, ig_out):
        wg_out[...] = wg_in[...]
        ig_out[...] = a[...] + b[...]

    return pl.pallas_call(
        finish,
        out_shape=(jax.ShapeDtypeStruct((blk, D), F32), jax.ShapeDtypeStruct((IN, D), F32)),
        in_specs=[vmem, vmem, vmem],
        out_specs=(vmem, vmem),
    )(wg, ig, igr)


def per_device(R, C, N, grad_out, *rest):
    H, D = grad_out.shape
    line = R == 2 and C == 4 and N == 4 and D % (8 * R * C) == 0
    line = line and H % TILE == 0 and H // TILE == 4
    return (on_line if line else general)(R, C, N, grad_out, *rest)


def solution(mesh):
    in_specs = (
        P(("row", "col"), "ch"),
        P(("row", "col"), "ch"),
        P(("row", "col"), "ch"),
        P("ch", None),
        P("row", "col", None, None, None),
        P("row", "col", None),
        P("row", "col"),
    )
    out_specs = (P(("row", "col"), "ch"), P("col", "ch"))
    R, C, N = mesh.shape["row"], mesh.shape["col"], mesh.shape["ch"]
    return jax.shard_map(
        functools.partial(per_device, R, C, N), mesh=mesh, in_specs=in_specs, out_specs=out_specs, check_vma=False
    )
```

```python
import functools

import jax
import jax.numpy as jnp
from jax import lax
from jax.experimental import pallas as pl
from jax.experimental.pallas import tpu as pltpu
from jax.sharding import PartitionSpec as P

TILE = 128
MESH = pl.DeviceIdType.MESH
F32 = jnp.float32
BF16 = jnp.bfloat16


def split(x):
    hi = x.astype(BF16)
    return hi, (x - hi.astype(F32)).astype(BF16)


def nn(a, b):
    return lax.dot_general(a, b, (((1,), (0,)), ((), ())), preferred_element_type=F32)


def nt(a, b):
    return lax.dot_general(a, b, (((1,), (1,)), ((), ())), preferred_element_type=F32)


def kernel(
    R, C, N, K,
    slot_ref, g_ref, mask_ref, sa_hbm, w_hbm, tiles_hbm,
    wg_ref, ig_ref, igr,
    M, G, tiles, at_hi, at_lo, w_f, w_hi, w_lo, sa, g_hi, g_lo,
    wgp, wgr, wgs, wgc, wgo,
    local_sem, zsend, zrecv, csend, crecv, wrsend, wrrecv, wcsend, wcrecv, wfsend, wfrecv,
    irsend, irrecv, iasend, iarecv,
):
    r, c, z = lax.axis_index("row"), lax.axis_index("col"), lax.axis_index("ch")
    HB, D = M.shape[2], M.shape[3]
    RC = R * C
    per = RC // N
    blk = wgp.shape[1]
    slots = tiles.shape[0]
    acc = ig_ref
    IN = acc.shape[0]
    in_tiles = IN // TILE
    tpb = HB // TILE
    piece = IN // R

    cp_w = pltpu.make_async_copy(w_hbm, w_f, local_sem.at[0])
    cp_sa = pltpu.make_async_copy(sa_hbm, sa, local_sem.at[1])
    cp_t = pltpu.make_async_copy(tiles_hbm, tiles, local_sem.at[2])
    cp_w.start()
    cp_sa.start()
    cp_t.start()

    def dev(r_, c_, z_):
        return {"row": r_, "col": c_, "ch": z_}

    q = r * C + c
    d_idx = z * per + q // N
    d_r, d_c, d_z = d_idx // C, d_idx % C, q % N
    s_q = (q % per) * N + z
    s_r, s_c, s_z = s_q // C, s_q % C, q // per
    away = jnp.logical_not((d_r == r) & (d_c == c) & (d_z == z))

    barrier = pltpu.get_barrier_semaphore()

    def hello(r_, c_, z_):
        pl.semaphore_signal(barrier, inc=1, device_id=dev(r_, c_, z_), device_id_type=MESH)

    for j in range(1, R):
        hello((r + j) % R, c, z)
    for j in range(1, C):
        hello(r, (c + j) % C, z)

    @pl.when(z > 0)
    def _():
        hello(r, c, z - 1)

    @pl.when(z < N - 1)
    def _():
        hello(r, c, z + 1)

    @pl.when(away)
    def _():
        hello(d_r, d_c, d_z)
        hello(s_r, s_c, s_z)

    def own(k):
        rows = pl.ds(pl.multiple_of(k * HB, HB), HB)
        M[z, k] = g_ref[rows, :] * mask_ref[rows, :].astype(F32)

    own(0)
    own(1)
    one_if = lambda cond: jnp.where(cond, 1, 0)
    greeted = R - 1 + C - 1 + one_if(z > 0) + one_if(z < N - 1) + 2 * one_if(away)
    pl.semaphore_wait(barrier, greeted)

    def zcopy(origin, k, step):
        way = 0 if step < 0 else 1
        return pltpu.make_async_remote_copy(
            src_ref=M.at[origin, k], dst_ref=M.at[origin, k],
            send_sem=zsend.at[way, origin, k], recv_sem=zrecv.at[origin, k],
            device_id=dev(r, c, z + step), device_id_type=MESH,
        )

    def own_send(k):
        @pl.when(z > 0)
        def _():
            zcopy(z, k, -1).start()

        @pl.when(z < N - 1)
        def _():
            zcopy(z, k, 1).start()

    own_send(0)
    own_send(1)
    acc[...] = jnp.zeros_like(acc)
    wgp[...] = jnp.zeros_like(wgp)
    cp_w.wait()
    for n in range(N):
        cols = slice(n * D, (n + 1) * D)
        w_hi[:, cols], w_lo[:, cols] = split(w_f[:, cols])
    cp_sa.wait()
    cp_t.wait()

    def prep(k, cc):
        for t in range(tpb):
            def one(i, _):
                p = ((cc * K + k) * tpb + t) * in_tiles + i
                v = slot_ref[p]
                tile = tiles[lax.rem(v, slots)]
                tile = jnp.where(v < slots, tile, jnp.zeros_like(tile))
                hi, lo = split(tile.T)
                rows = pl.ds(pl.multiple_of(i * TILE, TILE), TILE)
                cols = slice(cc * HB + t * TILE, cc * HB + (t + 1) * TILE)
                at_hi[k, rows, cols] = hi
                at_lo[k, rows, cols] = lo
                return 0

            lax.fori_loop(0, in_tiles, one, 0, unroll=2)

    def ccopy(k, j):
        return pltpu.make_async_remote_copy(
            src_ref=G.at[k, c], dst_ref=G.at[k, c],
            send_sem=csend.at[k, j], recv_sem=crecv.at[k, j],
            device_id=dev(r, (c + j) % C, z), device_id_type=MESH,
        )

    def cwait(k, j):
        o = (c + C - j) % C
        return pltpu.make_async_remote_copy(
            src_ref=G.at[k, o], dst_ref=G.at[k, o],
            send_sem=csend.at[k, j], recv_sem=crecv.at[k, j],
            device_id=dev(r, (c + j) % C, z), device_id_type=MESH,
        )

    def consume(k):
        for j in range(1, C):
            cwait(k, j).wait_recv()
        for n in range(C):
            rows = slice(n * HB, (n + 1) * HB)
            g_hi[rows, :], g_lo[rows, :] = split(G[k, n])

        def part(i, _):
            rows = pl.ds(pl.multiple_of(i * 256, 256), 256)
            a = at_hi[k, rows, :]
            acc[rows, :] += nn(a, g_hi[...]) + nn(a, g_lo[...]) + nn(at_lo[k, rows, :], g_hi[...])
            return 0

        lax.fori_loop(0, IN // 256, part, 0)

    def wrcopy(j):
        t = (r + j) % R
        return pltpu.make_async_remote_copy(
            src_ref=wgp.at[pl.ds(t * C, C)], dst_ref=wgr.at[j],
            send_sem=wrsend.at[j], recv_sem=wrrecv.at[j],
            device_id=dev(t, c, z), device_id_type=MESH,
        )

    groups = [[] for _ in range(N - 1)]
    for cc in range(C):
        groups[cc * max(N - 2, 1) // C].append(cc)

    def body(k, _):
        for d in range(1, N):
            @pl.when(z >= d)
            def _():
                zcopy(z - d, k, 1).wait_recv()

                @pl.when(z < N - 1)
                def _():
                    zcopy(z - d, k, 1).start()

            @pl.when(z + d < N)
            def _():
                zcopy(z + d, k, -1).wait_recv()

                @pl.when(z > 0)
                def _():
                    zcopy(z + d, k, -1).start()

            if d == 1:
                @pl.when(k + 2 < K)
                def _():
                    own(k + 2)
                    own_send(k + 2)

            for cc in groups[d - 1]:
                prep(k, cc)

        agg = jnp.zeros((HB, D), F32)
        for n in range(N):
            cols = slice(n * D, (n + 1) * D)
            hi, lo = split(M[n, k])
            agg += nt(hi, w_hi[:, cols]) + nt(lo, w_hi[:, cols]) + nt(hi, w_lo[:, cols])
        G[k, c] = agg
        for j in range(1, C):
            ccopy(k, j).start()

        rows = pl.ds(pl.multiple_of(k * HB, HB), HB)
        s_hi, s_lo = split(sa[rows, :].T)
        for n in range(N):
            hi, lo = split(M[n, k])
            res = nn(s_hi, hi) + nn(s_hi, lo) + nn(s_lo, hi)
            for h in range(per):
                wgp[h * N + n] += res[h * blk:(h + 1) * blk, :]

        @pl.when(k == K - 1)
        def _():
            for j in range(1, R):
                wrcopy(j).start()

        @pl.when(k > 0)
        def _():
            consume(k - 1)

        return 0

    lax.fori_loop(0, K, body, 0)

    def wccopy(j):
        t = (c + j) % C
        return pltpu.make_async_remote_copy(
            src_ref=wgs.at[t], dst_ref=wgc.at[j],
            send_sem=wcsend.at[j], recv_sem=wcrecv.at[j],
            device_id=dev(r, t, z), device_id_type=MESH,
        )

    wfcopy = pltpu.make_async_remote_copy(
        src_ref=wgo, dst_ref=wg_ref, send_sem=wfsend, recv_sem=wfrecv,
        device_id=dev(d_r, d_c, d_z), device_id_type=MESH,
    )

    def ircopy(j):
        t = (r + j) % R
        whole = R == 2
        rows = pl.ds(0, IN) if whole else pl.ds(pl.multiple_of(t * piece, piece), piece)
        return pltpu.make_async_remote_copy(
            src_ref=acc.at[rows], dst_ref=igr if whole else igr.at[j],
            send_sem=irsend.at[j], recv_sem=irrecv.at[j],
            device_id=dev(t, c, z), device_id_type=MESH,
        )

    mine = pl.ds(pl.multiple_of(r * piece, piece), piece)

    def iacopy(j):
        return pltpu.make_async_remote_copy(
            src_ref=ig_ref.at[mine], dst_ref=ig_ref.at[mine],
            send_sem=iasend.at[j], recv_sem=iarecv.at[j],
            device_id=dev((r + j) % R, c, z), device_id_type=MESH,
        )

    def iawait(j):
        theirs = pl.ds(pl.multiple_of(((r + R - j) % R) * piece, piece), piece)
        return pltpu.make_async_remote_copy(
            src_ref=ig_ref.at[theirs], dst_ref=ig_ref.at[theirs],
            send_sem=iasend.at[j], recv_sem=iarecv.at[j],
            device_id=dev((r + j) % R, c, z), device_id_type=MESH,
        )

    for j in range(1, R):
        wrcopy(j).wait_recv()
    total = wgp[pl.ds(r * C, C)]
    for j in range(1, R):
        total += wgr[j]
    wgs[...] = total
    for j in range(1, C):
        wccopy(j).start()

    consume(K - 1)
    for j in range(1, R):
        ircopy(j).start()
    for j in range(1, C):
        wccopy(j).wait_recv()
    wpart = wgs[c]
    for j in range(1, C):
        wpart += wgc[j]

    @pl.when(away)
    def _():
        wgo[...] = wpart
        wfcopy.start()
        wfcopy.wait()

    @pl.when(jnp.logical_not(away))
    def _():
        wg_ref[...] = wpart

    for j in range(1, R):
        ircopy(j).wait_recv()
    if R > 2:
        summed = acc[mine, :]
        for j in range(1, R):
            summed += igr[j]
        ig_ref[mine, :] = summed
        for j in range(1, R):
            iacopy(j).start()
        for j in range(1, R):
            iawait(j).wait_recv()

    for j in range(1, R):
        wrcopy(j).wait_send()
        ircopy(j).wait_send()
        if R > 2:
            iacopy(j).wait_send()
    for j in range(1, C):
        wccopy(j).wait_send()

    def drain(k, _):
        for j in range(1, C):
            ccopy(k, j).wait_send()
        for n in range(N):
            @pl.when((z > 0) & (z <= n))
            def _():
                zcopy(n, k, -1).wait_send()

            @pl.when((z < N - 1) & (z >= n))
            def _():
                zcopy(n, k, 1).wait_send()

        return 0

    lax.fori_loop(0, K, drain, 0)


def general(R, C, N, grad_out, relu_mask, saved_agg, weight, tile_vals, tile_pos, tile_count):
    H, D = grad_out.shape
    F = weight.shape[1]
    tiles = tile_vals[0, 0]
    slots = tiles.shape[0]
    out_rows = C * H
    IN = slots * TILE * TILE // out_rows
    HB = TILE
    K = H // HB
    blk = F // (R * C)
    s = jnp.arange(slots, dtype=jnp.int32)
    code = jnp.where(s < tile_count[0, 0], s, s + slots)
    where = jnp.sum(jnp.where(tile_pos[0, 0][None, :] == s[:, None], code[None, :], 0), axis=1).astype(jnp.int32)
    vmem = pl.BlockSpec(memory_space=pltpu.VMEM)
    hbm = pl.BlockSpec(memory_space=pl.ANY)
    dma = pltpu.SemaphoreType.DMA
    igr_shape = (IN, D) if R == 2 else (R, IN // R, D)
    wg, ig, igr = pl.pallas_call(
        functools.partial(kernel, R, C, N, K),
        out_shape=(
            jax.ShapeDtypeStruct((blk, D), F32),
            jax.ShapeDtypeStruct((IN, D), F32),
            jax.ShapeDtypeStruct(igr_shape, F32),
        ),
        in_specs=[pl.BlockSpec(memory_space=pltpu.SMEM), vmem, vmem, hbm, hbm, hbm],
        out_specs=(vmem, vmem, vmem),
        scratch_shapes=[
            pltpu.VMEM((N, K, HB, D), F32),
            pltpu.VMEM((K, C, HB, D), F32),
            pltpu.VMEM((slots, TILE, TILE), F32),
            pltpu.VMEM((K, IN, C * HB), BF16),
            pltpu.VMEM((K, IN, C * HB), BF16),
            pltpu.VMEM((D, F), F32),
            pltpu.VMEM((D, F), BF16),
            pltpu.VMEM((D, F), BF16),
            pltpu.VMEM((H, D), F32),
            pltpu.VMEM((C * HB, D), BF16),
            pltpu.VMEM((C * HB, D), BF16),
            pltpu.VMEM((R * C, blk, D), F32),
            pltpu.VMEM((R, C, blk, D), F32),
            pltpu.VMEM((C, blk, D), F32),
            pltpu.VMEM((C, blk, D), F32),
            pltpu.VMEM((blk, D), F32),
            dma((3,)),
            dma((2, N, K)), dma((N, K)),
            dma((K, C)), dma((K, C)),
            dma((R,)), dma((R,)),
            dma((C,)), dma((C,)),
            dma, dma,
            dma((R,)), dma((R,)),
            dma((R,)), dma((R,)),
        ],
        compiler_params=pltpu.CompilerParams(
            collective_id=0, has_side_effects=True, vmem_limit_bytes=60 * 1024 * 1024
        ),
    )(where, grad_out, relu_mask, saved_agg, weight, tiles)

    def finish(wg_in, a, b, wg_out, ig_out):
        wg_out[...] = wg_in[...]
        ig_out[...] = a[...] + b[...] if R == 2 else a[...]

    return pl.pallas_call(
        finish,
        out_shape=(jax.ShapeDtypeStruct((blk, D), F32), jax.ShapeDtypeStruct((IN, D), F32)),
        in_specs=[vmem, vmem, vmem if R == 2 else hbm],
        out_specs=(vmem, vmem),
    )(wg, ig, igr)


def cat_nn(a, b):
    return nn(jnp.concatenate([a[0], a[0], a[1]], axis=1), jnp.concatenate([b[0], b[1], b[0]], axis=0))


def line_kernel(
    R, C, N, chunks, raws, relays_end, relays_inner,
    slot_ref, g_ref, mask_ref, sa_hbm, w_hbm, tiles_hbm,
    wg_ref, ig_ref, igr,
    M, G, tiles, at_hi, at_lo, w_f, w_hi, w_lo, sa,
    we_f, we_hi, we_lo, sae, part, wgp, wgr, wgs, wgc, wgo, wgd,
    local_sem, zsend, zrecv, wesend, werecv, sasend, sarecv, psend, precv,
    csend, crecv, rsend, rrecv, tsend, trecv, dsend, drecv, irsend, irrecv,
):
    r, c, z = lax.axis_index("row"), lax.axis_index("col"), lax.axis_index("ch")
    H, D = M.shape[1], M.shape[2]
    T, K = H // TILE, len(chunks)
    per = R * C // N
    sub = wgo.shape[1]
    slots = tiles.shape[0]
    IN = ig_ref.shape[0]
    in_tiles = IN // TILE
    wide = (N - 1) * D
    nb = 2 * N - 1

    low = z < N // 2
    end = (z == 0) | (z == N - 1)
    inner = jnp.logical_not(end)
    z_in = jnp.where(low, z + 1, z - 1)
    z_out = jnp.where(low, z - 1, z + 1)
    e0 = jnp.where(low, 0, N - 1)
    e1 = jnp.where(low, 1, N - 2)
    o1 = jnp.where(low, 2, N - 3)
    o0 = jnp.where(low, N - 1, 0)
    p = r * C + c

    cp_w = pltpu.make_async_copy(w_hbm, w_f, local_sem.at[0])
    cp_sa = pltpu.make_async_copy(sa_hbm, sa, local_sem.at[1])
    cp_t = pltpu.make_async_copy(tiles_hbm, tiles, local_sem.at[2])
    cp_w.start()
    cp_sa.start()
    cp_t.start()

    def dev(r_, c_, z_):
        return {"row": r_, "col": c_, "ch": z_}

    one_if = lambda cond: jnp.where(cond, 1, 0)
    same = lambda r_, c_, z_: (r_ == r) & (c_ == c) & (z_ == z)
    far = jnp.logical_not

    own_q = per * z + r
    end_q = per * e0 + r
    block_n = [z, e0, o1, o0, e1, o1, o0]
    block_q = [own_q] * N + [end_q] * (N - 1)

    def goal(b):
        return block_q[b] // C, block_q[b] % C, block_n[b]

    my_a, my_r = p // per, p % per
    my_z = jnp.where(my_a == z, z, jnp.where(my_a == 0, 1, jnp.where(my_a == N - 1, N - 2, my_a)))

    barrier = pltpu.get_barrier_semaphore()

    def hello(r_, c_, z_):
        pl.semaphore_signal(barrier, inc=1, device_id=dev(r_, c_, z_), device_id_type=MESH)

    hello(1 - r, c, z)
    for j in range(1, C):
        hello(r, (c + j) % C, z)
    hello(r, c, z_in)
    pl.when(inner)(lambda: hello(r, c, z_out))
    for j in range(C):
        pl.when(far(same(my_r, j, my_z)))(lambda: hello(my_r, j, my_z))
    greeted = R - 1 + C - 1 + 1 + one_if(inner) + one_if(far(same(*goal(0))))
    for b in range(1, nb):
        greeted += one_if(inner & far(same(*goal(b))))

    def rows_of(k):
        return pl.ds(*chunks[k])

    for k in range(K):
        rows = rows_of(k)
        M[z, rows, :] = g_ref[rows, :] * mask_ref[rows, :].astype(F32)
    pl.semaphore_wait(barrier, greeted)

    def program(at_end):
        relays = relays_end if at_end else relays_inner
        pending = []

        def send(src, dst, ss, rs, to, cond=None):
            def make():
                return pltpu.make_async_remote_copy(
                    src_ref=src, dst_ref=dst, send_sem=ss, recv_sem=rs, device_id=to, device_id_type=MESH
                )

            pending.append((cond, make))
            if cond is None:
                make().start()
            else:
                pl.when(cond)(lambda: make().start())

        def recv(dst, ss, rs):
            pltpu.make_async_remote_copy(
                src_ref=dst, dst_ref=dst, send_sem=ss, recv_sem=rs, device_id=dev(1 - r, c, z), device_id_type=MESH
            ).wait_recv()

        def zpass(o, k):
            blk = M.at[o, rows_of(k)]
            send(blk, blk, zsend.at[0, o, k], zrecv.at[o, k], dev(r, c, z_in))

        def zout(o, k):
            if k in raws:
                blk = M.at[o, rows_of(k)]
                send(blk, blk, zsend.at[1, o, k], zrecv.at[o, k], dev(r, c, z_out))

        def zwait(o, k):
            recv(M.at[o, rows_of(k)], zsend.at[0, o, k], zrecv.at[o, k])

        def onward(k):
            zwait(e0, k)
            zpass(e0, k)

        def arrive(o, k):
            zwait(o, k)
            zout(o, k)

        def weights_pass():
            cols = pl.ds(pl.multiple_of(jnp.where(low, D, 0), D), wide)
            rows = pl.ds(pl.multiple_of(p * sub, sub), sub)
            send(w_f.at[rows, cols], we_f.at[p], wesend.at[0], werecv.at[0], dev(r, c, z_in))

        def sa_pass(t):
            send(sa.at[pl.ds(t * TILE, TILE)], sae.at[t], sasend.at[t], sarecv.at[t], dev(r, c, z_in))

        def outer(s, m):
            return cat_nn(s, split(m))

        def wadd(b, value, first):
            value = value.reshape(R, D // R, D)
            if first:
                wgp[b] = value
            else:
                wgp[b] += value

        def sa_own(t):
            return split(sa[t * TILE:(t + 1) * TILE, :].T)

        def tile_rows(o, t):
            return M[o, t * TILE:(t + 1) * TILE, :]

        def wgrad_own():
            for t in range(T):
                wadd(0, outer(sa_own(t), tile_rows(z, t)), t == 0)

        def wgrad_mine(t, bs):
            s = sa_own(t)
            for b in bs:
                wadd(b, outer(s, tile_rows(block_n[b], t)), t == 0)

        def wgrad_ends(t):
            recv(sae.at[t], sasend.at[t], sarecv.at[t])
            s = split(sae[t].T)
            for b in range(N, nb):
                wadd(b, outer(s, tile_rows(block_n[b], t)), t == 0)

        groups = ((0, 1), (1, 2), (2, N), (N, nb))

        def red_row(n):
            lo, hi = groups[n]
            bs = pl.ds(lo, hi - lo)
            send(wgp.at[bs, 1 - r], wgr.at[bs], rsend.at[n], rrecv.at[n], dev(1 - r, c, z))

        def red_col(n):
            lo, hi = groups[n]
            bs = pl.ds(lo, hi - lo)
            recv(wgr.at[bs], rsend.at[n], rrecv.at[n])
            for b in range(lo, hi):
                total = wgp[b, r] + wgr[b]
                for t in range(C):
                    wgs[t, b] = total[t * sub:(t + 1) * sub]
            for j in range(1, C):
                t = (c + j) % C
                send(wgs.at[t, bs], wgc.at[j, bs], tsend.at[n, j], trecv.at[n, j], dev(r, t, z))

        def red_out(n):
            lo, hi = groups[n]
            bs = pl.ds(lo, hi - lo)
            for j in range(1, C):
                recv(wgc.at[j, bs], tsend.at[n, j], trecv.at[n, j])
            for b in range(lo, hi):
                total = wgs[c, b]
                for j in range(1, C):
                    total += wgc[j, b]
                wgo[b] = total
                send(wgo.at[b], wgd.at[c], dsend.at[b], drecv.at[c], dev(*goal(b)), far(same(*goal(b))))

                @pl.when(same(*goal(b)))
                def _():
                    wgd[c] = wgo[b]

        def prep(t):
            inside = [k for k, (at, n) in enumerate(chunks) if at // TILE == t]
            HB = chunks[inside[0]][1]
            two = TILE // HB

            def one(i, _):
                rows = pl.ds(pl.multiple_of(i * TILE, TILE), TILE)
                for m in range(C // two):
                    got = []
                    for j in range(two):
                        v = slot_ref[((two * m + j) * T + t) * in_tiles + i]
                        tile = tiles[lax.rem(v, slots)]
                        got.append(jnp.where(v < slots, tile, jnp.zeros_like(tile)))
                    for h, k in enumerate(inside):
                        mix = jnp.concatenate([x[h * HB:(h + 1) * HB] for x in got], axis=0)
                        hi, lo = split(mix.T)
                        base = C * chunks[k][0] + m * TILE
                        at_hi[rows, base:base + TILE] = hi
                        at_lo[rows, base:base + TILE] = lo
                return 0

            lax.fori_loop(0, in_tiles, one, 0)

        c_x = c + 1 - 2 * (c % 2)
        c_y = (c + 2) % C
        c_d = (c_x + 2) % C

        def gather_g(k):
            blk = G.at[c, rows_of(k)]
            send(blk, blk, csend.at[k, 0], crecv.at[k, 0], dev(r, c_x, z))
            send(blk, blk, csend.at[k, 1], crecv.at[k, 1], dev(r, c_y, z))
            if k not in relays:
                send(blk, blk, csend.at[k, 2], crecv.at[k, 2], dev(r, c_d, z))

        def relay(k):
            at, n = chunks[k]
            first, second = pl.ds(at, n // 2), pl.ds(at + n // 2, n // 2)
            recv(G.at[c_x, rows_of(k)], csend.at[k, 0], crecv.at[k, 0])
            blk = G.at[c_x, first]
            send(blk, blk, csend.at[k, 2], crecv.at[k, 2], dev(r, c_y, z))
            recv(G.at[c_y, rows_of(k)], csend.at[k, 1], crecv.at[k, 1])
            blk = G.at[c_y, second]
            send(blk, blk, csend.at[k, 3], crecv.at[k, 3], dev(r, c_x, z))

        def consume(k, last=False):
            at, n = chunks[k]
            if k in relays:
                recv(G.at[c_d, pl.ds(at, n // 2)], csend.at[k, 2], crecv.at[k, 2])
                recv(G.at[c_d, pl.ds(at + n // 2, n // 2)], csend.at[k, 3], crecv.at[k, 3])
            else:
                for j, o in enumerate((c_x, c_y, c_d)):
                    recv(G.at[o, rows_of(k)], csend.at[k, j], crecv.at[k, j])
            cols = slice(C * at, C * (at + n))
            g = split(G[:, at:at + n, :].reshape(C * n, D))
            step = IN // 4

            def block(rows):
                add = cat_nn((at_hi[rows, cols], at_lo[rows, cols]), g)
                if k == 0:
                    ig_ref[rows, :] = add
                else:
                    ig_ref[rows, :] += add

            for i in range(4):
                rows = pl.ds(i * step, step)
                block(rows)
                if last:
                    send(ig_ref.at[rows], igr.at[rows], irsend.at[i], irrecv.at[i], dev(1 - r, c, z))

        def own_cols(o):
            return pl.ds(pl.multiple_of(o * D, D), D)

        def end_cols(o):
            return pl.ds(pl.multiple_of((o - one_if(low)) * D, D), D)

        def times_w(os, rows, hi_w, lo_w, col_of):
            left, right = [], []
            for o in os:
                hi, lo = split(M[o, rows, :])
                cols = col_of(o)
                wh = hi_w[:, cols]
                left += [hi, lo, hi]
                right += [wh, wh, lo_w[:, cols]]
            return nt(jnp.concatenate(left, axis=1), jnp.concatenate(right, axis=1))

        whole = pl.ds(0, H)

        def partial_own():
            part[...] = times_w([e1], whole, we_hi, we_lo, end_cols)

        def partial(k):
            rows = rows_of(k)
            part[rows, :] += times_w([o1, o0], rows, we_hi, we_lo, end_cols)
            pc = part.at[rows]
            send(pc, pc, psend.at[k], precv.at[k], dev(r, c, z_out))

        def agg_own():
            G[c] = times_w([z], whole, w_hi, w_lo, own_cols)

        def agg_inner(k):
            rows = rows_of(k)
            G[c, rows, :] += times_w([e0, o1, o0], rows, w_hi, w_lo, own_cols)
            gather_g(k)

        def agg_end(k):
            rows = rows_of(k)
            if k in raws:
                for o in (e1, o1, o0):
                    zwait(o, k)
                G[c, rows, :] += times_w([e1, o1, o0], rows, w_hi, w_lo, own_cols)
            else:
                recv(part.at[rows], psend.at[k], precv.at[k])
                G[c, rows, :] += part[rows, :]
            gather_g(k)

        def end_weights(stage):
            if stage == 0:
                recv(we_f.at[p], wesend.at[0], werecv.at[0])
                for j in range(1, C):
                    send(we_f.at[p], we_f.at[p], wesend.at[j], werecv.at[j], dev(r, (c + j) % C, z))
            elif stage == 1:
                for j in range(1, C):
                    recv(we_f.at[r * C + (c + C - j) % C], wesend.at[j], werecv.at[j])
                mine = pl.ds(r * C, C)
                send(we_f.at[mine], we_f.at[mine], wesend.at[C], werecv.at[C], dev(1 - r, c, z))
            else:
                recv(we_f.at[pl.ds((1 - r) * C, C)], wesend.at[C], werecv.at[C])
                for i in range(R * C):
                    rows = slice(i * sub, (i + 1) * sub)
                    we_hi[rows, :], we_lo[rows, :] = split(we_f[i])

        def split_w():
            for n in range(N):
                cols = slice(n * D, (n + 1) * D)
                w_hi[:, cols], w_lo[:, cols] = split(w_f[:, cols])

        def finish_all():
            for j in range(C):
                pl.when(far(same(my_r, j, my_z)))(lambda: recv(wgd.at[j], dsend.at[0], drecv.at[j]))
                wg_ref[j * sub:(j + 1) * sub, :] = wgd[j]
            for i in range(4):
                rows = pl.ds(i * (IN // 4), IN // 4)
                recv(igr.at[rows], irsend.at[i], irrecv.at[i])
            for cond, make in pending:
                if cond is None:
                    make().wait_send()
                else:
                    pl.when(cond)(lambda: make().wait_send())

        if at_end:
            zpass(z, 0)
            cp_w.wait()
            weights_pass()
            zpass(z, 1)
            zpass(z, 2)
            cp_sa.wait()
            sa_pass(0)
            zpass(z, 3)
            zpass(z, 4)
            zpass(z, 5)
            sa_pass(1)
            sa_pass(2)
            sa_pass(3)
            split_w()
            agg_own()
            cp_t.wait()
            prep(0)
            wgrad_own()
            red_row(0)
            prep(1)
            red_col(0)
            agg_end(0)
            agg_end(1)
            prep(2)
            prep(3)
            red_out(0)
            consume(0)
            consume(1)
            agg_end(2)
            agg_end(3)
            relay(2)
            agg_end(4)
            agg_end(5)
            relay(3)
            consume(2)
            consume(4)
            consume(5)
            consume(3, True)
        else:
            zpass(z, 0)
            zout(z, 0)
            zpass(z, 1)
            zout(z, 1)
            cp_w.wait()
            split_w()
            cp_t.wait()
            prep(0)
            agg_own()
            onward(0)
            zpass(z, 2)
            end_weights(0)
            prep(1)
            onward(1)
            zpass(z, 3)
            arrive(o1, 0)
            arrive(o0, 0)
            agg_inner(0)
            onward(2)
            zpass(z, 4)
            zpass(z, 5)
            cp_sa.wait()
            wgrad_own()
            red_row(0)
            arrive(o1, 1)
            arrive(o0, 1)
            agg_inner(1)
            relay(0)
            prep(2)
            end_weights(1)
            red_col(0)
            onward(3)
            relay(1)
            end_weights(2)
            partial_own()
            arrive(o1, 2)
            arrive(o0, 2)
            partial(2)
            agg_inner(2)
            onward(4)
            onward(5)
            consume(0)
            prep(3)
            consume(1)
            red_out(0)
            wgrad_ends(0)
            arrive(o1, 3)
            arrive(o0, 3)
            partial(3)
            agg_inner(3)
            wgrad_mine(0, (1, 2, 3))
            arrive(o1, 4)
            arrive(o0, 4)
            partial(4)
            agg_inner(4)
            relay(2)
            wgrad_mine(1, (1,))
            wgrad_mine(2, (1,))
            wgrad_mine(3, (1,))
            red_row(1)
            arrive(o1, 5)
            arrive(o0, 5)
            partial(5)
            agg_inner(5)
            wgrad_ends(1)
            wgrad_ends(2)
            wgrad_ends(3)
            red_row(3)
            wgrad_mine(1, (2, 3))
            wgrad_mine(2, (2, 3))
            wgrad_mine(3, (2, 3))
            red_row(2)
            red_col(3)
            red_col(2)
            red_col(1)
            relay(3)
            relay(4)
            relay(5)
            consume(2)
            red_out(3)
            consume(3)
            consume(4)
            red_out(2)
            red_out(1)
            consume(5, True)
        finish_all()

    pl.when(end)(lambda: program(True))
    pl.when(inner)(lambda: program(False))


def on_line(R, C, N, grad_out, relu_mask, saved_agg, weight, tile_vals, tile_pos, tile_count):
    H, D = grad_out.shape
    F = weight.shape[1]
    tiles = tile_vals[0, 0]
    slots = tiles.shape[0]
    IN = slots * TILE * TILE // (C * H)
    T = H // TILE
    half = TILE // 2
    fine = lambda at: [(at, half), (at + half, half)]
    chunks = fine(0) + [(t * TILE, TILE) for t in range(1, T - 1)] + fine(H - TILE)
    K = len(chunks)
    blk = F // (R * C)
    sub = D // (R * C)
    nb = 2 * N - 1
    s = jnp.arange(slots, dtype=jnp.int32)
    code = jnp.where(s < tile_count[0, 0], s, s + slots)
    where = jnp.sum(jnp.where(tile_pos[0, 0][None, :] == s[:, None], code[None, :], 0), axis=1).astype(jnp.int32)
    vmem = pl.BlockSpec(memory_space=pltpu.VMEM)
    hbm = pl.BlockSpec(memory_space=pl.ANY)
    dma = pltpu.SemaphoreType.DMA
    wg, ig, igr = pl.pallas_call(
        functools.partial(line_kernel, R, C, N, chunks, (0, 1), (2, 3), (0, 1, 2, 3, 4, 5)),
        out_shape=(
            jax.ShapeDtypeStruct((blk, D), F32),
            jax.ShapeDtypeStruct((IN, D), F32),
            jax.ShapeDtypeStruct((IN, D), F32),
        ),
        in_specs=[pl.BlockSpec(memory_space=pltpu.SMEM), vmem, vmem, hbm, hbm, hbm],
        out_specs=(vmem, vmem, vmem),
        scratch_shapes=[
            pltpu.VMEM((N, H, D), F32),
            pltpu.VMEM((C, H, D), F32),
            pltpu.VMEM((slots, TILE, TILE), F32),
            pltpu.VMEM((IN, C * H), BF16),
            pltpu.VMEM((IN, C * H), BF16),
            pltpu.VMEM((D, F), F32),
            pltpu.VMEM((D, F), BF16),
            pltpu.VMEM((D, F), BF16),
            pltpu.VMEM((H, D), F32),
            pltpu.VMEM((R * C, sub, (N - 1) * D), F32),
            pltpu.VMEM((D, (N - 1) * D), BF16),
            pltpu.VMEM((D, (N - 1) * D), BF16),
            pltpu.VMEM((T, TILE, D), F32),
            pltpu.VMEM((H, D), F32),
            pltpu.VMEM((nb, R, D // R, D), F32),
            pltpu.VMEM((nb, D // R, D), F32),
            pltpu.VMEM((C, nb, sub, D), F32),
            pltpu.VMEM((C, nb, sub, D), F32),
            pltpu.VMEM((nb, sub, D), F32),
            pltpu.VMEM((C, sub, D), F32),
            dma((3,)),
            dma((2, N, K)), dma((N, K)),
            dma((C + 1,)), dma((C + 1,)),
            dma((T,)), dma((T,)),
            dma((K,)), dma((K,)),
            dma((K, C)), dma((K, C)),
            dma((4,)), dma((4,)),
            dma((4, C)), dma((4, C)),
            dma((nb,)), dma((C,)),
            dma((4,)), dma((4,)),
        ],
        compiler_params=pltpu.CompilerParams(
            collective_id=0, has_side_effects=True, vmem_limit_bytes=60 * 1024 * 1024
        ),
    )(where, grad_out, relu_mask, saved_agg, weight, tiles)

    def finish(wg_in, a, b, wg_out, ig_out):
        wg_out[...] = wg_in[...]
        ig_out[...] = a[...] + b[...]

    return pl.pallas_call(
        finish,
        out_shape=(jax.ShapeDtypeStruct((blk, D), F32), jax.ShapeDtypeStruct((IN, D), F32)),
        in_specs=[vmem, vmem, vmem],
        out_specs=(vmem, vmem),
    )(wg, ig, igr)


def per_device(R, C, N, grad_out, *rest):
    H, D = grad_out.shape
    line = R == 2 and C == 4 and N == 4 and D % (8 * R * C) == 0
    line = line and H % TILE == 0 and H // TILE == 4
    return (on_line if line else general)(R, C, N, grad_out, *rest)


def solution(mesh):
    in_specs = (
        P(("row", "col"), "ch"),
        P(("row", "col"), "ch"),
        P(("row", "col"), "ch"),
        P("ch", None),
        P("row", "col", None, None, None),
        P("row", "col", None),
        P("row", "col"),
    )
    out_specs = (P(("row", "col"), "ch"), P("col", "ch"))
    R, C, N = mesh.shape["row"], mesh.shape["col"], mesh.shape["ch"]
    return jax.shard_map(
        functools.partial(per_device, R, C, N), mesh=mesh, in_specs=in_specs, out_specs=out_specs, check_vma=False
    )
```

```python
import functools

import jax
import jax.numpy as jnp
from jax import lax
from jax.experimental import pallas as pl
from jax.experimental.pallas import tpu as pltpu
from jax.sharding import PartitionSpec as P

TILE = 128
MESH = pl.DeviceIdType.MESH
F32 = jnp.float32
BF16 = jnp.bfloat16


def split(x):
    hi = x.astype(BF16)
    return hi, (x - hi.astype(F32)).astype(BF16)


def nn(a, b):
    return lax.dot_general(a, b, (((1,), (0,)), ((), ())), preferred_element_type=F32)


def nt(a, b):
    return lax.dot_general(a, b, (((1,), (1,)), ((), ())), preferred_element_type=F32)


def kernel(
    R, C, N, K,
    slot_ref, g_ref, mask_ref, sa_hbm, w_hbm, tiles_hbm,
    wg_ref, ig_ref, igr,
    M, G, tiles, at_hi, at_lo, w_f, w_hi, w_lo, sa, g_hi, g_lo,
    wgp, wgr, wgs, wgc, wgo,
    local_sem, zsend, zrecv, csend, crecv, wrsend, wrrecv, wcsend, wcrecv, wfsend, wfrecv,
    irsend, irrecv, iasend, iarecv,
):
    r, c, z = lax.axis_index("row"), lax.axis_index("col"), lax.axis_index("ch")
    HB, D = M.shape[2], M.shape[3]
    RC = R * C
    per = RC // N
    blk = wgp.shape[1]
    slots = tiles.shape[0]
    acc = ig_ref
    IN = acc.shape[0]
    in_tiles = IN // TILE
    tpb = HB // TILE
    piece = IN // R

    cp_w = pltpu.make_async_copy(w_hbm, w_f, local_sem.at[0])
    cp_sa = pltpu.make_async_copy(sa_hbm, sa, local_sem.at[1])
    cp_t = pltpu.make_async_copy(tiles_hbm, tiles, local_sem.at[2])
    cp_w.start()
    cp_sa.start()
    cp_t.start()

    def dev(r_, c_, z_):
        return {"row": r_, "col": c_, "ch": z_}

    q = r * C + c
    d_idx = z * per + q // N
    d_r, d_c, d_z = d_idx // C, d_idx % C, q % N
    s_q = (q % per) * N + z
    s_r, s_c, s_z = s_q // C, s_q % C, q // per
    away = jnp.logical_not((d_r == r) & (d_c == c) & (d_z == z))

    barrier = pltpu.get_barrier_semaphore()

    def hello(r_, c_, z_):
        pl.semaphore_signal(barrier, inc=1, device_id=dev(r_, c_, z_), device_id_type=MESH)

    for j in range(1, R):
        hello((r + j) % R, c, z)
    for j in range(1, C):
        hello(r, (c + j) % C, z)

    @pl.when(z > 0)
    def _():
        hello(r, c, z - 1)

    @pl.when(z < N - 1)
    def _():
        hello(r, c, z + 1)

    @pl.when(away)
    def _():
        hello(d_r, d_c, d_z)
        hello(s_r, s_c, s_z)

    def own(k):
        rows = pl.ds(pl.multiple_of(k * HB, HB), HB)
        M[z, k] = g_ref[rows, :] * mask_ref[rows, :].astype(F32)

    own(0)
    own(1)
    one_if = lambda cond: jnp.where(cond, 1, 0)
    greeted = R - 1 + C - 1 + one_if(z > 0) + one_if(z < N - 1) + 2 * one_if(away)
    pl.semaphore_wait(barrier, greeted)

    def zcopy(origin, k, step):
        way = 0 if step < 0 else 1
        return pltpu.make_async_remote_copy(
            src_ref=M.at[origin, k], dst_ref=M.at[origin, k],
            send_sem=zsend.at[way, origin, k], recv_sem=zrecv.at[origin, k],
            device_id=dev(r, c, z + step), device_id_type=MESH,
        )

    def own_send(k):
        @pl.when(z > 0)
        def _():
            zcopy(z, k, -1).start()

        @pl.when(z < N - 1)
        def _():
            zcopy(z, k, 1).start()

    own_send(0)
    own_send(1)
    acc[...] = jnp.zeros_like(acc)
    wgp[...] = jnp.zeros_like(wgp)
    cp_w.wait()
    for n in range(N):
        cols = slice(n * D, (n + 1) * D)
        w_hi[:, cols], w_lo[:, cols] = split(w_f[:, cols])
    cp_sa.wait()
    cp_t.wait()

    def prep(k, cc):
        for t in range(tpb):
            def one(i, _):
                p = ((cc * K + k) * tpb + t) * in_tiles + i
                v = slot_ref[p]
                tile = tiles[lax.rem(v, slots)]
                tile = jnp.where(v < slots, tile, jnp.zeros_like(tile))
                hi, lo = split(tile.T)
                rows = pl.ds(pl.multiple_of(i * TILE, TILE), TILE)
                cols = slice(cc * HB + t * TILE, cc * HB + (t + 1) * TILE)
                at_hi[k, rows, cols] = hi
                at_lo[k, rows, cols] = lo
                return 0

            lax.fori_loop(0, in_tiles, one, 0, unroll=2)

    def ccopy(k, j):
        return pltpu.make_async_remote_copy(
            src_ref=G.at[k, c], dst_ref=G.at[k, c],
            send_sem=csend.at[k, j], recv_sem=crecv.at[k, j],
            device_id=dev(r, (c + j) % C, z), device_id_type=MESH,
        )

    def cwait(k, j):
        o = (c + C - j) % C
        return pltpu.make_async_remote_copy(
            src_ref=G.at[k, o], dst_ref=G.at[k, o],
            send_sem=csend.at[k, j], recv_sem=crecv.at[k, j],
            device_id=dev(r, (c + j) % C, z), device_id_type=MESH,
        )

    def consume(k):
        for j in range(1, C):
            cwait(k, j).wait_recv()
        for n in range(C):
            rows = slice(n * HB, (n + 1) * HB)
            g_hi[rows, :], g_lo[rows, :] = split(G[k, n])

        def part(i, _):
            rows = pl.ds(pl.multiple_of(i * 256, 256), 256)
            a = at_hi[k, rows, :]
            acc[rows, :] += nn(a, g_hi[...]) + nn(a, g_lo[...]) + nn(at_lo[k, rows, :], g_hi[...])
            return 0

        lax.fori_loop(0, IN // 256, part, 0)

    def wrcopy(j):
        t = (r + j) % R
        return pltpu.make_async_remote_copy(
            src_ref=wgp.at[pl.ds(t * C, C)], dst_ref=wgr.at[j],
            send_sem=wrsend.at[j], recv_sem=wrrecv.at[j],
            device_id=dev(t, c, z), device_id_type=MESH,
        )

    groups = [[] for _ in range(N - 1)]
    for cc in range(C):
        groups[cc * max(N - 2, 1) // C].append(cc)

    def body(k, _):
        for d in range(1, N):
            @pl.when(z >= d)
            def _():
                zcopy(z - d, k, 1).wait_recv()

                @pl.when(z < N - 1)
                def _():
                    zcopy(z - d, k, 1).start()

            @pl.when(z + d < N)
            def _():
                zcopy(z + d, k, -1).wait_recv()

                @pl.when(z > 0)
                def _():
                    zcopy(z + d, k, -1).start()

            if d == 1:
                @pl.when(k + 2 < K)
                def _():
                    own(k + 2)
                    own_send(k + 2)

            for cc in groups[d - 1]:
                prep(k, cc)

        agg = jnp.zeros((HB, D), F32)
        for n in range(N):
            cols = slice(n * D, (n + 1) * D)
            hi, lo = split(M[n, k])
            agg += nt(hi, w_hi[:, cols]) + nt(lo, w_hi[:, cols]) + nt(hi, w_lo[:, cols])
        G[k, c] = agg
        for j in range(1, C):
            ccopy(k, j).start()

        rows = pl.ds(pl.multiple_of(k * HB, HB), HB)
        s_hi, s_lo = split(sa[rows, :].T)
        for n in range(N):
            hi, lo = split(M[n, k])
            res = nn(s_hi, hi) + nn(s_hi, lo) + nn(s_lo, hi)
            for h in range(per):
                wgp[h * N + n] += res[h * blk:(h + 1) * blk, :]

        @pl.when(k == K - 1)
        def _():
            for j in range(1, R):
                wrcopy(j).start()

        @pl.when(k > 0)
        def _():
            consume(k - 1)

        return 0

    lax.fori_loop(0, K, body, 0)

    def wccopy(j):
        t = (c + j) % C
        return pltpu.make_async_remote_copy(
            src_ref=wgs.at[t], dst_ref=wgc.at[j],
            send_sem=wcsend.at[j], recv_sem=wcrecv.at[j],
            device_id=dev(r, t, z), device_id_type=MESH,
        )

    wfcopy = pltpu.make_async_remote_copy(
        src_ref=wgo, dst_ref=wg_ref, send_sem=wfsend, recv_sem=wfrecv,
        device_id=dev(d_r, d_c, d_z), device_id_type=MESH,
    )

    def ircopy(j):
        t = (r + j) % R
        whole = R == 2
        rows = pl.ds(0, IN) if whole else pl.ds(pl.multiple_of(t * piece, piece), piece)
        return pltpu.make_async_remote_copy(
            src_ref=acc.at[rows], dst_ref=igr if whole else igr.at[j],
            send_sem=irsend.at[j], recv_sem=irrecv.at[j],
            device_id=dev(t, c, z), device_id_type=MESH,
        )

    mine = pl.ds(pl.multiple_of(r * piece, piece), piece)

    def iacopy(j):
        return pltpu.make_async_remote_copy(
            src_ref=ig_ref.at[mine], dst_ref=ig_ref.at[mine],
            send_sem=iasend.at[j], recv_sem=iarecv.at[j],
            device_id=dev((r + j) % R, c, z), device_id_type=MESH,
        )

    def iawait(j):
        theirs = pl.ds(pl.multiple_of(((r + R - j) % R) * piece, piece), piece)
        return pltpu.make_async_remote_copy(
            src_ref=ig_ref.at[theirs], dst_ref=ig_ref.at[theirs],
            send_sem=iasend.at[j], recv_sem=iarecv.at[j],
            device_id=dev((r + j) % R, c, z), device_id_type=MESH,
        )

    for j in range(1, R):
        wrcopy(j).wait_recv()
    total = wgp[pl.ds(r * C, C)]
    for j in range(1, R):
        total += wgr[j]
    wgs[...] = total
    for j in range(1, C):
        wccopy(j).start()

    consume(K - 1)
    for j in range(1, R):
        ircopy(j).start()
    for j in range(1, C):
        wccopy(j).wait_recv()
    wpart = wgs[c]
    for j in range(1, C):
        wpart += wgc[j]

    @pl.when(away)
    def _():
        wgo[...] = wpart
        wfcopy.start()
        wfcopy.wait()

    @pl.when(jnp.logical_not(away))
    def _():
        wg_ref[...] = wpart

    for j in range(1, R):
        ircopy(j).wait_recv()
    if R > 2:
        summed = acc[mine, :]
        for j in range(1, R):
            summed += igr[j]
        ig_ref[mine, :] = summed
        for j in range(1, R):
            iacopy(j).start()
        for j in range(1, R):
            iawait(j).wait_recv()

    for j in range(1, R):
        wrcopy(j).wait_send()
        ircopy(j).wait_send()
        if R > 2:
            iacopy(j).wait_send()
    for j in range(1, C):
        wccopy(j).wait_send()

    def drain(k, _):
        for j in range(1, C):
            ccopy(k, j).wait_send()
        for n in range(N):
            @pl.when((z > 0) & (z <= n))
            def _():
                zcopy(n, k, -1).wait_send()

            @pl.when((z < N - 1) & (z >= n))
            def _():
                zcopy(n, k, 1).wait_send()

        return 0

    lax.fori_loop(0, K, drain, 0)


def general(R, C, N, grad_out, relu_mask, saved_agg, weight, tile_vals, tile_pos, tile_count):
    H, D = grad_out.shape
    F = weight.shape[1]
    tiles = tile_vals[0, 0]
    slots = tiles.shape[0]
    out_rows = C * H
    IN = slots * TILE * TILE // out_rows
    HB = TILE
    K = H // HB
    blk = F // (R * C)
    s = jnp.arange(slots, dtype=jnp.int32)
    code = jnp.where(s < tile_count[0, 0], s, s + slots)
    where = jnp.sum(jnp.where(tile_pos[0, 0][None, :] == s[:, None], code[None, :], 0), axis=1).astype(jnp.int32)
    vmem = pl.BlockSpec(memory_space=pltpu.VMEM)
    hbm = pl.BlockSpec(memory_space=pl.ANY)
    dma = pltpu.SemaphoreType.DMA
    igr_shape = (IN, D) if R == 2 else (R, IN // R, D)
    wg, ig, igr = pl.pallas_call(
        functools.partial(kernel, R, C, N, K),
        out_shape=(
            jax.ShapeDtypeStruct((blk, D), F32),
            jax.ShapeDtypeStruct((IN, D), F32),
            jax.ShapeDtypeStruct(igr_shape, F32),
        ),
        in_specs=[pl.BlockSpec(memory_space=pltpu.SMEM), vmem, vmem, hbm, hbm, hbm],
        out_specs=(vmem, vmem, vmem),
        scratch_shapes=[
            pltpu.VMEM((N, K, HB, D), F32),
            pltpu.VMEM((K, C, HB, D), F32),
            pltpu.VMEM((slots, TILE, TILE), F32),
            pltpu.VMEM((K, IN, C * HB), BF16),
            pltpu.VMEM((K, IN, C * HB), BF16),
            pltpu.VMEM((D, F), F32),
            pltpu.VMEM((D, F), BF16),
            pltpu.VMEM((D, F), BF16),
            pltpu.VMEM((H, D), F32),
            pltpu.VMEM((C * HB, D), BF16),
            pltpu.VMEM((C * HB, D), BF16),
            pltpu.VMEM((R * C, blk, D), F32),
            pltpu.VMEM((R, C, blk, D), F32),
            pltpu.VMEM((C, blk, D), F32),
            pltpu.VMEM((C, blk, D), F32),
            pltpu.VMEM((blk, D), F32),
            dma((3,)),
            dma((2, N, K)), dma((N, K)),
            dma((K, C)), dma((K, C)),
            dma((R,)), dma((R,)),
            dma((C,)), dma((C,)),
            dma, dma,
            dma((R,)), dma((R,)),
            dma((R,)), dma((R,)),
        ],
        compiler_params=pltpu.CompilerParams(
            collective_id=0, has_side_effects=True, vmem_limit_bytes=60 * 1024 * 1024
        ),
    )(where, grad_out, relu_mask, saved_agg, weight, tiles)

    def finish(wg_in, a, b, wg_out, ig_out):
        wg_out[...] = wg_in[...]
        ig_out[...] = a[...] + b[...] if R == 2 else a[...]

    return pl.pallas_call(
        finish,
        out_shape=(jax.ShapeDtypeStruct((blk, D), F32), jax.ShapeDtypeStruct((IN, D), F32)),
        in_specs=[vmem, vmem, vmem if R == 2 else hbm],
        out_specs=(vmem, vmem),
    )(wg, ig, igr)


def cat_nn(a, b):
    return nn(jnp.concatenate([a[0], a[0], a[1]], axis=1), jnp.concatenate([b[0], b[1], b[0]], axis=0))


def line_kernel(
    R, C, N, chunks, raws, relays_end, relays_inner,
    count_ref, pos_ref, g_hbm, mask_hbm, sa_hbm, w_hbm, tiles_hbm,
    wg_ref, ig_ref, igr,
    slot_vec, slot_ref, mask, M, G, tiles, at_hi, at_lo, w_f, w_hi, w_lo, sa,
    we_f, we_hi, we_lo, sae, part, wgp, wgr, wgs, wgc, wgo, wgd,
    local_sem, zsend, zrecv, wesend, werecv, sasend, sarecv, psend, precv,
    csend, crecv, rsend, rrecv, tsend, trecv, dsend, drecv, irsend, irrecv,
):
    r, c, z = lax.axis_index("row"), lax.axis_index("col"), lax.axis_index("ch")
    H, D = M.shape[1], M.shape[2]
    T, K = H // TILE, len(chunks)
    per = R * C // N
    sub = wgo.shape[1]
    slots = tiles.shape[0]
    IN = ig_ref.shape[0]
    in_tiles = IN // TILE
    wide = (N - 1) * D
    nb = 2 * N - 1

    low = z < N // 2
    end = (z == 0) | (z == N - 1)
    inner = jnp.logical_not(end)
    z_in = jnp.where(low, z + 1, z - 1)
    z_out = jnp.where(low, z - 1, z + 1)
    e0 = jnp.where(low, 0, N - 1)
    e1 = jnp.where(low, 1, N - 2)
    o1 = jnp.where(low, 2, N - 3)
    o0 = jnp.where(low, N - 1, 0)
    p = r * C + c

    cp_g = pltpu.make_async_copy(g_hbm, M.at[z], local_sem.at[3])
    cp_m = pltpu.make_async_copy(mask_hbm, mask, local_sem.at[4])
    cp_s = pltpu.make_async_copy(slot_vec, slot_ref, local_sem.at[5])
    cp_w = pltpu.make_async_copy(w_hbm, w_f, local_sem.at[0])
    cp_sa = pltpu.make_async_copy(sa_hbm, sa, local_sem.at[1])
    cp_t = pltpu.make_async_copy(tiles_hbm, tiles, local_sem.at[2])

    def dev(r_, c_, z_):
        return {"row": r_, "col": c_, "ch": z_}

    one_if = lambda cond: jnp.where(cond, 1, 0)
    same = lambda r_, c_, z_: (r_ == r) & (c_ == c) & (z_ == z)
    far = jnp.logical_not

    own_q = per * z + r
    end_q = per * e0 + r
    block_n = [z, e0, o1, o0, e1, o1, o0]
    block_q = [own_q] * N + [end_q] * (N - 1)

    def goal(b):
        return block_q[b] // C, block_q[b] % C, block_n[b]

    my_a, my_r = p // per, p % per
    my_z = jnp.where(my_a == z, z, jnp.where(my_a == 0, 1, jnp.where(my_a == N - 1, N - 2, my_a)))

    barrier = pltpu.get_barrier_semaphore()

    def hello(r_, c_, z_):
        pl.semaphore_signal(barrier, inc=1, device_id=dev(r_, c_, z_), device_id_type=MESH)

    hello(1 - r, c, z)
    for j in range(1, C):
        hello(r, (c + j) % C, z)
    hello(r, c, z_in)
    pl.when(inner)(lambda: hello(r, c, z_out))
    for j in range(C):
        pl.when(far(same(my_r, j, my_z)))(lambda: hello(my_r, j, my_z))
    greeted = R - 1 + C - 1 + 1 + one_if(inner) + one_if(far(same(*goal(0))))
    for b in range(1, nb):
        greeted += one_if(inner & far(same(*goal(b))))

    for copy in (cp_g, cp_m, cp_w, cp_sa, cp_t):
        copy.start()

    def rows_of(k):
        return pl.ds(*chunks[k])

    square = (slots, slots)
    slot, place = lax.broadcasted_iota(jnp.int32, square, 0), lax.broadcasted_iota(jnp.int32, square, 1)
    code = jnp.where(slot < count_ref[0, 0], slot, slot + slots)
    hit = jnp.broadcast_to(pos_ref[...], square).T == place
    slot_vec[...] = jnp.sum(jnp.where(hit, code, 0), axis=0, keepdims=True)
    cp_s.start()
    cp_g.wait()
    cp_m.wait()
    for k in range(K):
        rows = rows_of(k)
        M[z, rows, :] = M[z, rows, :] * mask[rows, :].astype(F32)
    pl.semaphore_wait(barrier, greeted)

    def program(at_end):
        relays = relays_end if at_end else relays_inner
        pending = []

        def send(src, dst, ss, rs, to, cond=None):
            def make():
                return pltpu.make_async_remote_copy(
                    src_ref=src, dst_ref=dst, send_sem=ss, recv_sem=rs, device_id=to, device_id_type=MESH
                )

            pending.append((cond, make))
            if cond is None:
                make().start()
            else:
                pl.when(cond)(lambda: make().start())

        def recv(dst, ss, rs):
            pltpu.make_async_remote_copy(
                src_ref=dst, dst_ref=dst, send_sem=ss, recv_sem=rs, device_id=dev(1 - r, c, z), device_id_type=MESH
            ).wait_recv()

        def zpass(o, k):
            blk = M.at[o, rows_of(k)]
            send(blk, blk, zsend.at[0, o, k], zrecv.at[o, k], dev(r, c, z_in))

        def zout(o, k):
            if k in raws:
                blk = M.at[o, rows_of(k)]
                send(blk, blk, zsend.at[1, o, k], zrecv.at[o, k], dev(r, c, z_out))

        def zwait(o, k):
            recv(M.at[o, rows_of(k)], zsend.at[0, o, k], zrecv.at[o, k])

        def onward(k):
            zwait(e0, k)
            zpass(e0, k)

        def arrive(o, k):
            zwait(o, k)
            zout(o, k)

        def weights_pass():
            cols = pl.ds(pl.multiple_of(jnp.where(low, D, 0), D), wide)
            rows = pl.ds(pl.multiple_of(p * sub, sub), sub)
            send(w_f.at[rows, cols], we_f.at[p], wesend.at[0], werecv.at[0], dev(r, c, z_in))

        def sa_pass(t):
            send(sa.at[pl.ds(t * TILE, TILE)], sae.at[t], sasend.at[t], sarecv.at[t], dev(r, c, z_in))

        def outer(s, m):
            return cat_nn(s, split(m))

        def wadd(b, value, first):
            value = value.reshape(R, D // R, D)
            if first:
                wgp[b] = value
            else:
                wgp[b] += value

        def sa_own(t):
            return split(sa[t * TILE:(t + 1) * TILE, :].T)

        def tile_rows(o, t):
            return M[o, t * TILE:(t + 1) * TILE, :]

        def wgrad_own():
            for t in range(T):
                wadd(0, outer(sa_own(t), tile_rows(z, t)), t == 0)

        def wgrad_mine(t, bs):
            s = sa_own(t)
            for b in bs:
                wadd(b, outer(s, tile_rows(block_n[b], t)), t == 0)

        def wgrad_ends(t):
            recv(sae.at[t], sasend.at[t], sarecv.at[t])
            s = split(sae[t].T)
            for b in range(N, nb):
                wadd(b, outer(s, tile_rows(block_n[b], t)), t == 0)

        groups = ((0, 1), (1, 2), (2, N), (N, nb))

        def red_row(n):
            lo, hi = groups[n]
            bs = pl.ds(lo, hi - lo)
            send(wgp.at[bs, 1 - r], wgr.at[bs], rsend.at[n], rrecv.at[n], dev(1 - r, c, z))

        def red_col(n):
            lo, hi = groups[n]
            bs = pl.ds(lo, hi - lo)
            recv(wgr.at[bs], rsend.at[n], rrecv.at[n])
            for b in range(lo, hi):
                total = wgp[b, r] + wgr[b]
                for t in range(C):
                    wgs[t, b] = total[t * sub:(t + 1) * sub]
            for j in range(1, C):
                t = (c + j) % C
                send(wgs.at[t, bs], wgc.at[j, bs], tsend.at[n, j], trecv.at[n, j], dev(r, t, z))

        def red_out(n):
            lo, hi = groups[n]
            bs = pl.ds(lo, hi - lo)
            for j in range(1, C):
                recv(wgc.at[j, bs], tsend.at[n, j], trecv.at[n, j])
            for b in range(lo, hi):
                total = wgs[c, b]
                for j in range(1, C):
                    total += wgc[j, b]
                wgo[b] = total
                send(wgo.at[b], wgd.at[c], dsend.at[b], drecv.at[c], dev(*goal(b)), far(same(*goal(b))))

                @pl.when(same(*goal(b)))
                def _():
                    wgd[c] = wgo[b]

        def prep(t):
            inside = [k for k, (at, n) in enumerate(chunks) if at // TILE == t]
            HB = chunks[inside[0]][1]
            two = TILE // HB

            def one(i, _):
                rows = pl.ds(pl.multiple_of(i * TILE, TILE), TILE)
                for m in range(C // two):
                    got = []
                    for j in range(two):
                        v = slot_ref[0, ((two * m + j) * T + t) * in_tiles + i]
                        tile = tiles[lax.rem(v, slots)]
                        got.append(jnp.where(v < slots, tile, jnp.zeros_like(tile)))
                    for h, k in enumerate(inside):
                        mix = jnp.concatenate([x[h * HB:(h + 1) * HB] for x in got], axis=0)
                        hi, lo = split(mix.T)
                        base = C * chunks[k][0] + m * TILE
                        at_hi[rows, base:base + TILE] = hi
                        at_lo[rows, base:base + TILE] = lo
                return 0

            lax.fori_loop(0, in_tiles, one, 0)

        c_x = c + 1 - 2 * (c % 2)
        c_y = (c + 2) % C
        c_d = (c_x + 2) % C

        def gather_g(k):
            blk = G.at[c, rows_of(k)]
            send(blk, blk, csend.at[k, 0], crecv.at[k, 0], dev(r, c_x, z))
            send(blk, blk, csend.at[k, 1], crecv.at[k, 1], dev(r, c_y, z))
            if k not in relays:
                send(blk, blk, csend.at[k, 2], crecv.at[k, 2], dev(r, c_d, z))

        def relay(k):
            at, n = chunks[k]
            first, second = pl.ds(at, n // 2), pl.ds(at + n // 2, n // 2)
            recv(G.at[c_x, rows_of(k)], csend.at[k, 0], crecv.at[k, 0])
            blk = G.at[c_x, first]
            send(blk, blk, csend.at[k, 2], crecv.at[k, 2], dev(r, c_y, z))
            recv(G.at[c_y, rows_of(k)], csend.at[k, 1], crecv.at[k, 1])
            blk = G.at[c_y, second]
            send(blk, blk, csend.at[k, 3], crecv.at[k, 3], dev(r, c_x, z))

        def consume(k, last=False):
            at, n = chunks[k]
            if k in relays:
                recv(G.at[c_d, pl.ds(at, n // 2)], csend.at[k, 2], crecv.at[k, 2])
                recv(G.at[c_d, pl.ds(at + n // 2, n // 2)], csend.at[k, 3], crecv.at[k, 3])
            else:
                for j, o in enumerate((c_x, c_y, c_d)):
                    recv(G.at[o, rows_of(k)], csend.at[k, j], crecv.at[k, j])
            cols = slice(C * at, C * (at + n))
            g = split(G[:, at:at + n, :].reshape(C * n, D))
            step = IN // 4

            def block(rows):
                add = cat_nn((at_hi[rows, cols], at_lo[rows, cols]), g)
                if k == 0:
                    ig_ref[rows, :] = add
                else:
                    ig_ref[rows, :] += add

            for i in range(4):
                rows = pl.ds(i * step, step)
                block(rows)
                if last:
                    send(ig_ref.at[rows], igr.at[rows], irsend.at[i], irrecv.at[i], dev(1 - r, c, z))

        def own_cols(o):
            return pl.ds(pl.multiple_of(o * D, D), D)

        def end_cols(o):
            return pl.ds(pl.multiple_of((o - one_if(low)) * D, D), D)

        def times_w(os, rows, hi_w, lo_w, col_of):
            left, right = [], []
            for o in os:
                hi, lo = split(M[o, rows, :])
                cols = col_of(o)
                wh = hi_w[:, cols]
                left += [hi, lo, hi]
                right += [wh, wh, lo_w[:, cols]]
            return nt(jnp.concatenate(left, axis=1), jnp.concatenate(right, axis=1))

        whole = pl.ds(0, H)

        def partial_own():
            part[...] = times_w([e1], whole, we_hi, we_lo, end_cols)

        def partial(k):
            rows = rows_of(k)
            part[rows, :] += times_w([o1, o0], rows, we_hi, we_lo, end_cols)
            pc = part.at[rows]
            send(pc, pc, psend.at[k], precv.at[k], dev(r, c, z_out))

        def agg_own():
            G[c] = times_w([z], whole, w_hi, w_lo, own_cols)

        def agg_inner(k):
            rows = rows_of(k)
            G[c, rows, :] += times_w([e0, o1, o0], rows, w_hi, w_lo, own_cols)
            gather_g(k)

        def agg_end(k):
            rows = rows_of(k)
            if k in raws:
                for o in (e1, o1, o0):
                    zwait(o, k)
                G[c, rows, :] += times_w([e1, o1, o0], rows, w_hi, w_lo, own_cols)
            else:
                recv(part.at[rows], psend.at[k], precv.at[k])
                G[c, rows, :] += part[rows, :]
            gather_g(k)

        def end_weights(stage):
            if stage == 0:
                recv(we_f.at[p], wesend.at[0], werecv.at[0])
                for j in range(1, C):
                    send(we_f.at[p], we_f.at[p], wesend.at[j], werecv.at[j], dev(r, (c + j) % C, z))
            elif stage == 1:
                for j in range(1, C):
                    recv(we_f.at[r * C + (c + C - j) % C], wesend.at[j], werecv.at[j])
                mine = pl.ds(r * C, C)
                send(we_f.at[mine], we_f.at[mine], wesend.at[C], werecv.at[C], dev(1 - r, c, z))
            else:
                recv(we_f.at[pl.ds((1 - r) * C, C)], wesend.at[C], werecv.at[C])
                for i in range(R * C):
                    rows = slice(i * sub, (i + 1) * sub)
                    we_hi[rows, :], we_lo[rows, :] = split(we_f[i])

        def split_w():
            for n in range(N):
                cols = slice(n * D, (n + 1) * D)
                w_hi[:, cols], w_lo[:, cols] = split(w_f[:, cols])

        def finish_all():
            for j in range(C):
                pl.when(far(same(my_r, j, my_z)))(lambda: recv(wgd.at[j], dsend.at[0], drecv.at[j]))
                wg_ref[j * sub:(j + 1) * sub, :] = wgd[j]
            for i in range(4):
                rows = pl.ds(i * (IN // 4), IN // 4)
                recv(igr.at[rows], irsend.at[i], irrecv.at[i])
            for cond, make in pending:
                if cond is None:
                    make().wait_send()
                else:
                    pl.when(cond)(lambda: make().wait_send())

        if at_end:
            zpass(z, 0)
            cp_w.wait()
            weights_pass()
            zpass(z, 1)
            zpass(z, 2)
            cp_sa.wait()
            sa_pass(0)
            zpass(z, 3)
            zpass(z, 4)
            zpass(z, 5)
            sa_pass(1)
            sa_pass(2)
            sa_pass(3)
            split_w()
            agg_own()
            cp_t.wait()
            cp_s.wait()
            prep(0)
            wgrad_own()
            red_row(0)
            prep(1)
            red_col(0)
            agg_end(0)
            agg_end(1)
            prep(2)
            prep(3)
            red_out(0)
            consume(0)
            consume(1)
            agg_end(2)
            agg_end(3)
            relay(2)
            agg_end(4)
            agg_end(5)
            relay(3)
            consume(2)
            consume(4)
            consume(5)
            consume(3, True)
        else:
            zpass(z, 0)
            zout(z, 0)
            zpass(z, 1)
            zout(z, 1)
            cp_w.wait()
            split_w()
            cp_t.wait()
            cp_s.wait()
            prep(0)
            agg_own()
            onward(0)
            zpass(z, 2)
            end_weights(0)
            prep(1)
            onward(1)
            zpass(z, 3)
            arrive(o1, 0)
            arrive(o0, 0)
            agg_inner(0)
            onward(2)
            zpass(z, 4)
            zpass(z, 5)
            cp_sa.wait()
            wgrad_own()
            red_row(0)
            arrive(o1, 1)
            arrive(o0, 1)
            agg_inner(1)
            relay(0)
            prep(2)
            end_weights(1)
            red_col(0)
            onward(3)
            relay(1)
            end_weights(2)
            partial_own()
            arrive(o1, 2)
            arrive(o0, 2)
            partial(2)
            agg_inner(2)
            onward(4)
            onward(5)
            consume(0)
            prep(3)
            consume(1)
            red_out(0)
            wgrad_ends(0)
            arrive(o1, 3)
            arrive(o0, 3)
            partial(3)
            agg_inner(3)
            wgrad_mine(0, (1, 2, 3))
            arrive(o1, 4)
            arrive(o0, 4)
            partial(4)
            agg_inner(4)
            relay(2)
            wgrad_mine(1, (1,))
            wgrad_mine(2, (1,))
            wgrad_mine(3, (1,))
            red_row(1)
            arrive(o1, 5)
            arrive(o0, 5)
            partial(5)
            agg_inner(5)
            wgrad_ends(1)
            wgrad_ends(2)
            wgrad_ends(3)
            red_row(3)
            wgrad_mine(1, (2, 3))
            wgrad_mine(2, (2, 3))
            wgrad_mine(3, (2, 3))
            red_row(2)
            red_col(3)
            red_col(2)
            red_col(1)
            relay(3)
            relay(4)
            relay(5)
            consume(2)
            red_out(3)
            consume(3)
            consume(4)
            red_out(2)
            red_out(1)
            consume(5, True)
        finish_all()

    pl.when(end)(lambda: program(True))
    pl.when(inner)(lambda: program(False))


def on_line(R, C, N, grad_out, relu_mask, saved_agg, weight, tile_vals, tile_pos, tile_count):
    H, D = grad_out.shape
    F = weight.shape[1]
    tiles = tile_vals[0, 0]
    slots = tiles.shape[0]
    IN = slots * TILE * TILE // (C * H)
    T = H // TILE
    half = TILE // 2
    fine = lambda at: [(at, half), (at + half, half)]
    chunks = fine(0) + [(t * TILE, TILE) for t in range(1, T - 1)] + fine(H - TILE)
    K = len(chunks)
    blk = F // (R * C)
    sub = D // (R * C)
    nb = 2 * N - 1
    vmem = pl.BlockSpec(memory_space=pltpu.VMEM)
    hbm = pl.BlockSpec(memory_space=pl.ANY)
    dma = pltpu.SemaphoreType.DMA
    wg, ig, igr = pl.pallas_call(
        functools.partial(line_kernel, R, C, N, chunks, (0, 1), (2, 3), (0, 1, 2, 3, 4, 5)),
        out_shape=(
            jax.ShapeDtypeStruct((blk, D), F32),
            jax.ShapeDtypeStruct((IN, D), F32),
            jax.ShapeDtypeStruct((IN, D), F32),
        ),
        in_specs=[pl.BlockSpec(memory_space=pltpu.SMEM), vmem, hbm, hbm, hbm, hbm, hbm],
        out_specs=(vmem, vmem, vmem),
        scratch_shapes=[
            pltpu.VMEM((1, slots), jnp.int32),
            pltpu.SMEM((1, slots), jnp.int32),
            pltpu.VMEM((H, D), jnp.int32),
            pltpu.VMEM((N, H, D), F32),
            pltpu.VMEM((C, H, D), F32),
            pltpu.VMEM((slots, TILE, TILE), F32),
            pltpu.VMEM((IN, C * H), BF16),
            pltpu.VMEM((IN, C * H), BF16),
            pltpu.VMEM((D, F), F32),
            pltpu.VMEM((D, F), BF16),
            pltpu.VMEM((D, F), BF16),
            pltpu.VMEM((H, D), F32),
            pltpu.VMEM((R * C, sub, (N - 1) * D), F32),
            pltpu.VMEM((D, (N - 1) * D), BF16),
            pltpu.VMEM((D, (N - 1) * D), BF16),
            pltpu.VMEM((T, TILE, D), F32),
            pltpu.VMEM((H, D), F32),
            pltpu.VMEM((nb, R, D // R, D), F32),
            pltpu.VMEM((nb, D // R, D), F32),
            pltpu.VMEM((C, nb, sub, D), F32),
            pltpu.VMEM((C, nb, sub, D), F32),
            pltpu.VMEM((nb, sub, D), F32),
            pltpu.VMEM((C, sub, D), F32),
            dma((6,)),
            dma((2, N, K)), dma((N, K)),
            dma((C + 1,)), dma((C + 1,)),
            dma((T,)), dma((T,)),
            dma((K,)), dma((K,)),
            dma((K, C)), dma((K, C)),
            dma((4,)), dma((4,)),
            dma((4, C)), dma((4, C)),
            dma((nb,)), dma((C,)),
            dma((4,)), dma((4,)),
        ],
        compiler_params=pltpu.CompilerParams(
            collective_id=0, has_side_effects=True, vmem_limit_bytes=60 * 1024 * 1024
        ),
    )(tile_count, tile_pos[0], grad_out, relu_mask, saved_agg, weight, tiles)

    def finish(wg_in, a, b, wg_out, ig_out):
        wg_out[...] = wg_in[...]
        ig_out[...] = a[...] + b[...]

    return pl.pallas_call(
        finish,
        out_shape=(jax.ShapeDtypeStruct((blk, D), F32), jax.ShapeDtypeStruct((IN, D), F32)),
        in_specs=[vmem, vmem, vmem],
        out_specs=(vmem, vmem),
    )(wg, ig, igr)


def per_device(R, C, N, grad_out, *rest):
    H, D = grad_out.shape
    line = R == 2 and C == 4 and N == 4 and D % (8 * R * C) == 0
    line = line and H % TILE == 0 and H // TILE == 4 and rest[3].shape[2] == TILE
    return (on_line if line else general)(R, C, N, grad_out, *rest)


def solution(mesh):
    in_specs = (
        P(("row", "col"), "ch"),
        P(("row", "col"), "ch"),
        P(("row", "col"), "ch"),
        P("ch", None),
        P("row", "col", None, None, None),
        P("row", "col", None),
        P("row", "col"),
    )
    out_specs = (P(("row", "col"), "ch"), P("col", "ch"))
    R, C, N = mesh.shape["row"], mesh.shape["col"], mesh.shape["ch"]
    return jax.shard_map(
        functools.partial(per_device, R, C, N), mesh=mesh, in_specs=in_specs, out_specs=out_specs, check_vma=False
    )
```

```python
import functools

import jax
import jax.numpy as jnp
from jax import lax
from jax.experimental import pallas as pl
from jax.experimental.pallas import tpu as pltpu
from jax.sharding import PartitionSpec as P

TILE = 128
MESH = pl.DeviceIdType.MESH
F32 = jnp.float32
BF16 = jnp.bfloat16


def split(x):
    hi = x.astype(BF16)
    return hi, (x - hi.astype(F32)).astype(BF16)


def nn(a, b):
    return lax.dot_general(a, b, (((1,), (0,)), ((), ())), preferred_element_type=F32)


def nt(a, b):
    return lax.dot_general(a, b, (((1,), (1,)), ((), ())), preferred_element_type=F32)


def kernel(
    R, C, N, K,
    slot_ref, g_ref, mask_ref, sa_hbm, w_hbm, tiles_hbm,
    wg_ref, ig_ref, igr,
    M, G, tiles, at_hi, at_lo, w_f, w_hi, w_lo, sa, g_hi, g_lo,
    wgp, wgr, wgs, wgc, wgo,
    local_sem, zsend, zrecv, csend, crecv, wrsend, wrrecv, wcsend, wcrecv, wfsend, wfrecv,
    irsend, irrecv, iasend, iarecv,
):
    r, c, z = lax.axis_index("row"), lax.axis_index("col"), lax.axis_index("ch")
    HB, D = M.shape[2], M.shape[3]
    RC = R * C
    per = RC // N
    blk = wgp.shape[1]
    slots = tiles.shape[0]
    acc = ig_ref
    IN = acc.shape[0]
    in_tiles = IN // TILE
    tpb = HB // TILE
    piece = IN // R

    cp_w = pltpu.make_async_copy(w_hbm, w_f, local_sem.at[0])
    cp_sa = pltpu.make_async_copy(sa_hbm, sa, local_sem.at[1])
    cp_t = pltpu.make_async_copy(tiles_hbm, tiles, local_sem.at[2])
    cp_w.start()
    cp_sa.start()
    cp_t.start()

    def dev(r_, c_, z_):
        return {"row": r_, "col": c_, "ch": z_}

    q = r * C + c
    d_idx = z * per + q // N
    d_r, d_c, d_z = d_idx // C, d_idx % C, q % N
    s_q = (q % per) * N + z
    s_r, s_c, s_z = s_q // C, s_q % C, q // per
    away = jnp.logical_not((d_r == r) & (d_c == c) & (d_z == z))

    barrier = pltpu.get_barrier_semaphore()

    def hello(r_, c_, z_):
        pl.semaphore_signal(barrier, inc=1, device_id=dev(r_, c_, z_), device_id_type=MESH)

    for j in range(1, R):
        hello((r + j) % R, c, z)
    for j in range(1, C):
        hello(r, (c + j) % C, z)

    @pl.when(z > 0)
    def _():
        hello(r, c, z - 1)

    @pl.when(z < N - 1)
    def _():
        hello(r, c, z + 1)

    @pl.when(away)
    def _():
        hello(d_r, d_c, d_z)
        hello(s_r, s_c, s_z)

    def own(k):
        rows = pl.ds(pl.multiple_of(k * HB, HB), HB)
        M[z, k] = g_ref[rows, :] * mask_ref[rows, :].astype(F32)

    own(0)
    own(1)
    one_if = lambda cond: jnp.where(cond, 1, 0)
    greeted = R - 1 + C - 1 + one_if(z > 0) + one_if(z < N - 1) + 2 * one_if(away)
    pl.semaphore_wait(barrier, greeted)

    def zcopy(origin, k, step):
        way = 0 if step < 0 else 1
        return pltpu.make_async_remote_copy(
            src_ref=M.at[origin, k], dst_ref=M.at[origin, k],
            send_sem=zsend.at[way, origin, k], recv_sem=zrecv.at[origin, k],
            device_id=dev(r, c, z + step), device_id_type=MESH,
        )

    def own_send(k):
        @pl.when(z > 0)
        def _():
            zcopy(z, k, -1).start()

        @pl.when(z < N - 1)
        def _():
            zcopy(z, k, 1).start()

    own_send(0)
    own_send(1)
    acc[...] = jnp.zeros_like(acc)
    wgp[...] = jnp.zeros_like(wgp)
    cp_w.wait()
    for n in range(N):
        cols = slice(n * D, (n + 1) * D)
        w_hi[:, cols], w_lo[:, cols] = split(w_f[:, cols])
    cp_sa.wait()
    cp_t.wait()

    def prep(k, cc):
        for t in range(tpb):
            def one(i, _):
                p = ((cc * K + k) * tpb + t) * in_tiles + i
                v = slot_ref[p]
                tile = tiles[lax.rem(v, slots)]
                tile = jnp.where(v < slots, tile, jnp.zeros_like(tile))
                hi, lo = split(tile.T)
                rows = pl.ds(pl.multiple_of(i * TILE, TILE), TILE)
                cols = slice(cc * HB + t * TILE, cc * HB + (t + 1) * TILE)
                at_hi[k, rows, cols] = hi
                at_lo[k, rows, cols] = lo
                return 0

            lax.fori_loop(0, in_tiles, one, 0, unroll=2)

    def ccopy(k, j):
        return pltpu.make_async_remote_copy(
            src_ref=G.at[k, c], dst_ref=G.at[k, c],
            send_sem=csend.at[k, j], recv_sem=crecv.at[k, j],
            device_id=dev(r, (c + j) % C, z), device_id_type=MESH,
        )

    def cwait(k, j):
        o = (c + C - j) % C
        return pltpu.make_async_remote_copy(
            src_ref=G.at[k, o], dst_ref=G.at[k, o],
            send_sem=csend.at[k, j], recv_sem=crecv.at[k, j],
            device_id=dev(r, (c + j) % C, z), device_id_type=MESH,
        )

    def consume(k):
        for j in range(1, C):
            cwait(k, j).wait_recv()
        for n in range(C):
            rows = slice(n * HB, (n + 1) * HB)
            g_hi[rows, :], g_lo[rows, :] = split(G[k, n])

        def part(i, _):
            rows = pl.ds(pl.multiple_of(i * 256, 256), 256)
            a = at_hi[k, rows, :]
            acc[rows, :] += nn(a, g_hi[...]) + nn(a, g_lo[...]) + nn(at_lo[k, rows, :], g_hi[...])
            return 0

        lax.fori_loop(0, IN // 256, part, 0)

    def wrcopy(j):
        t = (r + j) % R
        return pltpu.make_async_remote_copy(
            src_ref=wgp.at[pl.ds(t * C, C)], dst_ref=wgr.at[j],
            send_sem=wrsend.at[j], recv_sem=wrrecv.at[j],
            device_id=dev(t, c, z), device_id_type=MESH,
        )

    groups = [[] for _ in range(N - 1)]
    for cc in range(C):
        groups[cc * max(N - 2, 1) // C].append(cc)

    def body(k, _):
        for d in range(1, N):
            @pl.when(z >= d)
            def _():
                zcopy(z - d, k, 1).wait_recv()

                @pl.when(z < N - 1)
                def _():
                    zcopy(z - d, k, 1).start()

            @pl.when(z + d < N)
            def _():
                zcopy(z + d, k, -1).wait_recv()

                @pl.when(z > 0)
                def _():
                    zcopy(z + d, k, -1).start()

            if d == 1:
                @pl.when(k + 2 < K)
                def _():
                    own(k + 2)
                    own_send(k + 2)

            for cc in groups[d - 1]:
                prep(k, cc)

        agg = jnp.zeros((HB, D), F32)
        for n in range(N):
            cols = slice(n * D, (n + 1) * D)
            hi, lo = split(M[n, k])
            agg += nt(hi, w_hi[:, cols]) + nt(lo, w_hi[:, cols]) + nt(hi, w_lo[:, cols])
        G[k, c] = agg
        for j in range(1, C):
            ccopy(k, j).start()

        rows = pl.ds(pl.multiple_of(k * HB, HB), HB)
        s_hi, s_lo = split(sa[rows, :].T)
        for n in range(N):
            hi, lo = split(M[n, k])
            res = nn(s_hi, hi) + nn(s_hi, lo) + nn(s_lo, hi)
            for h in range(per):
                wgp[h * N + n] += res[h * blk:(h + 1) * blk, :]

        @pl.when(k == K - 1)
        def _():
            for j in range(1, R):
                wrcopy(j).start()

        @pl.when(k > 0)
        def _():
            consume(k - 1)

        return 0

    lax.fori_loop(0, K, body, 0)

    def wccopy(j):
        t = (c + j) % C
        return pltpu.make_async_remote_copy(
            src_ref=wgs.at[t], dst_ref=wgc.at[j],
            send_sem=wcsend.at[j], recv_sem=wcrecv.at[j],
            device_id=dev(r, t, z), device_id_type=MESH,
        )

    wfcopy = pltpu.make_async_remote_copy(
        src_ref=wgo, dst_ref=wg_ref, send_sem=wfsend, recv_sem=wfrecv,
        device_id=dev(d_r, d_c, d_z), device_id_type=MESH,
    )

    def ircopy(j):
        t = (r + j) % R
        whole = R == 2
        rows = pl.ds(0, IN) if whole else pl.ds(pl.multiple_of(t * piece, piece), piece)
        return pltpu.make_async_remote_copy(
            src_ref=acc.at[rows], dst_ref=igr if whole else igr.at[j],
            send_sem=irsend.at[j], recv_sem=irrecv.at[j],
            device_id=dev(t, c, z), device_id_type=MESH,
        )

    mine = pl.ds(pl.multiple_of(r * piece, piece), piece)

    def iacopy(j):
        return pltpu.make_async_remote_copy(
            src_ref=ig_ref.at[mine], dst_ref=ig_ref.at[mine],
            send_sem=iasend.at[j], recv_sem=iarecv.at[j],
            device_id=dev((r + j) % R, c, z), device_id_type=MESH,
        )

    def iawait(j):
        theirs = pl.ds(pl.multiple_of(((r + R - j) % R) * piece, piece), piece)
        return pltpu.make_async_remote_copy(
            src_ref=ig_ref.at[theirs], dst_ref=ig_ref.at[theirs],
            send_sem=iasend.at[j], recv_sem=iarecv.at[j],
            device_id=dev((r + j) % R, c, z), device_id_type=MESH,
        )

    for j in range(1, R):
        wrcopy(j).wait_recv()
    total = wgp[pl.ds(r * C, C)]
    for j in range(1, R):
        total += wgr[j]
    wgs[...] = total
    for j in range(1, C):
        wccopy(j).start()

    consume(K - 1)
    for j in range(1, R):
        ircopy(j).start()
    for j in range(1, C):
        wccopy(j).wait_recv()
    wpart = wgs[c]
    for j in range(1, C):
        wpart += wgc[j]

    @pl.when(away)
    def _():
        wgo[...] = wpart
        wfcopy.start()
        wfcopy.wait()

    @pl.when(jnp.logical_not(away))
    def _():
        wg_ref[...] = wpart

    for j in range(1, R):
        ircopy(j).wait_recv()
    if R > 2:
        summed = acc[mine, :]
        for j in range(1, R):
            summed += igr[j]
        ig_ref[mine, :] = summed
        for j in range(1, R):
            iacopy(j).start()
        for j in range(1, R):
            iawait(j).wait_recv()

    for j in range(1, R):
        wrcopy(j).wait_send()
        ircopy(j).wait_send()
        if R > 2:
            iacopy(j).wait_send()
    for j in range(1, C):
        wccopy(j).wait_send()

    def drain(k, _):
        for j in range(1, C):
            ccopy(k, j).wait_send()
        for n in range(N):
            @pl.when((z > 0) & (z <= n))
            def _():
                zcopy(n, k, -1).wait_send()

            @pl.when((z < N - 1) & (z >= n))
            def _():
                zcopy(n, k, 1).wait_send()

        return 0

    lax.fori_loop(0, K, drain, 0)


def general(R, C, N, grad_out, relu_mask, saved_agg, weight, tile_vals, tile_pos, tile_count):
    H, D = grad_out.shape
    F = weight.shape[1]
    tiles = tile_vals[0, 0]
    slots = tiles.shape[0]
    out_rows = C * H
    IN = slots * TILE * TILE // out_rows
    HB = TILE
    K = H // HB
    blk = F // (R * C)
    s = jnp.arange(slots, dtype=jnp.int32)
    code = jnp.where(s < tile_count[0, 0], s, s + slots)
    where = jnp.sum(jnp.where(tile_pos[0, 0][None, :] == s[:, None], code[None, :], 0), axis=1).astype(jnp.int32)
    vmem = pl.BlockSpec(memory_space=pltpu.VMEM)
    hbm = pl.BlockSpec(memory_space=pl.ANY)
    dma = pltpu.SemaphoreType.DMA
    igr_shape = (IN, D) if R == 2 else (R, IN // R, D)
    wg, ig, igr = pl.pallas_call(
        functools.partial(kernel, R, C, N, K),
        out_shape=(
            jax.ShapeDtypeStruct((blk, D), F32),
            jax.ShapeDtypeStruct((IN, D), F32),
            jax.ShapeDtypeStruct(igr_shape, F32),
        ),
        in_specs=[pl.BlockSpec(memory_space=pltpu.SMEM), vmem, vmem, hbm, hbm, hbm],
        out_specs=(vmem, vmem, vmem),
        scratch_shapes=[
            pltpu.VMEM((N, K, HB, D), F32),
            pltpu.VMEM((K, C, HB, D), F32),
            pltpu.VMEM((slots, TILE, TILE), F32),
            pltpu.VMEM((K, IN, C * HB), BF16),
            pltpu.VMEM((K, IN, C * HB), BF16),
            pltpu.VMEM((D, F), F32),
            pltpu.VMEM((D, F), BF16),
            pltpu.VMEM((D, F), BF16),
            pltpu.VMEM((H, D), F32),
            pltpu.VMEM((C * HB, D), BF16),
            pltpu.VMEM((C * HB, D), BF16),
            pltpu.VMEM((R * C, blk, D), F32),
            pltpu.VMEM((R, C, blk, D), F32),
            pltpu.VMEM((C, blk, D), F32),
            pltpu.VMEM((C, blk, D), F32),
            pltpu.VMEM((blk, D), F32),
            dma((3,)),
            dma((2, N, K)), dma((N, K)),
            dma((K, C)), dma((K, C)),
            dma((R,)), dma((R,)),
            dma((C,)), dma((C,)),
            dma, dma,
            dma((R,)), dma((R,)),
            dma((R,)), dma((R,)),
        ],
        compiler_params=pltpu.CompilerParams(
            collective_id=0, has_side_effects=True, vmem_limit_bytes=60 * 1024 * 1024
        ),
    )(where, grad_out, relu_mask, saved_agg, weight, tiles)

    def finish(wg_in, a, b, wg_out, ig_out):
        wg_out[...] = wg_in[...]
        ig_out[...] = a[...] + b[...] if R == 2 else a[...]

    return pl.pallas_call(
        finish,
        out_shape=(jax.ShapeDtypeStruct((blk, D), F32), jax.ShapeDtypeStruct((IN, D), F32)),
        in_specs=[vmem, vmem, vmem if R == 2 else hbm],
        out_specs=(vmem, vmem),
    )(wg, ig, igr)


def cat_nn(a, b):
    return nn(jnp.concatenate([a[0], a[0], a[1]], axis=1), jnp.concatenate([b[0], b[1], b[0]], axis=0))


def line_kernel(
    R, C, N, chunks, raws, relays_end, relays_inner,
    count_ref, pos_ref, g_hbm, mask_hbm, sa_hbm, w_hbm, tiles_hbm,
    wg_ref, ig_ref, igr,
    slot_vec, slot_ref, mask, M, G, tiles, at_hi, at_lo, w_f, w_hi, w_lo, sa,
    we_f, we_hi, we_lo, sae, part, wgp, wgr, wgs, wgc, wgo, wgd,
    local_sem, zsend, zrecv, wesend, werecv, sasend, sarecv, psend, precv,
    csend, crecv, rsend, rrecv, tsend, trecv, dsend, drecv, irsend, irrecv,
):
    r, c, z = lax.axis_index("row"), lax.axis_index("col"), lax.axis_index("ch")
    H, D = M.shape[1], M.shape[2]
    T, K = H // TILE, len(chunks)
    per = R * C // N
    sub = wgo.shape[1]
    slots = tiles.shape[0]
    IN = ig_ref.shape[0]
    in_tiles = IN // TILE
    wide = (N - 1) * D
    nb = 2 * N - 1

    low = z < N // 2
    end = (z == 0) | (z == N - 1)
    inner = jnp.logical_not(end)
    z_in = jnp.where(low, z + 1, z - 1)
    z_out = jnp.where(low, z - 1, z + 1)
    e0 = jnp.where(low, 0, N - 1)
    e1 = jnp.where(low, 1, N - 2)
    o1 = jnp.where(low, 2, N - 3)
    o0 = jnp.where(low, N - 1, 0)
    p = r * C + c

    cp_g = pltpu.make_async_copy(g_hbm, M.at[z], local_sem.at[3])
    cp_m = pltpu.make_async_copy(mask_hbm, mask, local_sem.at[4])
    cp_s = pltpu.make_async_copy(slot_vec, slot_ref, local_sem.at[5])
    cp_w = pltpu.make_async_copy(w_hbm, w_f, local_sem.at[0])
    cp_sa = pltpu.make_async_copy(sa_hbm, sa, local_sem.at[1])
    cp_t = pltpu.make_async_copy(tiles_hbm, tiles, local_sem.at[2])

    def dev(r_, c_, z_):
        return {"row": r_, "col": c_, "ch": z_}

    one_if = lambda cond: jnp.where(cond, 1, 0)
    same = lambda r_, c_, z_: (r_ == r) & (c_ == c) & (z_ == z)
    far = jnp.logical_not

    own_q = per * z + r
    end_q = per * e0 + r
    block_n = [z, e0, o1, o0, e1, o1, o0]
    block_q = [own_q] * N + [end_q] * (N - 1)

    def goal(b):
        return block_q[b] // C, block_q[b] % C, block_n[b]

    my_a, my_r = p // per, p % per
    my_z = jnp.where(my_a == z, z, jnp.where(my_a == 0, 1, jnp.where(my_a == N - 1, N - 2, my_a)))

    my_far = ((my_a == 0) | (my_a == N - 1)) & (my_a != z)

    barrier = pltpu.get_barrier_semaphore()

    def hello(r_, c_, z_):
        pl.semaphore_signal(barrier, inc=1, device_id=dev(r_, c_, z_), device_id_type=MESH)

    hello(1 - r, c, z)
    for j in range(1, C):
        hello(r, (c + j) % C, z)
    hello(r, c, z_in)
    pl.when(inner)(lambda: hello(r, c, z_out))
    for j in range(C):
        pl.when(far(same(my_r, j, my_z)))(lambda: hello(my_r, j, my_z))
        pl.when(my_far)(lambda: hello(my_r, j, my_a))
    greeted = R - 1 + C - 1 + 1 + one_if(inner) + (N - 1) * one_if(end) + one_if(far(same(*goal(0))))
    for b in range(1, nb):
        greeted += one_if(inner & far(same(*goal(b))))

    for copy in (cp_g, cp_m, cp_w, cp_sa, cp_t):
        copy.start()

    def rows_of(k):
        return pl.ds(*chunks[k])

    square = (slots, slots)
    slot, place = lax.broadcasted_iota(jnp.int32, square, 0), lax.broadcasted_iota(jnp.int32, square, 1)
    code = jnp.where(slot < count_ref[0, 0], slot, slot + slots)
    hit = jnp.broadcast_to(pos_ref[...], square).T == place
    slot_vec[...] = jnp.sum(jnp.where(hit, code, 0), axis=0, keepdims=True)
    cp_s.start()
    cp_g.wait()
    cp_m.wait()
    for k in range(K):
        rows = rows_of(k)
        M[z, rows, :] = M[z, rows, :] * mask[rows, :].astype(F32)
    pl.semaphore_wait(barrier, greeted)

    def program(at_end):
        relays = relays_end if at_end else relays_inner
        pending = []

        def send(src, dst, ss, rs, to, cond=None):
            def make():
                return pltpu.make_async_remote_copy(
                    src_ref=src, dst_ref=dst, send_sem=ss, recv_sem=rs, device_id=to, device_id_type=MESH
                )

            pending.append((cond, make))
            if cond is None:
                make().start()
            else:
                pl.when(cond)(lambda: make().start())

        def recv(dst, ss, rs):
            pltpu.make_async_remote_copy(
                src_ref=dst, dst_ref=dst, send_sem=ss, recv_sem=rs, device_id=dev(1 - r, c, z), device_id_type=MESH
            ).wait_recv()

        def zpass(o, k):
            blk = M.at[o, rows_of(k)]
            send(blk, blk, zsend.at[0, o, k], zrecv.at[o, k], dev(r, c, z_in))

        def zout(o, k):
            if k in raws:
                blk = M.at[o, rows_of(k)]
                send(blk, blk, zsend.at[1, o, k], zrecv.at[o, k], dev(r, c, z_out))

        def zwait(o, k):
            recv(M.at[o, rows_of(k)], zsend.at[0, o, k], zrecv.at[o, k])

        def onward(k):
            zwait(e0, k)
            zpass(e0, k)

        def arrive(o, k):
            zwait(o, k)
            zout(o, k)

        def weights_pass():
            cols = pl.ds(pl.multiple_of(jnp.where(low, D, 0), D), wide)
            rows = pl.ds(pl.multiple_of(p * sub, sub), sub)
            send(w_f.at[rows, cols], we_f.at[p], wesend.at[0], werecv.at[0], dev(r, c, z_in))

        def sa_pass(t):
            send(sa.at[pl.ds(t * TILE, TILE)], sae.at[t], sasend.at[t], sarecv.at[t], dev(r, c, z_in))

        def outer(s, m):
            return cat_nn(s, split(m))

        def wadd(b, value, first):
            value = value.reshape(R, D // R, D)
            if first:
                wgp[b] = value
            else:
                wgp[b] += value

        def sa_own(t):
            return split(sa[t * TILE:(t + 1) * TILE, :].T)

        def tile_rows(o, t):
            return M[o, t * TILE:(t + 1) * TILE, :]

        def wgrad_own():
            for t in range(T):
                wadd(0, outer(sa_own(t), tile_rows(z, t)), t == 0)

        def wgrad_mine(t, bs):
            s = sa_own(t)
            for b in bs:
                wadd(b, outer(s, tile_rows(block_n[b], t)), t == 0)

        def wgrad_ends(t, first):
            if not at_end:
                recv(sae.at[t], sasend.at[t], sarecv.at[t])
            s = sa_own(t) if at_end else split(sae[t].T)
            for b in range(N, nb):
                wadd(b, outer(s, tile_rows(block_n[b], t)), first)

        groups = ((0, 1), (1, 2), (2, N), (N, nb))

        def red_row(n):
            lo, hi = groups[n]
            bs = pl.ds(lo, hi - lo)
            send(wgp.at[bs, 1 - r], wgr.at[bs], rsend.at[n], rrecv.at[n], dev(1 - r, c, z))

        def red_col(n):
            lo, hi = groups[n]
            bs = pl.ds(lo, hi - lo)
            recv(wgr.at[bs], rsend.at[n], rrecv.at[n])
            for b in range(lo, hi):
                total = wgp[b, r] + wgr[b]
                for t in range(C):
                    wgs[t, b] = total[t * sub:(t + 1) * sub]
            for j in range(1, C):
                t = (c + j) % C
                send(wgs.at[t, bs], wgc.at[j, bs], tsend.at[n, j], trecv.at[n, j], dev(r, t, z))

        def red_out(n):
            lo, hi = groups[n]
            bs = pl.ds(lo, hi - lo)
            for j in range(1, C):
                recv(wgc.at[j, bs], tsend.at[n, j], trecv.at[n, j])
            for b in range(lo, hi):
                total = wgs[c, b]
                for j in range(1, C):
                    total += wgc[j, b]
                wgo[b] = total
                x = 1 if at_end and b >= N else 0
                send(wgo.at[b], wgd.at[x, c], dsend.at[b], drecv.at[x, c], dev(*goal(b)), far(same(*goal(b))))

                @pl.when(same(*goal(b)))
                def _():
                    wgd[x, c] = wgo[b]

        def prep(t):
            inside = [k for k, (at, n) in enumerate(chunks) if at // TILE == t]
            HB = chunks[inside[0]][1]
            two = TILE // HB

            def one(i, _):
                rows = pl.ds(pl.multiple_of(i * TILE, TILE), TILE)
                for m in range(C // two):
                    got = []
                    for j in range(two):
                        v = slot_ref[0, ((two * m + j) * T + t) * in_tiles + i]
                        tile = tiles[lax.rem(v, slots)]
                        got.append(jnp.where(v < slots, tile, jnp.zeros_like(tile)))
                    for h, k in enumerate(inside):
                        mix = jnp.concatenate([x[h * HB:(h + 1) * HB] for x in got], axis=0)
                        hi, lo = split(mix.T)
                        base = C * chunks[k][0] + m * TILE
                        at_hi[rows, base:base + TILE] = hi
                        at_lo[rows, base:base + TILE] = lo
                return 0

            lax.fori_loop(0, in_tiles, one, 0)

        c_x = c + 1 - 2 * (c % 2)
        c_y = (c + 2) % C
        c_d = (c_x + 2) % C

        def gather_g(k):
            blk = G.at[c, rows_of(k)]
            send(blk, blk, csend.at[k, 0], crecv.at[k, 0], dev(r, c_x, z))
            send(blk, blk, csend.at[k, 1], crecv.at[k, 1], dev(r, c_y, z))
            if k not in relays:
                send(blk, blk, csend.at[k, 2], crecv.at[k, 2], dev(r, c_d, z))

        def relay(k):
            at, n = chunks[k]
            first, second = pl.ds(at, n // 2), pl.ds(at + n // 2, n // 2)
            recv(G.at[c_x, rows_of(k)], csend.at[k, 0], crecv.at[k, 0])
            blk = G.at[c_x, first]
            send(blk, blk, csend.at[k, 2], crecv.at[k, 2], dev(r, c_y, z))
            recv(G.at[c_y, rows_of(k)], csend.at[k, 1], crecv.at[k, 1])
            blk = G.at[c_y, second]
            send(blk, blk, csend.at[k, 3], crecv.at[k, 3], dev(r, c_x, z))

        def consume(k, last=False):
            at, n = chunks[k]
            if k in relays:
                recv(G.at[c_d, pl.ds(at, n // 2)], csend.at[k, 2], crecv.at[k, 2])
                recv(G.at[c_d, pl.ds(at + n // 2, n // 2)], csend.at[k, 3], crecv.at[k, 3])
            else:
                for j, o in enumerate((c_x, c_y, c_d)):
                    recv(G.at[o, rows_of(k)], csend.at[k, j], crecv.at[k, j])
            cols = slice(C * at, C * (at + n))
            g = split(G[:, at:at + n, :].reshape(C * n, D))
            step = IN // 4

            def block(rows):
                add = cat_nn((at_hi[rows, cols], at_lo[rows, cols]), g)
                if k == 0:
                    ig_ref[rows, :] = add
                else:
                    ig_ref[rows, :] += add

            for i in range(4):
                rows = pl.ds(i * step, step)
                block(rows)
                if last:
                    send(ig_ref.at[rows], igr.at[rows], irsend.at[i], irrecv.at[i], dev(1 - r, c, z))

        def own_cols(o):
            return pl.ds(pl.multiple_of(o * D, D), D)

        def end_cols(o):
            return pl.ds(pl.multiple_of((o - one_if(low)) * D, D), D)

        def times_w(os, rows, hi_w, lo_w, col_of):
            left, right = [], []
            for o in os:
                hi, lo = split(M[o, rows, :])
                cols = col_of(o)
                wh = hi_w[:, cols]
                left += [hi, lo, hi]
                right += [wh, wh, lo_w[:, cols]]
            return nt(jnp.concatenate(left, axis=1), jnp.concatenate(right, axis=1))

        whole = pl.ds(0, H)

        def partial_own():
            part[...] = times_w([e1], whole, we_hi, we_lo, end_cols)

        def partial(k):
            rows = rows_of(k)
            part[rows, :] += times_w([o1, o0], rows, we_hi, we_lo, end_cols)
            pc = part.at[rows]
            send(pc, pc, psend.at[k], precv.at[k], dev(r, c, z_out))

        def agg_own():
            G[c] = times_w([z], whole, w_hi, w_lo, own_cols)

        def agg_inner(k):
            rows = rows_of(k)
            G[c, rows, :] += times_w([e0, o1, o0], rows, w_hi, w_lo, own_cols)
            gather_g(k)

        def agg_end(k):
            rows = rows_of(k)
            if k in raws:
                for o in (e1, o1, o0):
                    zwait(o, k)
                G[c, rows, :] += times_w([e1, o1, o0], rows, w_hi, w_lo, own_cols)
            else:
                recv(part.at[rows], psend.at[k], precv.at[k])
                G[c, rows, :] += part[rows, :]
            gather_g(k)

        def end_weights(stage):
            if stage == 0:
                recv(we_f.at[p], wesend.at[0], werecv.at[0])
                for j in range(1, C):
                    send(we_f.at[p], we_f.at[p], wesend.at[j], werecv.at[j], dev(r, (c + j) % C, z))
            elif stage == 1:
                for j in range(1, C):
                    recv(we_f.at[r * C + (c + C - j) % C], wesend.at[j], werecv.at[j])
                mine = pl.ds(r * C, C)
                send(we_f.at[mine], we_f.at[mine], wesend.at[C], werecv.at[C], dev(1 - r, c, z))
            else:
                recv(we_f.at[pl.ds((1 - r) * C, C)], wesend.at[C], werecv.at[C])
                for i in range(R * C):
                    rows = slice(i * sub, (i + 1) * sub)
                    we_hi[rows, :], we_lo[rows, :] = split(we_f[i])

        def split_w():
            for n in range(N):
                cols = slice(n * D, (n + 1) * D)
                w_hi[:, cols], w_lo[:, cols] = split(w_f[:, cols])

        def finish_all():
            for j in range(C):
                pl.when(far(same(my_r, j, my_z)))(lambda: recv(wgd.at[0, j], dsend.at[0], drecv.at[0, j]))
                rows = slice(j * sub, (j + 1) * sub)
                wg_ref[rows, :] = wgd[0, j]

                @pl.when(my_far)
                def _():
                    recv(wgd.at[1, j], dsend.at[0], drecv.at[1, j])
                    wg_ref[rows, :] += wgd[1, j]

            for i in range(4):
                rows = pl.ds(i * (IN // 4), IN // 4)
                recv(igr.at[rows], irsend.at[i], irrecv.at[i])
            for cond, make in pending:
                if cond is None:
                    make().wait_send()
                else:
                    pl.when(cond)(lambda: make().wait_send())

        if at_end:
            cp_w.wait()
            weights_pass()
            zpass(z, 0)
            split_w()
            zpass(z, 1)
            zpass(z, 2)
            cp_t.wait()
            cp_s.wait()
            prep(2)
            prep(3)
            zpass(z, 4)
            prep(0)
            zpass(z, 3)
            cp_sa.wait()
            wgrad_own()
            zpass(z, 5)
            agg_own()
            sa_pass(1)
            sa_pass(2)
            red_row(0)
            agg_end(0)
            sa_pass(3)
            red_col(0)
            agg_end(1)
            wgrad_ends(0, True)
            relay(0)
            red_row(3)
            red_col(3)
            relay(1)
            agg_end(4)
            agg_end(2)
            agg_end(3)
            prep(1)
            relay(4)
            agg_end(5)
            red_out(0)
            red_out(3)
            consume(0)
            relay(3)
            relay(2)
            relay(5)
            consume(4)
            consume(3)
            consume(1)
            consume(2)
            consume(5, True)
        else:
            zpass(z, 1)
            zpass(z, 0)
            cp_t.wait()
            cp_s.wait()
            prep(3)
            zpass(z, 2)
            zout(z, 1)
            end_weights(0)
            cp_sa.wait()
            wgrad_own()
            onward(0)
            zout(z, 0)
            arrive(o1, 1)
            cp_w.wait()
            split_w()
            onward(1)
            arrive(o1, 0)
            agg_own()
            zpass(z, 4)
            prep(0)
            red_row(0)
            arrive(o0, 0)
            onward(2)
            agg_inner(0)
            red_col(0)
            arrive(o0, 1)
            end_weights(1)
            wgrad_mine(0, (1, 2, 3))
            onward(4)
            arrive(o1, 4)
            agg_inner(1)
            arrive(o1, 2)
            zpass(z, 3)
            relay(0)
            wgrad_mine(1, (1,))
            end_weights(2)
            partial_own()
            onward(3)
            arrive(o0, 2)
            agg_inner(2)
            onward(5)
            arrive(o0, 4)
            wgrad_mine(2, (1,))
            agg_inner(4)
            wgrad_mine(3, (1,))
            partial(4)
            red_row(1)
            relay(1)
            red_col(1)
            consume(0)
            zpass(z, 5)
            partial(2)
            relay(2)
            wgrad_ends(1, True)
            prep(1)
            arrive(o1, 3)
            arrive(o0, 3)
            agg_inner(3)
            partial(3)
            wgrad_ends(2, False)
            red_out(0)
            arrive(o0, 5)
            wgrad_mine(2, (2, 3))
            arrive(o1, 5)
            wgrad_ends(3, False)
            wgrad_mine(3, (2, 3))
            wgrad_mine(1, (2, 3))
            red_row(2)
            agg_inner(5)
            consume(1)
            partial(5)
            red_row(3)
            red_col(2)
            red_col(3)
            relay(3)
            relay(5)
            red_out(1)
            relay(4)
            red_out(2)
            consume(2)
            red_out(3)
            prep(2)
            consume(3)
            consume(4)
            consume(5, True)
        finish_all()

    pl.when(end)(lambda: program(True))
    pl.when(inner)(lambda: program(False))


def on_line(R, C, N, grad_out, relu_mask, saved_agg, weight, tile_vals, tile_pos, tile_count):
    H, D = grad_out.shape
    F = weight.shape[1]
    tiles = tile_vals[0, 0]
    slots = tiles.shape[0]
    IN = slots * TILE * TILE // (C * H)
    T = H // TILE
    chunks = [(t * TILE + h * (TILE // n), TILE // n) for t, n in enumerate(CUTS) for h in range(n)]
    K = len(chunks)
    blk = F // (R * C)
    sub = D // (R * C)
    nb = 2 * N - 1
    vmem = pl.BlockSpec(memory_space=pltpu.VMEM)
    hbm = pl.BlockSpec(memory_space=pl.ANY)
    dma = pltpu.SemaphoreType.DMA
    wg, ig, igr = pl.pallas_call(
        functools.partial(line_kernel, R, C, N, chunks, (0, 1), (0, 1, 2, 3, 4, 5), (0, 1, 2, 3, 4, 5)),
        out_shape=(
            jax.ShapeDtypeStruct((blk, D), F32),
            jax.ShapeDtypeStruct((IN, D), F32),
            jax.ShapeDtypeStruct((IN, D), F32),
        ),
        in_specs=[pl.BlockSpec(memory_space=pltpu.SMEM), vmem, hbm, hbm, hbm, hbm, hbm],
        out_specs=(vmem, vmem, vmem),
        scratch_shapes=[
            pltpu.VMEM((1, slots), jnp.int32),
            pltpu.SMEM((1, slots), jnp.int32),
            pltpu.VMEM((H, D), jnp.int32),
            pltpu.VMEM((N, H, D), F32),
            pltpu.VMEM((C, H, D), F32),
            pltpu.VMEM((slots, TILE, TILE), F32),
            pltpu.VMEM((IN, C * H), BF16),
            pltpu.VMEM((IN, C * H), BF16),
            pltpu.VMEM((D, F), F32),
            pltpu.VMEM((D, F), BF16),
            pltpu.VMEM((D, F), BF16),
            pltpu.VMEM((H, D), F32),
            pltpu.VMEM((R * C, sub, (N - 1) * D), F32),
            pltpu.VMEM((D, (N - 1) * D), BF16),
            pltpu.VMEM((D, (N - 1) * D), BF16),
            pltpu.VMEM((T, TILE, D), F32),
            pltpu.VMEM((H, D), F32),
            pltpu.VMEM((nb, R, D // R, D), F32),
            pltpu.VMEM((nb, D // R, D), F32),
            pltpu.VMEM((C, nb, sub, D), F32),
            pltpu.VMEM((C, nb, sub, D), F32),
            pltpu.VMEM((nb, sub, D), F32),
            pltpu.VMEM((2, C, sub, D), F32),
            dma((6,)),
            dma((2, N, K)), dma((N, K)),
            dma((C + 1,)), dma((C + 1,)),
            dma((T,)), dma((T,)),
            dma((K,)), dma((K,)),
            dma((K, C)), dma((K, C)),
            dma((4,)), dma((4,)),
            dma((4, C)), dma((4, C)),
            dma((nb,)), dma((2, C)),
            dma((4,)), dma((4,)),
        ],
        compiler_params=pltpu.CompilerParams(
            collective_id=0, has_side_effects=True, vmem_limit_bytes=60 * 1024 * 1024
        ),
    )(tile_count, tile_pos[0], grad_out, relu_mask, saved_agg, weight, tiles)

    def finish(wg_in, a, b, wg_out, ig_out):
        wg_out[...] = wg_in[...]
        ig_out[...] = a[...] + b[...]

    return pl.pallas_call(
        finish,
        out_shape=(jax.ShapeDtypeStruct((blk, D), F32), jax.ShapeDtypeStruct((IN, D), F32)),
        in_specs=[vmem, vmem, vmem],
        out_specs=(vmem, vmem),
    )(wg, ig, igr)


CUTS = (2, 1, 1, 2)


def per_device(R, C, N, grad_out, *rest):
    H, D = grad_out.shape
    line = R == 2 and C == 4 and N == 4 and D % (8 * R * C) == 0
    line = line and H == len(CUTS) * TILE and rest[3].shape[2] == TILE
    return (on_line if line else general)(R, C, N, grad_out, *rest)


def solution(mesh):
    in_specs = (
        P(("row", "col"), "ch"),
        P(("row", "col"), "ch"),
        P(("row", "col"), "ch"),
        P("ch", None),
        P("row", "col", None, None, None),
        P("row", "col", None),
        P("row", "col"),
    )
    out_specs = (P(("row", "col"), "ch"), P("col", "ch"))
    R, C, N = mesh.shape["row"], mesh.shape["col"], mesh.shape["ch"]
    return jax.shard_map(
        functools.partial(per_device, R, C, N), mesh=mesh, in_specs=in_specs, out_specs=out_specs, check_vma=False
    )
```

```python
import functools

import jax
import jax.numpy as jnp
from jax import lax
from jax.experimental import pallas as pl
from jax.experimental.pallas import tpu as pltpu
from jax.sharding import PartitionSpec as P

TILE = 128
MESH = pl.DeviceIdType.MESH
F32 = jnp.float32
BF16 = jnp.bfloat16


def split(x):
    hi = x.astype(BF16)
    return hi, (x - hi.astype(F32)).astype(BF16)


def nn(a, b):
    return lax.dot_general(a, b, (((1,), (0,)), ((), ())), preferred_element_type=F32)


def nt(a, b):
    return lax.dot_general(a, b, (((1,), (1,)), ((), ())), preferred_element_type=F32)


def kernel(
    R, C, N, K,
    slot_ref, g_ref, mask_ref, sa_hbm, w_hbm, tiles_hbm,
    wg_ref, ig_ref, igr,
    M, G, tiles, at_hi, at_lo, w_f, w_hi, w_lo, sa, g_hi, g_lo,
    wgp, wgr, wgs, wgc, wgo,
    local_sem, zsend, zrecv, csend, crecv, wrsend, wrrecv, wcsend, wcrecv, wfsend, wfrecv,
    irsend, irrecv, iasend, iarecv,
):
    r, c, z = lax.axis_index("row"), lax.axis_index("col"), lax.axis_index("ch")
    HB, D = M.shape[2], M.shape[3]
    RC = R * C
    per = RC // N
    blk = wgp.shape[1]
    slots = tiles.shape[0]
    acc = ig_ref
    IN = acc.shape[0]
    in_tiles = IN // TILE
    tpb = HB // TILE
    piece = IN // R

    cp_w = pltpu.make_async_copy(w_hbm, w_f, local_sem.at[0])
    cp_sa = pltpu.make_async_copy(sa_hbm, sa, local_sem.at[1])
    cp_t = pltpu.make_async_copy(tiles_hbm, tiles, local_sem.at[2])
    cp_w.start()
    cp_sa.start()
    cp_t.start()

    def dev(r_, c_, z_):
        return {"row": r_, "col": c_, "ch": z_}

    q = r * C + c
    d_idx = z * per + q // N
    d_r, d_c, d_z = d_idx // C, d_idx % C, q % N
    s_q = (q % per) * N + z
    s_r, s_c, s_z = s_q // C, s_q % C, q // per
    away = jnp.logical_not((d_r == r) & (d_c == c) & (d_z == z))

    barrier = pltpu.get_barrier_semaphore()

    def hello(r_, c_, z_):
        pl.semaphore_signal(barrier, inc=1, device_id=dev(r_, c_, z_), device_id_type=MESH)

    for j in range(1, R):
        hello((r + j) % R, c, z)
    for j in range(1, C):
        hello(r, (c + j) % C, z)

    @pl.when(z > 0)
    def _():
        hello(r, c, z - 1)

    @pl.when(z < N - 1)
    def _():
        hello(r, c, z + 1)

    @pl.when(away)
    def _():
        hello(d_r, d_c, d_z)
        hello(s_r, s_c, s_z)

    def own(k):
        rows = pl.ds(pl.multiple_of(k * HB, HB), HB)
        M[z, k] = g_ref[rows, :] * mask_ref[rows, :].astype(F32)

    own(0)
    own(1)
    one_if = lambda cond: jnp.where(cond, 1, 0)
    greeted = R - 1 + C - 1 + one_if(z > 0) + one_if(z < N - 1) + 2 * one_if(away)
    pl.semaphore_wait(barrier, greeted)

    def zcopy(origin, k, step):
        way = 0 if step < 0 else 1
        return pltpu.make_async_remote_copy(
            src_ref=M.at[origin, k], dst_ref=M.at[origin, k],
            send_sem=zsend.at[way, origin, k], recv_sem=zrecv.at[origin, k],
            device_id=dev(r, c, z + step), device_id_type=MESH,
        )

    def own_send(k):
        @pl.when(z > 0)
        def _():
            zcopy(z, k, -1).start()

        @pl.when(z < N - 1)
        def _():
            zcopy(z, k, 1).start()

    own_send(0)
    own_send(1)
    acc[...] = jnp.zeros_like(acc)
    wgp[...] = jnp.zeros_like(wgp)
    cp_w.wait()
    for n in range(N):
        cols = slice(n * D, (n + 1) * D)
        w_hi[:, cols], w_lo[:, cols] = split(w_f[:, cols])
    cp_sa.wait()
    cp_t.wait()

    def prep(k, cc):
        for t in range(tpb):
            def one(i, _):
                p = ((cc * K + k) * tpb + t) * in_tiles + i
                v = slot_ref[p]
                tile = tiles[lax.rem(v, slots)]
                tile = jnp.where(v < slots, tile, jnp.zeros_like(tile))
                hi, lo = split(tile.T)
                rows = pl.ds(pl.multiple_of(i * TILE, TILE), TILE)
                cols = slice(cc * HB + t * TILE, cc * HB + (t + 1) * TILE)
                at_hi[k, rows, cols] = hi
                at_lo[k, rows, cols] = lo
                return 0

            lax.fori_loop(0, in_tiles, one, 0, unroll=2)

    def ccopy(k, j):
        return pltpu.make_async_remote_copy(
            src_ref=G.at[k, c], dst_ref=G.at[k, c],
            send_sem=csend.at[k, j], recv_sem=crecv.at[k, j],
            device_id=dev(r, (c + j) % C, z), device_id_type=MESH,
        )

    def cwait(k, j):
        o = (c + C - j) % C
        return pltpu.make_async_remote_copy(
            src_ref=G.at[k, o], dst_ref=G.at[k, o],
            send_sem=csend.at[k, j], recv_sem=crecv.at[k, j],
            device_id=dev(r, (c + j) % C, z), device_id_type=MESH,
        )

    def consume(k):
        for j in range(1, C):
            cwait(k, j).wait_recv()
        for n in range(C):
            rows = slice(n * HB, (n + 1) * HB)
            g_hi[rows, :], g_lo[rows, :] = split(G[k, n])

        def part(i, _):
            rows = pl.ds(pl.multiple_of(i * 256, 256), 256)
            a = at_hi[k, rows, :]
            acc[rows, :] += nn(a, g_hi[...]) + nn(a, g_lo[...]) + nn(at_lo[k, rows, :], g_hi[...])
            return 0

        lax.fori_loop(0, IN // 256, part, 0)

    def wrcopy(j):
        t = (r + j) % R
        return pltpu.make_async_remote_copy(
            src_ref=wgp.at[pl.ds(t * C, C)], dst_ref=wgr.at[j],
            send_sem=wrsend.at[j], recv_sem=wrrecv.at[j],
            device_id=dev(t, c, z), device_id_type=MESH,
        )

    groups = [[] for _ in range(N - 1)]
    for cc in range(C):
        groups[cc * max(N - 2, 1) // C].append(cc)

    def body(k, _):
        for d in range(1, N):
            @pl.when(z >= d)
            def _():
                zcopy(z - d, k, 1).wait_recv()

                @pl.when(z < N - 1)
                def _():
                    zcopy(z - d, k, 1).start()

            @pl.when(z + d < N)
            def _():
                zcopy(z + d, k, -1).wait_recv()

                @pl.when(z > 0)
                def _():
                    zcopy(z + d, k, -1).start()

            if d == 1:
                @pl.when(k + 2 < K)
                def _():
                    own(k + 2)
                    own_send(k + 2)

            for cc in groups[d - 1]:
                prep(k, cc)

        agg = jnp.zeros((HB, D), F32)
        for n in range(N):
            cols = slice(n * D, (n + 1) * D)
            hi, lo = split(M[n, k])
            agg += nt(hi, w_hi[:, cols]) + nt(lo, w_hi[:, cols]) + nt(hi, w_lo[:, cols])
        G[k, c] = agg
        for j in range(1, C):
            ccopy(k, j).start()

        rows = pl.ds(pl.multiple_of(k * HB, HB), HB)
        s_hi, s_lo = split(sa[rows, :].T)
        for n in range(N):
            hi, lo = split(M[n, k])
            res = nn(s_hi, hi) + nn(s_hi, lo) + nn(s_lo, hi)
            for h in range(per):
                wgp[h * N + n] += res[h * blk:(h + 1) * blk, :]

        @pl.when(k == K - 1)
        def _():
            for j in range(1, R):
                wrcopy(j).start()

        @pl.when(k > 0)
        def _():
            consume(k - 1)

        return 0

    lax.fori_loop(0, K, body, 0)

    def wccopy(j):
        t = (c + j) % C
        return pltpu.make_async_remote_copy(
            src_ref=wgs.at[t], dst_ref=wgc.at[j],
            send_sem=wcsend.at[j], recv_sem=wcrecv.at[j],
            device_id=dev(r, t, z), device_id_type=MESH,
        )

    wfcopy = pltpu.make_async_remote_copy(
        src_ref=wgo, dst_ref=wg_ref, send_sem=wfsend, recv_sem=wfrecv,
        device_id=dev(d_r, d_c, d_z), device_id_type=MESH,
    )

    def ircopy(j):
        t = (r + j) % R
        whole = R == 2
        rows = pl.ds(0, IN) if whole else pl.ds(pl.multiple_of(t * piece, piece), piece)
        return pltpu.make_async_remote_copy(
            src_ref=acc.at[rows], dst_ref=igr if whole else igr.at[j],
            send_sem=irsend.at[j], recv_sem=irrecv.at[j],
            device_id=dev(t, c, z), device_id_type=MESH,
        )

    mine = pl.ds(pl.multiple_of(r * piece, piece), piece)

    def iacopy(j):
        return pltpu.make_async_remote_copy(
            src_ref=ig_ref.at[mine], dst_ref=ig_ref.at[mine],
            send_sem=iasend.at[j], recv_sem=iarecv.at[j],
            device_id=dev((r + j) % R, c, z), device_id_type=MESH,
        )

    def iawait(j):
        theirs = pl.ds(pl.multiple_of(((r + R - j) % R) * piece, piece), piece)
        return pltpu.make_async_remote_copy(
            src_ref=ig_ref.at[theirs], dst_ref=ig_ref.at[theirs],
            send_sem=iasend.at[j], recv_sem=iarecv.at[j],
            device_id=dev((r + j) % R, c, z), device_id_type=MESH,
        )

    for j in range(1, R):
        wrcopy(j).wait_recv()
    total = wgp[pl.ds(r * C, C)]
    for j in range(1, R):
        total += wgr[j]
    wgs[...] = total
    for j in range(1, C):
        wccopy(j).start()

    consume(K - 1)
    for j in range(1, R):
        ircopy(j).start()
    for j in range(1, C):
        wccopy(j).wait_recv()
    wpart = wgs[c]
    for j in range(1, C):
        wpart += wgc[j]

    @pl.when(away)
    def _():
        wgo[...] = wpart
        wfcopy.start()
        wfcopy.wait()

    @pl.when(jnp.logical_not(away))
    def _():
        wg_ref[...] = wpart

    for j in range(1, R):
        ircopy(j).wait_recv()
    if R > 2:
        summed = acc[mine, :]
        for j in range(1, R):
            summed += igr[j]
        ig_ref[mine, :] = summed
        for j in range(1, R):
            iacopy(j).start()
        for j in range(1, R):
            iawait(j).wait_recv()

    for j in range(1, R):
        wrcopy(j).wait_send()
        ircopy(j).wait_send()
        if R > 2:
            iacopy(j).wait_send()
    for j in range(1, C):
        wccopy(j).wait_send()

    def drain(k, _):
        for j in range(1, C):
            ccopy(k, j).wait_send()
        for n in range(N):
            @pl.when((z > 0) & (z <= n))
            def _():
                zcopy(n, k, -1).wait_send()

            @pl.when((z < N - 1) & (z >= n))
            def _():
                zcopy(n, k, 1).wait_send()

        return 0

    lax.fori_loop(0, K, drain, 0)


def general(R, C, N, grad_out, relu_mask, saved_agg, weight, tile_vals, tile_pos, tile_count):
    H, D = grad_out.shape
    F = weight.shape[1]
    tiles = tile_vals[0, 0]
    slots = tiles.shape[0]
    out_rows = C * H
    IN = slots * TILE * TILE // out_rows
    HB = TILE
    K = H // HB
    blk = F // (R * C)
    s = jnp.arange(slots, dtype=jnp.int32)
    code = jnp.where(s < tile_count[0, 0], s, s + slots)
    where = jnp.sum(jnp.where(tile_pos[0, 0][None, :] == s[:, None], code[None, :], 0), axis=1).astype(jnp.int32)
    vmem = pl.BlockSpec(memory_space=pltpu.VMEM)
    hbm = pl.BlockSpec(memory_space=pl.ANY)
    dma = pltpu.SemaphoreType.DMA
    igr_shape = (IN, D) if R == 2 else (R, IN // R, D)
    wg, ig, igr = pl.pallas_call(
        functools.partial(kernel, R, C, N, K),
        out_shape=(
            jax.ShapeDtypeStruct((blk, D), F32),
            jax.ShapeDtypeStruct((IN, D), F32),
            jax.ShapeDtypeStruct(igr_shape, F32),
        ),
        in_specs=[pl.BlockSpec(memory_space=pltpu.SMEM), vmem, vmem, hbm, hbm, hbm],
        out_specs=(vmem, vmem, vmem),
        scratch_shapes=[
            pltpu.VMEM((N, K, HB, D), F32),
            pltpu.VMEM((K, C, HB, D), F32),
            pltpu.VMEM((slots, TILE, TILE), F32),
            pltpu.VMEM((K, IN, C * HB), BF16),
            pltpu.VMEM((K, IN, C * HB), BF16),
            pltpu.VMEM((D, F), F32),
            pltpu.VMEM((D, F), BF16),
            pltpu.VMEM((D, F), BF16),
            pltpu.VMEM((H, D), F32),
            pltpu.VMEM((C * HB, D), BF16),
            pltpu.VMEM((C * HB, D), BF16),
            pltpu.VMEM((R * C, blk, D), F32),
            pltpu.VMEM((R, C, blk, D), F32),
            pltpu.VMEM((C, blk, D), F32),
            pltpu.VMEM((C, blk, D), F32),
            pltpu.VMEM((blk, D), F32),
            dma((3,)),
            dma((2, N, K)), dma((N, K)),
            dma((K, C)), dma((K, C)),
            dma((R,)), dma((R,)),
            dma((C,)), dma((C,)),
            dma, dma,
            dma((R,)), dma((R,)),
            dma((R,)), dma((R,)),
        ],
        compiler_params=pltpu.CompilerParams(
            collective_id=0, has_side_effects=True, vmem_limit_bytes=60 * 1024 * 1024
        ),
    )(where, grad_out, relu_mask, saved_agg, weight, tiles)

    def finish(wg_in, a, b, wg_out, ig_out):
        wg_out[...] = wg_in[...]
        ig_out[...] = a[...] + b[...] if R == 2 else a[...]

    return pl.pallas_call(
        finish,
        out_shape=(jax.ShapeDtypeStruct((blk, D), F32), jax.ShapeDtypeStruct((IN, D), F32)),
        in_specs=[vmem, vmem, vmem if R == 2 else hbm],
        out_specs=(vmem, vmem),
    )(wg, ig, igr)


def cat_nn(a, b):
    return nn(jnp.concatenate([a[0], a[0], a[1]], axis=1), jnp.concatenate([b[0], b[1], b[0]], axis=0))


def line_kernel(
    R, C, N, chunks, raws, relays_end, relays_inner,
    count_ref, pos_ref, g_hbm, mask_hbm, sa_hbm, w_hbm, tiles_hbm,
    wg_ref, ig_hbm, igr,
    ig_ref, slot_vec, slot_ref, mask, M, G, tiles, at_hi, at_lo, w_f, w_hi, w_lo, sa,
    we_f, we_hi, we_lo, sae, part, wgp, wgr, wgs, wgc, wgo, wgd,
    local_sem, zsend, zrecv, wesend, werecv, sasend, sarecv, psend, precv,
    csend, crecv, rsend, rrecv, tsend, trecv, dsend, drecv, irsend, irrecv, igsem,
):
    r, c, z = lax.axis_index("row"), lax.axis_index("col"), lax.axis_index("ch")
    H, D = M.shape[1], M.shape[2]
    T, K = H // TILE, len(chunks)
    per = R * C // N
    sub = wgo.shape[1]
    slots = tiles.shape[0]
    IN = ig_ref.shape[0]
    in_tiles = IN // TILE
    wide = (N - 1) * D
    nb = 2 * N - 1

    low = z < N // 2
    end = (z == 0) | (z == N - 1)
    inner = jnp.logical_not(end)
    z_in = jnp.where(low, z + 1, z - 1)
    z_out = jnp.where(low, z - 1, z + 1)
    e0 = jnp.where(low, 0, N - 1)
    e1 = jnp.where(low, 1, N - 2)
    o1 = jnp.where(low, 2, N - 3)
    o0 = jnp.where(low, N - 1, 0)
    p = r * C + c

    cp_g = pltpu.make_async_copy(g_hbm, M.at[z], local_sem.at[3])
    cp_m = pltpu.make_async_copy(mask_hbm, mask, local_sem.at[4])
    cp_s = pltpu.make_async_copy(slot_vec, slot_ref, local_sem.at[5])
    cp_w = pltpu.make_async_copy(w_hbm, w_f, local_sem.at[0])
    cp_sa = pltpu.make_async_copy(sa_hbm, sa, local_sem.at[1])
    cp_t = pltpu.make_async_copy(tiles_hbm, tiles, local_sem.at[2])

    def dev(r_, c_, z_):
        return {"row": r_, "col": c_, "ch": z_}

    one_if = lambda cond: jnp.where(cond, 1, 0)
    same = lambda r_, c_, z_: (r_ == r) & (c_ == c) & (z_ == z)
    far = jnp.logical_not

    own_q = per * z + r
    end_q = per * e0 + r
    block_n = [z, e0, o1, o0, e1, o1, o0]
    block_q = [own_q] * N + [end_q] * (N - 1)

    def goal(b):
        return block_q[b] // C, block_q[b] % C, block_n[b]

    my_a, my_r = p // per, p % per
    my_z = jnp.where(my_a == z, z, jnp.where(my_a == 0, 1, jnp.where(my_a == N - 1, N - 2, my_a)))

    my_far = ((my_a == 0) | (my_a == N - 1)) & (my_a != z)

    barrier = pltpu.get_barrier_semaphore()

    def hello(r_, c_, z_):
        pl.semaphore_signal(barrier, inc=1, device_id=dev(r_, c_, z_), device_id_type=MESH)

    hello(1 - r, c, z)
    for j in range(1, C):
        hello(r, (c + j) % C, z)
    hello(r, c, z_in)
    pl.when(inner)(lambda: hello(r, c, z_out))
    for j in range(C):
        pl.when(far(same(my_r, j, my_z)))(lambda: hello(my_r, j, my_z))
        pl.when(my_far)(lambda: hello(my_r, j, my_a))
    greeted = R - 1 + C - 1 + 1 + one_if(inner) + (N - 1) * one_if(end) + one_if(far(same(*goal(0))))
    for b in range(1, nb):
        greeted += one_if(inner & far(same(*goal(b))))

    for copy in (cp_g, cp_m, cp_w, cp_sa, cp_t):
        copy.start()

    def rows_of(k):
        return pl.ds(*chunks[k])

    square = (slots, slots)
    slot, place = lax.broadcasted_iota(jnp.int32, square, 0), lax.broadcasted_iota(jnp.int32, square, 1)
    code = jnp.where(slot < count_ref[0, 0], slot, slot + slots)
    hit = jnp.broadcast_to(pos_ref[...], square).T == place
    slot_vec[...] = jnp.sum(jnp.where(hit, code, 0), axis=0, keepdims=True)
    cp_s.start()
    cp_g.wait()
    cp_m.wait()
    for k in range(K):
        rows = rows_of(k)
        M[z, rows, :] = M[z, rows, :] * mask[rows, :].astype(F32)
    pl.semaphore_wait(barrier, greeted)

    def program(at_end):
        relays = relays_end if at_end else relays_inner
        pending = []

        def send(src, dst, ss, rs, to, cond=None):
            def make():
                return pltpu.make_async_remote_copy(
                    src_ref=src, dst_ref=dst, send_sem=ss, recv_sem=rs, device_id=to, device_id_type=MESH
                )

            pending.append((cond, make))
            if cond is None:
                make().start()
            else:
                pl.when(cond)(lambda: make().start())

        def recv(dst, ss, rs):
            pltpu.make_async_remote_copy(
                src_ref=dst, dst_ref=dst, send_sem=ss, recv_sem=rs, device_id=dev(1 - r, c, z), device_id_type=MESH
            ).wait_recv()

        def zpass(o, k):
            blk = M.at[o, rows_of(k)]
            send(blk, blk, zsend.at[0, o, k], zrecv.at[o, k], dev(r, c, z_in))

        def zout(o, k):
            if k in raws:
                blk = M.at[o, rows_of(k)]
                send(blk, blk, zsend.at[1, o, k], zrecv.at[o, k], dev(r, c, z_out))

        def zwait(o, k):
            recv(M.at[o, rows_of(k)], zsend.at[0, o, k], zrecv.at[o, k])

        def onward(k):
            zwait(e0, k)
            zpass(e0, k)

        def arrive(o, k):
            zwait(o, k)
            zout(o, k)

        def weights_pass():
            cols = pl.ds(pl.multiple_of(jnp.where(low, D, 0), D), wide)
            rows = pl.ds(pl.multiple_of(p * sub, sub), sub)
            send(w_f.at[rows, cols], we_f.at[p], wesend.at[0], werecv.at[0], dev(r, c, z_in))

        def sa_pass(t):
            send(sa.at[pl.ds(t * TILE, TILE)], sae.at[t], sasend.at[t], sarecv.at[t], dev(r, c, z_in))

        def outer(s, m):
            return cat_nn(s, split(m))

        def wadd(b, value, first):
            value = value.reshape(R, D // R, D)
            if first:
                wgp[b] = value
            else:
                wgp[b] += value

        def sa_own(t):
            return split(sa[t * TILE:(t + 1) * TILE, :].T)

        def tile_rows(o, t):
            return M[o, t * TILE:(t + 1) * TILE, :]

        def wgrad_own():
            for t in range(T):
                wadd(0, outer(sa_own(t), tile_rows(z, t)), t == 0)

        def wgrad_mine(t, bs):
            s = sa_own(t)
            for b in bs:
                wadd(b, outer(s, tile_rows(block_n[b], t)), t == 0)

        def wgrad_ends(t, first):
            if not at_end:
                recv(sae.at[t], sasend.at[t], sarecv.at[t])
            s = sa_own(t) if at_end else split(sae[t].T)
            for b in range(N, nb):
                wadd(b, outer(s, tile_rows(block_n[b], t)), first)

        groups = ((0, 1), (1, 2), (2, N), (N, nb))

        def red_row(n):
            lo, hi = groups[n]
            bs = pl.ds(lo, hi - lo)
            send(wgp.at[bs, 1 - r], wgr.at[bs], rsend.at[n], rrecv.at[n], dev(1 - r, c, z))

        def red_col(n):
            lo, hi = groups[n]
            bs = pl.ds(lo, hi - lo)
            recv(wgr.at[bs], rsend.at[n], rrecv.at[n])
            for b in range(lo, hi):
                total = wgp[b, r] + wgr[b]
                for t in range(C):
                    wgs[t, b] = total[t * sub:(t + 1) * sub]
            for j in range(1, C):
                t = (c + j) % C
                send(wgs.at[t, bs], wgc.at[j, bs], tsend.at[n, j], trecv.at[n, j], dev(r, t, z))

        def red_out(n):
            lo, hi = groups[n]
            bs = pl.ds(lo, hi - lo)
            for j in range(1, C):
                recv(wgc.at[j, bs], tsend.at[n, j], trecv.at[n, j])
            for b in range(lo, hi):
                total = wgs[c, b]
                for j in range(1, C):
                    total += wgc[j, b]
                wgo[b] = total
                x = 1 if at_end and b >= N else 0
                send(wgo.at[b], wgd.at[x, c], dsend.at[b], drecv.at[x, c], dev(*goal(b)), far(same(*goal(b))))

                @pl.when(same(*goal(b)))
                def _():
                    wgd[x, c] = wgo[b]

        def prep(t):
            inside = [k for k, (at, n) in enumerate(chunks) if at // TILE == t]
            HB = chunks[inside[0]][1]
            two = TILE // HB

            def one(i, _):
                rows = pl.ds(pl.multiple_of(i * TILE, TILE), TILE)
                for m in range(C // two):
                    got = []
                    for j in range(two):
                        v = slot_ref[0, ((two * m + j) * T + t) * in_tiles + i]
                        tile = tiles[lax.rem(v, slots)]
                        got.append(jnp.where(v < slots, tile, jnp.zeros_like(tile)))
                    for h, k in enumerate(inside):
                        mix = jnp.concatenate([x[h * HB:(h + 1) * HB] for x in got], axis=0)
                        hi, lo = split(mix.T)
                        base = C * chunks[k][0] + m * TILE
                        at_hi[rows, base:base + TILE] = hi
                        at_lo[rows, base:base + TILE] = lo
                return 0

            lax.fori_loop(0, in_tiles, one, 0, unroll=4)

        c_x = c + 1 - 2 * (c % 2)
        c_y = (c + 2) % C
        c_d = (c_x + 2) % C

        def gather_g(k):
            blk = G.at[c, rows_of(k)]
            send(blk, blk, csend.at[k, 0], crecv.at[k, 0], dev(r, c_x, z))
            send(blk, blk, csend.at[k, 1], crecv.at[k, 1], dev(r, c_y, z))
            if k not in relays:
                send(blk, blk, csend.at[k, 2], crecv.at[k, 2], dev(r, c_d, z))

        def relay(k):
            at, n = chunks[k]
            first, second = pl.ds(at, n // 2), pl.ds(at + n // 2, n // 2)
            recv(G.at[c_x, rows_of(k)], csend.at[k, 0], crecv.at[k, 0])
            blk = G.at[c_x, first]
            send(blk, blk, csend.at[k, 2], crecv.at[k, 2], dev(r, c_y, z))
            recv(G.at[c_y, rows_of(k)], csend.at[k, 1], crecv.at[k, 1])
            blk = G.at[c_y, second]
            send(blk, blk, csend.at[k, 3], crecv.at[k, 3], dev(r, c_x, z))

        def consume(k, last=False):
            at, n = chunks[k]
            if k in relays:
                recv(G.at[c_d, pl.ds(at, n // 2)], csend.at[k, 2], crecv.at[k, 2])
                recv(G.at[c_d, pl.ds(at + n // 2, n // 2)], csend.at[k, 3], crecv.at[k, 3])
            else:
                for j, o in enumerate((c_x, c_y, c_d)):
                    recv(G.at[o, rows_of(k)], csend.at[k, j], crecv.at[k, j])
            cols = slice(C * at, C * (at + n))
            g = split(G[:, at:at + n, :].reshape(C * n, D))
            step = IN // 4

            def block(rows):
                add = cat_nn((at_hi[rows, cols], at_lo[rows, cols]), g)
                if k == 0:
                    ig_ref[rows, :] = add
                else:
                    ig_ref[rows, :] += add

            for i in range(4):
                rows = pl.ds(i * step, step)
                block(rows)
                if last:
                    pltpu.make_async_copy(ig_ref.at[rows], ig_hbm.at[rows], igsem.at[i]).start()
                    send(ig_ref.at[rows], igr.at[rows], irsend.at[i], irrecv.at[i], dev(1 - r, c, z))

        def own_cols(o):
            return pl.ds(pl.multiple_of(o * D, D), D)

        def end_cols(o):
            return pl.ds(pl.multiple_of((o - one_if(low)) * D, D), D)

        def times_w(os, rows, hi_w, lo_w, col_of):
            left, right = [], []
            for o in os:
                hi, lo = split(M[o, rows, :])
                cols = col_of(o)
                wh = hi_w[:, cols]
                left += [hi, lo, hi]
                right += [wh, wh, lo_w[:, cols]]
            return nt(jnp.concatenate(left, axis=1), jnp.concatenate(right, axis=1))

        whole = pl.ds(0, H)

        def partial_own():
            part[...] = times_w([e1], whole, we_hi, we_lo, end_cols)

        def partial(k):
            rows = rows_of(k)
            part[rows, :] += times_w([o1, o0], rows, we_hi, we_lo, end_cols)
            pc = part.at[rows]
            send(pc, pc, psend.at[k], precv.at[k], dev(r, c, z_out))

        def agg_own():
            G[c] = times_w([z], whole, w_hi, w_lo, own_cols)

        def agg_inner(k):
            rows = rows_of(k)
            G[c, rows, :] += times_w([e0, o1, o0], rows, w_hi, w_lo, own_cols)
            gather_g(k)

        def agg_end(k):
            rows = rows_of(k)
            if k in raws:
                for o in (e1, o1, o0):
                    zwait(o, k)
                G[c, rows, :] += times_w([e1, o1, o0], rows, w_hi, w_lo, own_cols)
            else:
                recv(part.at[rows], psend.at[k], precv.at[k])
                G[c, rows, :] += part[rows, :]
            gather_g(k)

        def end_weights(stage):
            if stage == 0:
                recv(we_f.at[p], wesend.at[0], werecv.at[0])
                for j in range(1, C):
                    send(we_f.at[p], we_f.at[p], wesend.at[j], werecv.at[j], dev(r, (c + j) % C, z))
            elif stage == 1:
                for j in range(1, C):
                    recv(we_f.at[r * C + (c + C - j) % C], wesend.at[j], werecv.at[j])
                mine = pl.ds(r * C, C)
                send(we_f.at[mine], we_f.at[mine], wesend.at[C], werecv.at[C], dev(1 - r, c, z))
            else:
                recv(we_f.at[pl.ds((1 - r) * C, C)], wesend.at[C], werecv.at[C])
                for i in range(R * C):
                    rows = slice(i * sub, (i + 1) * sub)
                    we_hi[rows, :], we_lo[rows, :] = split(we_f[i])

        def split_w():
            for n in range(N):
                cols = slice(n * D, (n + 1) * D)
                w_hi[:, cols], w_lo[:, cols] = split(w_f[:, cols])

        def finish_all():
            for j in range(C):
                pl.when(far(same(my_r, j, my_z)))(lambda: recv(wgd.at[0, j], dsend.at[0], drecv.at[0, j]))
                rows = slice(j * sub, (j + 1) * sub)
                wg_ref[rows, :] = wgd[0, j]

                @pl.when(my_far)
                def _():
                    recv(wgd.at[1, j], dsend.at[0], drecv.at[1, j])
                    wg_ref[rows, :] += wgd[1, j]

            for i in range(4):
                rows = pl.ds(i * (IN // 4), IN // 4)
                recv(igr.at[rows], irsend.at[i], irrecv.at[i])
                pltpu.make_async_copy(ig_ref.at[rows], ig_hbm.at[rows], igsem.at[i]).wait()
            for cond, make in pending:
                if cond is None:
                    make().wait_send()
                else:
                    pl.when(cond)(lambda: make().wait_send())

        if at_end:
            zpass(z, 0)
            cp_w.wait()
            weights_pass()
            zpass(z, 1)
            cp_sa.wait()
            wgrad_own()
            zpass(z, 2)
            red_row(0)
            split_w()
            cp_t.wait()
            cp_s.wait()
            prep(1)
            red_col(0)
            zpass(z, 3)
            prep(0)
            zpass(z, 5)
            zpass(z, 4)
            agg_own()
            sa_pass(1)
            agg_end(0)
            agg_end(1)
            sa_pass(2)
            prep(3)
            wgrad_ends(0, True)
            sa_pass(3)
            red_out(0)
            red_row(3)
            relay(0)
            relay(1)
            red_col(3)
            consume(0)
            agg_end(2)
            consume(1)
            agg_end(3)
            agg_end(5)
            agg_end(4)
            relay(3)
            prep(2)
            red_out(3)
            relay(2)
            relay(4)
            relay(5)
            consume(3)
            consume(2)
            consume(4)
            consume(5, True)
        else:
            zpass(z, 1)
            zpass(z, 0)
            zout(z, 1)
            zpass(z, 2)
            cp_t.wait()
            cp_s.wait()
            prep(1)
            zout(z, 0)
            cp_sa.wait()
            wgrad_own()
            onward(0)
            arrive(o1, 0)
            cp_w.wait()
            split_w()
            end_weights(0)
            arrive(o1, 1)
            agg_own()
            onward(1)
            red_row(0)
            zpass(z, 5)
            prep(0)
            arrive(o0, 0)
            agg_inner(0)
            onward(2)
            arrive(o0, 1)
            red_col(0)
            agg_inner(1)
            zpass(z, 3)
            end_weights(1)
            onward(3)
            wgrad_mine(0, (1, 2, 3))
            relay(0)
            arrive(o1, 2)
            wgrad_mine(2, (1,))
            arrive(o0, 2)
            agg_inner(2)
            end_weights(2)
            zpass(z, 4)
            onward(4)
            partial_own()
            onward(5)
            relay(1)
            partial(2)
            wgrad_mine(3, (1,))
            wgrad_mine(1, (1,))
            red_row(1)
            red_out(0)
            arrive(o1, 3)
            red_col(1)
            relay(2)
            arrive(o0, 3)
            agg_inner(3)
            partial(3)
            wgrad_mine(2, (2, 3))
            wgrad_ends(1, True)
            arrive(o1, 5)
            arrive(o1, 4)
            wgrad_mine(1, (2, 3))
            arrive(o0, 4)
            wgrad_ends(2, False)
            agg_inner(4)
            arrive(o0, 5)
            wgrad_ends(3, False)
            red_row(3)
            wgrad_mine(3, (2, 3))
            agg_inner(5)
            partial(5)
            red_out(1)
            red_col(3)
            partial(4)
            red_row(2)
            prep(3)
            consume(0)
            consume(1)
            red_col(2)
            relay(4)
            relay(3)
            consume(2)
            red_out(3)
            prep(2)
            relay(5)
            red_out(2)
            consume(4)
            consume(3)
            consume(5, True)
        finish_all()

    pl.when(end)(lambda: program(True))
    pl.when(inner)(lambda: program(False))


def on_line(R, C, N, grad_out, relu_mask, saved_agg, weight, tile_vals, tile_pos, tile_count):
    H, D = grad_out.shape
    F = weight.shape[1]
    tiles = tile_vals[0, 0]
    slots = tiles.shape[0]
    IN = slots * TILE * TILE // (C * H)
    T = H // TILE
    chunks = [(t * TILE + h * (TILE // n), TILE // n) for t, n in enumerate(CUTS) for h in range(n)]
    K = len(chunks)
    blk = F // (R * C)
    sub = D // (R * C)
    nb = 2 * N - 1
    vmem = pl.BlockSpec(memory_space=pltpu.VMEM)
    hbm = pl.BlockSpec(memory_space=pl.ANY)
    dma = pltpu.SemaphoreType.DMA
    wg, ig, igr = pl.pallas_call(
        functools.partial(line_kernel, R, C, N, chunks, (0, 1), (0, 1, 2, 3, 4, 5), (0, 1, 2, 3, 4, 5)),
        out_shape=(
            jax.ShapeDtypeStruct((blk, D), F32),
            jax.ShapeDtypeStruct((IN, D), F32),
            jax.ShapeDtypeStruct((IN, D), F32),
        ),
        in_specs=[pl.BlockSpec(memory_space=pltpu.SMEM), vmem, hbm, hbm, hbm, hbm, hbm],
        out_specs=(vmem, hbm, hbm),
        scratch_shapes=[
            pltpu.VMEM((IN, D), F32),
            pltpu.VMEM((1, slots), jnp.int32),
            pltpu.SMEM((1, slots), jnp.int32),
            pltpu.VMEM((H, D), jnp.int32),
            pltpu.VMEM((N, H, D), F32),
            pltpu.VMEM((C, H, D), F32),
            pltpu.VMEM((slots, TILE, TILE), F32),
            pltpu.VMEM((IN, C * H), BF16),
            pltpu.VMEM((IN, C * H), BF16),
            pltpu.VMEM((D, F), F32),
            pltpu.VMEM((D, F), BF16),
            pltpu.VMEM((D, F), BF16),
            pltpu.VMEM((H, D), F32),
            pltpu.VMEM((R * C, sub, (N - 1) * D), F32),
            pltpu.VMEM((D, (N - 1) * D), BF16),
            pltpu.VMEM((D, (N - 1) * D), BF16),
            pltpu.VMEM((T, TILE, D), F32),
            pltpu.VMEM((H, D), F32),
            pltpu.VMEM((nb, R, D // R, D), F32),
            pltpu.VMEM((nb, D // R, D), F32),
            pltpu.VMEM((C, nb, sub, D), F32),
            pltpu.VMEM((C, nb, sub, D), F32),
            pltpu.VMEM((nb, sub, D), F32),
            pltpu.VMEM((2, C, sub, D), F32),
            dma((6,)),
            dma((2, N, K)), dma((N, K)),
            dma((C + 1,)), dma((C + 1,)),
            dma((T,)), dma((T,)),
            dma((K,)), dma((K,)),
            dma((K, C)), dma((K, C)),
            dma((4,)), dma((4,)),
            dma((4, C)), dma((4, C)),
            dma((nb,)), dma((2, C)),
            dma((4,)), dma((4,)), dma((4,)),
        ],
        compiler_params=pltpu.CompilerParams(
            collective_id=0, has_side_effects=True, vmem_limit_bytes=60 * 1024 * 1024
        ),
    )(tile_count, tile_pos[0], grad_out, relu_mask, saved_agg, weight, tiles)

    def finish(wg_in, a, b, wg_out, ig_out):
        wg_out[...] = wg_in[...]
        ig_out[...] = a[...] + b[...]

    return pl.pallas_call(
        finish,
        out_shape=(jax.ShapeDtypeStruct((blk, D), F32), jax.ShapeDtypeStruct((IN, D), F32)),
        in_specs=[vmem, vmem, vmem],
        out_specs=(vmem, vmem),
    )(wg, ig, igr)


CUTS = (2, 1, 1, 2)


def per_device(R, C, N, grad_out, *rest):
    H, D = grad_out.shape
    line = R == 2 and C == 4 and N == 4 and D % (8 * R * C) == 0
    line = line and H == len(CUTS) * TILE and rest[3].shape[2] == TILE
    return (on_line if line else general)(R, C, N, grad_out, *rest)


def solution(mesh):
    in_specs = (
        P(("row", "col"), "ch"),
        P(("row", "col"), "ch"),
        P(("row", "col"), "ch"),
        P("ch", None),
        P("row", "col", None, None, None),
        P("row", "col", None),
        P("row", "col"),
    )
    out_specs = (P(("row", "col"), "ch"), P("col", "ch"))
    R, C, N = mesh.shape["row"], mesh.shape["col"], mesh.shape["ch"]
    return jax.shard_map(
        functools.partial(per_device, R, C, N), mesh=mesh, in_specs=in_specs, out_specs=out_specs, check_vma=False
    )
```

```python
import functools

import jax
import jax.numpy as jnp
from jax import lax
from jax.experimental import pallas as pl
from jax.experimental.pallas import tpu as pltpu
from jax.sharding import PartitionSpec as P

TILE = 128
MESH = pl.DeviceIdType.MESH
F32 = jnp.float32
BF16 = jnp.bfloat16


def split(x):
    hi = x.astype(BF16)
    return hi, (x - hi.astype(F32)).astype(BF16)


def nn(a, b):
    return lax.dot_general(a, b, (((1,), (0,)), ((), ())), preferred_element_type=F32)


def nt(a, b):
    return lax.dot_general(a, b, (((1,), (1,)), ((), ())), preferred_element_type=F32)


def kernel(
    R, C, N, K,
    slot_ref, g_ref, mask_ref, sa_hbm, w_hbm, tiles_hbm,
    wg_ref, ig_ref, igr,
    M, G, tiles, at_hi, at_lo, w_f, w_hi, w_lo, sa, g_hi, g_lo,
    wgp, wgr, wgs, wgc, wgo,
    local_sem, zsend, zrecv, csend, crecv, wrsend, wrrecv, wcsend, wcrecv, wfsend, wfrecv,
    irsend, irrecv, iasend, iarecv,
):
    r, c, z = lax.axis_index("row"), lax.axis_index("col"), lax.axis_index("ch")
    HB, D = M.shape[2], M.shape[3]
    RC = R * C
    per = RC // N
    blk = wgp.shape[1]
    slots = tiles.shape[0]
    acc = ig_ref
    IN = acc.shape[0]
    in_tiles = IN // TILE
    tpb = HB // TILE
    piece = IN // R

    cp_w = pltpu.make_async_copy(w_hbm, w_f, local_sem.at[0])
    cp_sa = pltpu.make_async_copy(sa_hbm, sa, local_sem.at[1])
    cp_t = pltpu.make_async_copy(tiles_hbm, tiles, local_sem.at[2])
    cp_w.start()
    cp_sa.start()
    cp_t.start()

    def dev(r_, c_, z_):
        return {"row": r_, "col": c_, "ch": z_}

    q = r * C + c
    d_idx = z * per + q // N
    d_r, d_c, d_z = d_idx // C, d_idx % C, q % N
    s_q = (q % per) * N + z
    s_r, s_c, s_z = s_q // C, s_q % C, q // per
    away = jnp.logical_not((d_r == r) & (d_c == c) & (d_z == z))

    barrier = pltpu.get_barrier_semaphore()

    def hello(r_, c_, z_):
        pl.semaphore_signal(barrier, inc=1, device_id=dev(r_, c_, z_), device_id_type=MESH)

    for j in range(1, R):
        hello((r + j) % R, c, z)
    for j in range(1, C):
        hello(r, (c + j) % C, z)

    @pl.when(z > 0)
    def _():
        hello(r, c, z - 1)

    @pl.when(z < N - 1)
    def _():
        hello(r, c, z + 1)

    @pl.when(away)
    def _():
        hello(d_r, d_c, d_z)
        hello(s_r, s_c, s_z)

    def own(k):
        rows = pl.ds(pl.multiple_of(k * HB, HB), HB)
        M[z, k] = g_ref[rows, :] * mask_ref[rows, :].astype(F32)

    own(0)
    own(1)
    one_if = lambda cond: jnp.where(cond, 1, 0)
    greeted = R - 1 + C - 1 + one_if(z > 0) + one_if(z < N - 1) + 2 * one_if(away)
    pl.semaphore_wait(barrier, greeted)

    def zcopy(origin, k, step):
        way = 0 if step < 0 else 1
        return pltpu.make_async_remote_copy(
            src_ref=M.at[origin, k], dst_ref=M.at[origin, k],
            send_sem=zsend.at[way, origin, k], recv_sem=zrecv.at[origin, k],
            device_id=dev(r, c, z + step), device_id_type=MESH,
        )

    def own_send(k):
        @pl.when(z > 0)
        def _():
            zcopy(z, k, -1).start()

        @pl.when(z < N - 1)
        def _():
            zcopy(z, k, 1).start()

    own_send(0)
    own_send(1)
    acc[...] = jnp.zeros_like(acc)
    wgp[...] = jnp.zeros_like(wgp)
    cp_w.wait()
    for n in range(N):
        cols = slice(n * D, (n + 1) * D)
        w_hi[:, cols], w_lo[:, cols] = split(w_f[:, cols])
    cp_sa.wait()
    cp_t.wait()

    def prep(k, cc):
        for t in range(tpb):
            def one(i, _):
                p = ((cc * K + k) * tpb + t) * in_tiles + i
                v = slot_ref[p]
                tile = tiles[lax.rem(v, slots)]
                tile = jnp.where(v < slots, tile, jnp.zeros_like(tile))
                hi, lo = split(tile.T)
                rows = pl.ds(pl.multiple_of(i * TILE, TILE), TILE)
                cols = slice(cc * HB + t * TILE, cc * HB + (t + 1) * TILE)
                at_hi[k, rows, cols] = hi
                at_lo[k, rows, cols] = lo
                return 0

            lax.fori_loop(0, in_tiles, one, 0, unroll=2)

    def ccopy(k, j):
        return pltpu.make_async_remote_copy(
            src_ref=G.at[k, c], dst_ref=G.at[k, c],
            send_sem=csend.at[k, j], recv_sem=crecv.at[k, j],
            device_id=dev(r, (c + j) % C, z), device_id_type=MESH,
        )

    def cwait(k, j):
        o = (c + C - j) % C
        return pltpu.make_async_remote_copy(
            src_ref=G.at[k, o], dst_ref=G.at[k, o],
            send_sem=csend.at[k, j], recv_sem=crecv.at[k, j],
            device_id=dev(r, (c + j) % C, z), device_id_type=MESH,
        )

    def consume(k):
        for j in range(1, C):
            cwait(k, j).wait_recv()
        for n in range(C):
            rows = slice(n * HB, (n + 1) * HB)
            g_hi[rows, :], g_lo[rows, :] = split(G[k, n])

        def part(i, _):
            rows = pl.ds(pl.multiple_of(i * 256, 256), 256)
            a = at_hi[k, rows, :]
            acc[rows, :] += nn(a, g_hi[...]) + nn(a, g_lo[...]) + nn(at_lo[k, rows, :], g_hi[...])
            return 0

        lax.fori_loop(0, IN // 256, part, 0)

    def wrcopy(j):
        t = (r + j) % R
        return pltpu.make_async_remote_copy(
            src_ref=wgp.at[pl.ds(t * C, C)], dst_ref=wgr.at[j],
            send_sem=wrsend.at[j], recv_sem=wrrecv.at[j],
            device_id=dev(t, c, z), device_id_type=MESH,
        )

    groups = [[] for _ in range(N - 1)]
    for cc in range(C):
        groups[cc * max(N - 2, 1) // C].append(cc)

    def body(k, _):
        for d in range(1, N):
            @pl.when(z >= d)
            def _():
                zcopy(z - d, k, 1).wait_recv()

                @pl.when(z < N - 1)
                def _():
                    zcopy(z - d, k, 1).start()

            @pl.when(z + d < N)
            def _():
                zcopy(z + d, k, -1).wait_recv()

                @pl.when(z > 0)
                def _():
                    zcopy(z + d, k, -1).start()

            if d == 1:
                @pl.when(k + 2 < K)
                def _():
                    own(k + 2)
                    own_send(k + 2)

            for cc in groups[d - 1]:
                prep(k, cc)

        agg = jnp.zeros((HB, D), F32)
        for n in range(N):
            cols = slice(n * D, (n + 1) * D)
            hi, lo = split(M[n, k])
            agg += nt(hi, w_hi[:, cols]) + nt(lo, w_hi[:, cols]) + nt(hi, w_lo[:, cols])
        G[k, c] = agg
        for j in range(1, C):
            ccopy(k, j).start()

        rows = pl.ds(pl.multiple_of(k * HB, HB), HB)
        s_hi, s_lo = split(sa[rows, :].T)
        for n in range(N):
            hi, lo = split(M[n, k])
            res = nn(s_hi, hi) + nn(s_hi, lo) + nn(s_lo, hi)
            for h in range(per):
                wgp[h * N + n] += res[h * blk:(h + 1) * blk, :]

        @pl.when(k == K - 1)
        def _():
            for j in range(1, R):
                wrcopy(j).start()

        @pl.when(k > 0)
        def _():
            consume(k - 1)

        return 0

    lax.fori_loop(0, K, body, 0)

    def wccopy(j):
        t = (c + j) % C
        return pltpu.make_async_remote_copy(
            src_ref=wgs.at[t], dst_ref=wgc.at[j],
            send_sem=wcsend.at[j], recv_sem=wcrecv.at[j],
            device_id=dev(r, t, z), device_id_type=MESH,
        )

    wfcopy = pltpu.make_async_remote_copy(
        src_ref=wgo, dst_ref=wg_ref, send_sem=wfsend, recv_sem=wfrecv,
        device_id=dev(d_r, d_c, d_z), device_id_type=MESH,
    )

    def ircopy(j):
        t = (r + j) % R
        whole = R == 2
        rows = pl.ds(0, IN) if whole else pl.ds(pl.multiple_of(t * piece, piece), piece)
        return pltpu.make_async_remote_copy(
            src_ref=acc.at[rows], dst_ref=igr if whole else igr.at[j],
            send_sem=irsend.at[j], recv_sem=irrecv.at[j],
            device_id=dev(t, c, z), device_id_type=MESH,
        )

    mine = pl.ds(pl.multiple_of(r * piece, piece), piece)

    def iacopy(j):
        return pltpu.make_async_remote_copy(
            src_ref=ig_ref.at[mine], dst_ref=ig_ref.at[mine],
            send_sem=iasend.at[j], recv_sem=iarecv.at[j],
            device_id=dev((r + j) % R, c, z), device_id_type=MESH,
        )

    def iawait(j):
        theirs = pl.ds(pl.multiple_of(((r + R - j) % R) * piece, piece), piece)
        return pltpu.make_async_remote_copy(
            src_ref=ig_ref.at[theirs], dst_ref=ig_ref.at[theirs],
            send_sem=iasend.at[j], recv_sem=iarecv.at[j],
            device_id=dev((r + j) % R, c, z), device_id_type=MESH,
        )

    for j in range(1, R):
        wrcopy(j).wait_recv()
    total = wgp[pl.ds(r * C, C)]
    for j in range(1, R):
        total += wgr[j]
    wgs[...] = total
    for j in range(1, C):
        wccopy(j).start()

    consume(K - 1)
    for j in range(1, R):
        ircopy(j).start()
    for j in range(1, C):
        wccopy(j).wait_recv()
    wpart = wgs[c]
    for j in range(1, C):
        wpart += wgc[j]

    @pl.when(away)
    def _():
        wgo[...] = wpart
        wfcopy.start()
        wfcopy.wait()

    @pl.when(jnp.logical_not(away))
    def _():
        wg_ref[...] = wpart

    for j in range(1, R):
        ircopy(j).wait_recv()
    if R > 2:
        summed = acc[mine, :]
        for j in range(1, R):
            summed += igr[j]
        ig_ref[mine, :] = summed
        for j in range(1, R):
            iacopy(j).start()
        for j in range(1, R):
            iawait(j).wait_recv()

    for j in range(1, R):
        wrcopy(j).wait_send()
        ircopy(j).wait_send()
        if R > 2:
            iacopy(j).wait_send()
    for j in range(1, C):
        wccopy(j).wait_send()

    def drain(k, _):
        for j in range(1, C):
            ccopy(k, j).wait_send()
        for n in range(N):
            @pl.when((z > 0) & (z <= n))
            def _():
                zcopy(n, k, -1).wait_send()

            @pl.when((z < N - 1) & (z >= n))
            def _():
                zcopy(n, k, 1).wait_send()

        return 0

    lax.fori_loop(0, K, drain, 0)


def general(R, C, N, grad_out, relu_mask, saved_agg, weight, tile_vals, tile_pos, tile_count):
    H, D = grad_out.shape
    F = weight.shape[1]
    tiles = tile_vals[0, 0]
    slots = tiles.shape[0]
    out_rows = C * H
    IN = slots * TILE * TILE // out_rows
    HB = TILE
    K = H // HB
    blk = F // (R * C)
    s = jnp.arange(slots, dtype=jnp.int32)
    code = jnp.where(s < tile_count[0, 0], s, s + slots)
    where = jnp.sum(jnp.where(tile_pos[0, 0][None, :] == s[:, None], code[None, :], 0), axis=1).astype(jnp.int32)
    vmem = pl.BlockSpec(memory_space=pltpu.VMEM)
    hbm = pl.BlockSpec(memory_space=pl.ANY)
    dma = pltpu.SemaphoreType.DMA
    igr_shape = (IN, D) if R == 2 else (R, IN // R, D)
    wg, ig, igr = pl.pallas_call(
        functools.partial(kernel, R, C, N, K),
        out_shape=(
            jax.ShapeDtypeStruct((blk, D), F32),
            jax.ShapeDtypeStruct((IN, D), F32),
            jax.ShapeDtypeStruct(igr_shape, F32),
        ),
        in_specs=[pl.BlockSpec(memory_space=pltpu.SMEM), vmem, vmem, hbm, hbm, hbm],
        out_specs=(vmem, vmem, vmem),
        scratch_shapes=[
            pltpu.VMEM((N, K, HB, D), F32),
            pltpu.VMEM((K, C, HB, D), F32),
            pltpu.VMEM((slots, TILE, TILE), F32),
            pltpu.VMEM((K, IN, C * HB), BF16),
            pltpu.VMEM((K, IN, C * HB), BF16),
            pltpu.VMEM((D, F), F32),
            pltpu.VMEM((D, F), BF16),
            pltpu.VMEM((D, F), BF16),
            pltpu.VMEM((H, D), F32),
            pltpu.VMEM((C * HB, D), BF16),
            pltpu.VMEM((C * HB, D), BF16),
            pltpu.VMEM((R * C, blk, D), F32),
            pltpu.VMEM((R, C, blk, D), F32),
            pltpu.VMEM((C, blk, D), F32),
            pltpu.VMEM((C, blk, D), F32),
            pltpu.VMEM((blk, D), F32),
            dma((3,)),
            dma((2, N, K)), dma((N, K)),
            dma((K, C)), dma((K, C)),
            dma((R,)), dma((R,)),
            dma((C,)), dma((C,)),
            dma, dma,
            dma((R,)), dma((R,)),
            dma((R,)), dma((R,)),
        ],
        compiler_params=pltpu.CompilerParams(
            collective_id=0, has_side_effects=True, vmem_limit_bytes=60 * 1024 * 1024
        ),
    )(where, grad_out, relu_mask, saved_agg, weight, tiles)

    def finish(wg_in, a, b, wg_out, ig_out):
        wg_out[...] = wg_in[...]
        ig_out[...] = a[...] + b[...] if R == 2 else a[...]

    return pl.pallas_call(
        finish,
        out_shape=(jax.ShapeDtypeStruct((blk, D), F32), jax.ShapeDtypeStruct((IN, D), F32)),
        in_specs=[vmem, vmem, vmem if R == 2 else hbm],
        out_specs=(vmem, vmem),
    )(wg, ig, igr)


def cat_nn(a, b):
    return nn(jnp.concatenate([a[0], a[0], a[1]], axis=1), jnp.concatenate([b[0], b[1], b[0]], axis=0))


def line_kernel(
    R, C, N, chunks, raws, relays_end, relays_inner,
    count_ref, pos_ref, g_hbm, mask_hbm, sa_hbm, w_hbm, tiles_hbm,
    wg_ref, ig_hbm, igr,
    ig_ref, slot_vec, slot_ref, mask, M, G, tiles, at_hi, at_lo, w_f, w_hi, w_lo, sa,
    we_f, we_hi, we_lo, sae, part, wgp, wgr, wgs, wgc, wgo, wgd,
    local_sem, zsend, zrecv, wesend, werecv, sasend, sarecv, psend, precv,
    csend, crecv, rsend, rrecv, tsend, trecv, dsend, drecv, irsend, irrecv, igsem,
):
    r, c, z = lax.axis_index("row"), lax.axis_index("col"), lax.axis_index("ch")
    H, D = M.shape[1], M.shape[2]
    T, K = H // TILE, len(chunks)
    per = R * C // N
    sub = wgo.shape[1]
    slots = tiles.shape[0]
    IN = ig_ref.shape[0]
    in_tiles = IN // TILE
    wide = (N - 1) * D
    nb = 2 * N - 1

    low = z < N // 2
    end = (z == 0) | (z == N - 1)
    inner = jnp.logical_not(end)
    z_in = jnp.where(low, z + 1, z - 1)
    z_out = jnp.where(low, z - 1, z + 1)
    e0 = jnp.where(low, 0, N - 1)
    e1 = jnp.where(low, 1, N - 2)
    o1 = jnp.where(low, 2, N - 3)
    o0 = jnp.where(low, N - 1, 0)
    p = r * C + c

    cp_g = pltpu.make_async_copy(g_hbm, M.at[z], local_sem.at[3])
    cp_m = pltpu.make_async_copy(mask_hbm, mask, local_sem.at[4])
    cp_s = pltpu.make_async_copy(slot_vec, slot_ref, local_sem.at[5])
    cp_w = pltpu.make_async_copy(w_hbm, w_f, local_sem.at[0])
    cp_sa = pltpu.make_async_copy(sa_hbm, sa, local_sem.at[1])
    cp_t = pltpu.make_async_copy(tiles_hbm, tiles, local_sem.at[2])

    def dev(r_, c_, z_):
        return {"row": r_, "col": c_, "ch": z_}

    one_if = lambda cond: jnp.where(cond, 1, 0)
    same = lambda r_, c_, z_: (r_ == r) & (c_ == c) & (z_ == z)
    far = jnp.logical_not

    own_q = per * z + r
    end_q = per * e0 + r
    block_n = [z, e0, o1, o0, e1, o1, o0]
    block_q = [own_q] * N + [end_q] * (N - 1)

    def goal(b):
        return block_q[b] // C, block_q[b] % C, block_n[b]

    my_a, my_r = p // per, p % per
    my_z = jnp.where(my_a == z, z, jnp.where(my_a == 0, 1, jnp.where(my_a == N - 1, N - 2, my_a)))

    my_far = ((my_a == 0) | (my_a == N - 1)) & (my_a != z)

    barrier = pltpu.get_barrier_semaphore()

    def hello(r_, c_, z_):
        pl.semaphore_signal(barrier, inc=1, device_id=dev(r_, c_, z_), device_id_type=MESH)

    hello(1 - r, c, z)
    for j in range(1, C):
        hello(r, (c + j) % C, z)
    hello(r, c, z_in)
    pl.when(inner)(lambda: hello(r, c, z_out))
    for j in range(C):
        pl.when(far(same(my_r, j, my_z)))(lambda: hello(my_r, j, my_z))
        pl.when(my_far)(lambda: hello(my_r, j, my_a))
    greeted = R - 1 + C - 1 + 1 + one_if(inner) + (N - 1) * one_if(end) + one_if(far(same(*goal(0))))
    for b in range(1, nb):
        greeted += one_if(inner & far(same(*goal(b))))

    for copy in (cp_g, cp_m, cp_w, cp_sa, cp_t):
        copy.start()

    def rows_of(k):
        return pl.ds(*chunks[k])

    square = (slots, slots)
    slot, place = lax.broadcasted_iota(jnp.int32, square, 0), lax.broadcasted_iota(jnp.int32, square, 1)
    code = jnp.where(slot < count_ref[0, 0], slot, slot + slots)
    hit = jnp.broadcast_to(pos_ref[...], square).T == place
    slot_vec[...] = jnp.sum(jnp.where(hit, code, 0), axis=0, keepdims=True)
    cp_s.start()
    cp_g.wait()
    cp_m.wait()
    for k in range(K):
        rows = rows_of(k)
        M[z, rows, :] = M[z, rows, :] * mask[rows, :].astype(F32)
    pl.semaphore_wait(barrier, greeted)

    def program(at_end):
        relays = relays_end if at_end else relays_inner
        pending = []

        def send(src, dst, ss, rs, to, cond=None):
            def make():
                return pltpu.make_async_remote_copy(
                    src_ref=src, dst_ref=dst, send_sem=ss, recv_sem=rs, device_id=to, device_id_type=MESH
                )

            pending.append((cond, make))
            if cond is None:
                make().start()
            else:
                pl.when(cond)(lambda: make().start())

        def recv(dst, ss, rs):
            pltpu.make_async_remote_copy(
                src_ref=dst, dst_ref=dst, send_sem=ss, recv_sem=rs, device_id=dev(1 - r, c, z), device_id_type=MESH
            ).wait_recv()

        def zpass(o, k):
            blk = M.at[o, rows_of(k)]
            send(blk, blk, zsend.at[0, o, k], zrecv.at[o, k], dev(r, c, z_in))

        def zout(o, k):
            if k in raws:
                blk = M.at[o, rows_of(k)]
                send(blk, blk, zsend.at[1, o, k], zrecv.at[o, k], dev(r, c, z_out))

        def zwait(o, k):
            recv(M.at[o, rows_of(k)], zsend.at[0, o, k], zrecv.at[o, k])

        def onward(k):
            zwait(e0, k)
            zpass(e0, k)

        def arrive(o, k):
            zwait(o, k)
            zout(o, k)

        def weights_pass():
            cols = pl.ds(pl.multiple_of(jnp.where(low, D, 0), D), wide)
            rows = pl.ds(pl.multiple_of(p * sub, sub), sub)
            send(w_f.at[rows, cols], we_f.at[p], wesend.at[0], werecv.at[0], dev(r, c, z_in))

        def sa_pass(t):
            send(sa.at[pl.ds(t * TILE, TILE)], sae.at[t], sasend.at[t], sarecv.at[t], dev(r, c, z_in))

        def outer(s, m):
            return cat_nn(s, split(m))

        def wadd(b, value, first):
            value = value.reshape(R, D // R, D)
            if first:
                wgp[b] = value
            else:
                wgp[b] += value

        def sa_own(t):
            return split(sa[t * TILE:(t + 1) * TILE, :].T)

        def tile_rows(o, t):
            return M[o, t * TILE:(t + 1) * TILE, :]

        def wgrad_own():
            for t in range(T):
                wadd(0, outer(sa_own(t), tile_rows(z, t)), t == 0)

        def wgrad_mine(t, bs):
            s = sa_own(t)
            for b in bs:
                wadd(b, outer(s, tile_rows(block_n[b], t)), t == 0)

        def wgrad_ends(t, first):
            if not at_end:
                recv(sae.at[t], sasend.at[t], sarecv.at[t])
            s = sa_own(t) if at_end else split(sae[t].T)
            for b in range(N, nb):
                wadd(b, outer(s, tile_rows(block_n[b], t)), first)

        groups = ((0, 1), (1, 2), (2, N), (N, nb))

        def red_row(n):
            lo, hi = groups[n]
            bs = pl.ds(lo, hi - lo)
            send(wgp.at[bs, 1 - r], wgr.at[bs], rsend.at[n], rrecv.at[n], dev(1 - r, c, z))

        def red_col(n):
            lo, hi = groups[n]
            bs = pl.ds(lo, hi - lo)
            recv(wgr.at[bs], rsend.at[n], rrecv.at[n])
            for b in range(lo, hi):
                total = wgp[b, r] + wgr[b]
                for t in range(C):
                    wgs[t, b] = total[t * sub:(t + 1) * sub]
            for j in range(1, C):
                t = (c + j) % C
                send(wgs.at[t, bs], wgc.at[j, bs], tsend.at[n, j], trecv.at[n, j], dev(r, t, z))

        def red_out(n):
            lo, hi = groups[n]
            bs = pl.ds(lo, hi - lo)
            for j in range(1, C):
                recv(wgc.at[j, bs], tsend.at[n, j], trecv.at[n, j])
            for b in range(lo, hi):
                total = wgs[c, b]
                for j in range(1, C):
                    total += wgc[j, b]
                wgo[b] = total
                x = 1 if at_end and b >= N else 0
                send(wgo.at[b], wgd.at[x, c], dsend.at[b], drecv.at[x, c], dev(*goal(b)), far(same(*goal(b))))

                @pl.when(same(*goal(b)))
                def _():
                    wgd[x, c] = wgo[b]

        def prep(t):
            inside = [k for k, (at, n) in enumerate(chunks) if at // TILE == t]
            HB = chunks[inside[0]][1]
            two = TILE // HB

            def one(i, _):
                rows = pl.ds(pl.multiple_of(i * TILE, TILE), TILE)
                for m in range(C // two):
                    got = []
                    for j in range(two):
                        v = slot_ref[0, ((two * m + j) * T + t) * in_tiles + i]
                        tile = tiles[lax.rem(v, slots)]
                        got.append(jnp.where(v < slots, tile, jnp.zeros_like(tile)))
                    for h, k in enumerate(inside):
                        mix = jnp.concatenate([x[h * HB:(h + 1) * HB] for x in got], axis=0)
                        hi, lo = split(mix.T)
                        base = C * chunks[k][0] + m * TILE
                        at_hi[rows, base:base + TILE] = hi
                        at_lo[rows, base:base + TILE] = lo
                return 0

            lax.fori_loop(0, in_tiles, one, 0, unroll=4)

        c_x = c + 1 - 2 * (c % 2)
        c_y = (c + 2) % C
        c_d = (c_x + 2) % C

        def gather_g(k):
            blk = G.at[c, rows_of(k)]
            send(blk, blk, csend.at[k, 0], crecv.at[k, 0], dev(r, c_x, z))
            send(blk, blk, csend.at[k, 1], crecv.at[k, 1], dev(r, c_y, z))
            if k not in relays:
                send(blk, blk, csend.at[k, 2], crecv.at[k, 2], dev(r, c_d, z))

        def relay(k):
            at, n = chunks[k]
            first, second = pl.ds(at, n // 2), pl.ds(at + n // 2, n // 2)
            recv(G.at[c_x, rows_of(k)], csend.at[k, 0], crecv.at[k, 0])
            blk = G.at[c_x, first]
            send(blk, blk, csend.at[k, 2], crecv.at[k, 2], dev(r, c_y, z))
            recv(G.at[c_y, rows_of(k)], csend.at[k, 1], crecv.at[k, 1])
            blk = G.at[c_y, second]
            send(blk, blk, csend.at[k, 3], crecv.at[k, 3], dev(r, c_x, z))

        def consume(k, last=False):
            at, n = chunks[k]
            if k in relays:
                recv(G.at[c_d, pl.ds(at, n // 2)], csend.at[k, 2], crecv.at[k, 2])
                recv(G.at[c_d, pl.ds(at + n // 2, n // 2)], csend.at[k, 3], crecv.at[k, 3])
            else:
                for j, o in enumerate((c_x, c_y, c_d)):
                    recv(G.at[o, rows_of(k)], csend.at[k, j], crecv.at[k, j])
            cols = slice(C * at, C * (at + n))
            g = split(G[:, at:at + n, :].reshape(C * n, D))
            step = IN // 4

            def block(rows):
                add = cat_nn((at_hi[rows, cols], at_lo[rows, cols]), g)
                if k == 0:
                    ig_ref[rows, :] = add
                else:
                    ig_ref[rows, :] += add

            for i in range(4):
                rows = pl.ds(i * step, step)
                block(rows)
                if last:
                    pltpu.make_async_copy(ig_ref.at[rows], ig_hbm.at[rows], igsem.at[i]).start()
                    send(ig_ref.at[rows], igr.at[rows], irsend.at[i], irrecv.at[i], dev(1 - r, c, z))

        def own_cols(o):
            return pl.ds(pl.multiple_of(o * D, D), D)

        def end_cols(o):
            return pl.ds(pl.multiple_of((o - one_if(low)) * D, D), D)

        def times_w(os, rows, hi_w, lo_w, col_of):
            left, right = [], []
            for o in os:
                hi, lo = split(M[o, rows, :])
                cols = col_of(o)
                wh = hi_w[:, cols]
                left += [hi, lo, hi]
                right += [wh, wh, lo_w[:, cols]]
            return nt(jnp.concatenate(left, axis=1), jnp.concatenate(right, axis=1))

        whole = pl.ds(0, H)

        def partial_own():
            part[...] = times_w([e1], whole, we_hi, we_lo, end_cols)

        def partial(k):
            rows = rows_of(k)
            part[rows, :] += times_w([o1, o0], rows, we_hi, we_lo, end_cols)
            pc = part.at[rows]
            send(pc, pc, psend.at[k], precv.at[k], dev(r, c, z_out))

        def agg_own():
            G[c] = times_w([z], whole, w_hi, w_lo, own_cols)

        def agg_inner(k):
            rows = rows_of(k)
            G[c, rows, :] += times_w([e0, o1, o0], rows, w_hi, w_lo, own_cols)
            gather_g(k)

        def agg_end(k):
            rows = rows_of(k)
            if k in raws:
                for o in (e1, o1, o0):
                    zwait(o, k)
                G[c, rows, :] += times_w([e1, o1, o0], rows, w_hi, w_lo, own_cols)
            else:
                recv(part.at[rows], psend.at[k], precv.at[k])
                G[c, rows, :] += part[rows, :]
            gather_g(k)

        def end_weights(stage):
            if stage == 0:
                recv(we_f.at[p], wesend.at[0], werecv.at[0])
                for j in range(1, C):
                    send(we_f.at[p], we_f.at[p], wesend.at[j], werecv.at[j], dev(r, (c + j) % C, z))
            elif stage == 1:
                for j in range(1, C):
                    recv(we_f.at[r * C + (c + C - j) % C], wesend.at[j], werecv.at[j])
                mine = pl.ds(r * C, C)
                send(we_f.at[mine], we_f.at[mine], wesend.at[C], werecv.at[C], dev(1 - r, c, z))
            else:
                recv(we_f.at[pl.ds((1 - r) * C, C)], wesend.at[C], werecv.at[C])
                for i in range(R * C):
                    rows = slice(i * sub, (i + 1) * sub)
                    we_hi[rows, :], we_lo[rows, :] = split(we_f[i])

        def split_w():
            for n in range(N):
                cols = slice(n * D, (n + 1) * D)
                w_hi[:, cols], w_lo[:, cols] = split(w_f[:, cols])

        def finish_all():
            for j in range(C):
                pl.when(far(same(my_r, j, my_z)))(lambda: recv(wgd.at[0, j], dsend.at[0], drecv.at[0, j]))
                rows = slice(j * sub, (j + 1) * sub)
                wg_ref[rows, :] = wgd[0, j]

                @pl.when(my_far)
                def _():
                    recv(wgd.at[1, j], dsend.at[0], drecv.at[1, j])
                    wg_ref[rows, :] += wgd[1, j]

            for i in range(4):
                rows = pl.ds(i * (IN // 4), IN // 4)
                recv(igr.at[rows], irsend.at[i], irrecv.at[i])
                pltpu.make_async_copy(ig_ref.at[rows], ig_hbm.at[rows], igsem.at[i]).wait()
            for cond, make in pending:
                if cond is None:
                    make().wait_send()
                else:
                    pl.when(cond)(lambda: make().wait_send())

        if at_end:
            cp_w.wait()
            weights_pass()
            cp_sa.wait()
            wgrad_own()
            red_row(0)
            split_w()
            zpass(z, 0)
            zpass(z, 1)
            cp_t.wait()
            cp_s.wait()
            prep(0)
            zpass(z, 6)
            zpass(z, 5)
            zpass(z, 2)
            agg_own()
            zpass(z, 7)
            red_col(0)
            zpass(z, 4)
            red_out(0)
            zpass(z, 3)
            prep(3)
            sa_pass(3)
            agg_end(0)
            sa_pass(2)
            agg_end(1)
            wgrad_ends(0, True)
            red_row(3)
            sa_pass(1)
            relay(0)
            agg_end(6)
            red_col(3)
            prep(1)
            agg_end(2)
            agg_end(5)
            relay(1)
            red_out(3)
            agg_end(7)
            agg_end(4)
            consume(0)
            agg_end(3)
            relay(5)
            prep(2)
            relay(6)
            relay(2)
            consume(1)
            relay(4)
            relay(3)
            relay(7)
            consume(5)
            consume(6)
            consume(2)
            consume(4)
            consume(3)
            consume(7, True)
        else:
            zpass(z, 2)
            zpass(z, 1)
            zpass(z, 6)
            cp_t.wait()
            cp_s.wait()
            prep(0)
            zpass(z, 0)
            prep(2)
            zout(z, 0)
            prep(3)
            end_weights(0)
            onward(0)
            cp_w.wait()
            split_w()
            zout(z, 1)
            arrive(o1, 1)
            onward(1)
            cp_sa.wait()
            wgrad_own()
            zpass(z, 5)
            red_row(0)
            arrive(o1, 0)
            prep(1)
            onward(6)
            red_col(0)
            arrive(o0, 0)
            agg_own()
            onward(5)
            zpass(z, 3)
            arrive(o0, 1)
            agg_inner(1)
            agg_inner(0)
            arrive(o1, 6)
            end_weights(1)
            onward(2)
            zpass(z, 4)
            wgrad_mine(0, (1, 2, 3))
            arrive(o0, 6)
            arrive(o1, 5)
            agg_inner(6)
            end_weights(2)
            partial_own()
            onward(7)
            zpass(z, 7)
            arrive(o0, 5)
            onward(4)
            partial(6)
            onward(3)
            relay(1)
            relay(0)
            wgrad_mine(3, (1,))
            wgrad_mine(1, (1,))
            agg_inner(5)
            wgrad_mine(2, (1,))
            arrive(o0, 2)
            relay(6)
            red_row(1)
            arrive(o1, 2)
            agg_inner(2)
            red_col(1)
            partial(2)
            red_out(0)
            arrive(o0, 7)
            arrive(o1, 4)
            partial(5)
            arrive(o1, 3)
            arrive(o1, 7)
            relay(5)
            agg_inner(7)
            wgrad_mine(3, (2, 3))
            partial(7)
            wgrad_ends(3, True)
            arrive(o0, 4)
            wgrad_mine(2, (2, 3))
            agg_inner(4)
            arrive(o0, 3)
            wgrad_mine(1, (2, 3))
            red_row(2)
            agg_inner(3)
            partial(4)
            partial(3)
            wgrad_ends(1, False)
            wgrad_ends(2, False)
            red_col(2)
            red_row(3)
            red_col(3)
            consume(0)
            red_out(2)
            red_out(1)
            consume(6)
            relay(4)
            relay(2)
            relay(3)
            consume(5)
            consume(1)
            relay(7)
            red_out(3)
            consume(4)
            consume(2)
            consume(3)
            consume(7, True)
        finish_all()

    pl.when(end)(lambda: program(True))
    pl.when(inner)(lambda: program(False))


def on_line(R, C, N, grad_out, relu_mask, saved_agg, weight, tile_vals, tile_pos, tile_count):
    H, D = grad_out.shape
    F = weight.shape[1]
    tiles = tile_vals[0, 0]
    slots = tiles.shape[0]
    IN = slots * TILE * TILE // (C * H)
    T = H // TILE
    chunks = [(t * TILE + h * (TILE // n), TILE // n) for t, n in enumerate(CUTS) for h in range(n)]
    K = len(chunks)
    blk = F // (R * C)
    sub = D // (R * C)
    nb = 2 * N - 1
    vmem = pl.BlockSpec(memory_space=pltpu.VMEM)
    hbm = pl.BlockSpec(memory_space=pl.ANY)
    dma = pltpu.SemaphoreType.DMA
    wg, ig, igr = pl.pallas_call(
        functools.partial(line_kernel, R, C, N, chunks, (0, 1), (0, 1, 2, 3, 4, 5, 6, 7), (0, 1, 2, 3, 4, 5, 6, 7)),
        out_shape=(
            jax.ShapeDtypeStruct((blk, D), F32),
            jax.ShapeDtypeStruct((IN, D), F32),
            jax.ShapeDtypeStruct((IN, D), F32),
        ),
        in_specs=[pl.BlockSpec(memory_space=pltpu.SMEM), vmem, hbm, hbm, hbm, hbm, hbm],
        out_specs=(vmem, hbm, hbm),
        scratch_shapes=[
            pltpu.VMEM((IN, D), F32),
            pltpu.VMEM((1, slots), jnp.int32),
            pltpu.SMEM((1, slots), jnp.int32),
            pltpu.VMEM((H, D), jnp.int32),
            pltpu.VMEM((N, H, D), F32),
            pltpu.VMEM((C, H, D), F32),
            pltpu.VMEM((slots, TILE, TILE), F32),
            pltpu.VMEM((IN, C * H), BF16),
            pltpu.VMEM((IN, C * H), BF16),
            pltpu.VMEM((D, F), F32),
            pltpu.VMEM((D, F), BF16),
            pltpu.VMEM((D, F), BF16),
            pltpu.VMEM((H, D), F32),
            pltpu.VMEM((R * C, sub, (N - 1) * D), F32),
            pltpu.VMEM((D, (N - 1) * D), BF16),
            pltpu.VMEM((D, (N - 1) * D), BF16),
            pltpu.VMEM((T, TILE, D), F32),
            pltpu.VMEM((H, D), F32),
            pltpu.VMEM((nb, R, D // R, D), F32),
            pltpu.VMEM((nb, D // R, D), F32),
            pltpu.VMEM((C, nb, sub, D), F32),
            pltpu.VMEM((C, nb, sub, D), F32),
            pltpu.VMEM((nb, sub, D), F32),
            pltpu.VMEM((2, C, sub, D), F32),
            dma((6,)),
            dma((2, N, K)), dma((N, K)),
            dma((C + 1,)), dma((C + 1,)),
            dma((T,)), dma((T,)),
            dma((K,)), dma((K,)),
            dma((K, C)), dma((K, C)),
            dma((4,)), dma((4,)),
            dma((4, C)), dma((4, C)),
            dma((nb,)), dma((2, C)),
            dma((4,)), dma((4,)), dma((4,)),
        ],
        compiler_params=pltpu.CompilerParams(
            collective_id=0, has_side_effects=True, vmem_limit_bytes=60 * 1024 * 1024
        ),
    )(tile_count, tile_pos[0], grad_out, relu_mask, saved_agg, weight, tiles)

    def finish(wg_in, a, b, wg_out, ig_out):
        wg_out[...] = wg_in[...]
        ig_out[...] = a[...] + b[...]

    return pl.pallas_call(
        finish,
        out_shape=(jax.ShapeDtypeStruct((blk, D), F32), jax.ShapeDtypeStruct((IN, D), F32)),
        in_specs=[vmem, vmem, vmem],
        out_specs=(vmem, vmem),
    )(wg, ig, igr)


CUTS = (2, 2, 2, 2)


def per_device(R, C, N, grad_out, *rest):
    H, D = grad_out.shape
    line = R == 2 and C == 4 and N == 4 and D % (8 * R * C) == 0
    line = line and H == len(CUTS) * TILE and rest[3].shape[2] == TILE
    return (on_line if line else general)(R, C, N, grad_out, *rest)


def solution(mesh):
    in_specs = (
        P(("row", "col"), "ch"),
        P(("row", "col"), "ch"),
        P(("row", "col"), "ch"),
        P("ch", None),
        P("row", "col", None, None, None),
        P("row", "col", None),
        P("row", "col"),
    )
    out_specs = (P(("row", "col"), "ch"), P("col", "ch"))
    R, C, N = mesh.shape["row"], mesh.shape["col"], mesh.shape["ch"]
    return jax.shard_map(
        functools.partial(per_device, R, C, N), mesh=mesh, in_specs=in_specs, out_specs=out_specs, check_vma=False
    )
```
